32 devices in a mesh: seq: 4 (over x, core), wide: 8 (over z, y).
Axes of the slice: x: 2, y: 2, z: 4, core: 2. Of those that a mesh axis runs over, the one named last changes fastest.
Arguments:
- tokens: bfloat16 [8, 512, 1536], P('wide', 'seq'), may hold values from -6 to 6
- segments: int32 [8, 512], P('wide'), may hold values from 0 to 3, never falling along the last dimension, each value on 1 to 256 neighbouring positions
- w_query: float32 [1536, 1536], P(('seq', 'wide')), may hold values from -0.15625 to 0.15625
- w_key: float32 [1536, 1536], P(('seq', 'wide')), may hold values from -0.15625 to 0.15625
- w_value: float32 [1536, 1536], P(('seq', 'wide')), may hold values from -0.15625 to 0.15625
- w_out: float32 [1536, 1536], P(('seq', 'wide')), may hold values from -0.15625 to 0.15625
- gain_attn: float32 [1536], P(('seq', 'wide')), may hold values from 0.5 to 1.5
- gain_group: float32 [1536], P(('seq', 'wide')), may hold values from 0.5 to 1.5
- gain_ffn: float32 [1536], P(('seq', 'wide')), may hold values from 0.5 to 1.5
- conv_kernel: float32 [16, 6, 11], replicated, may hold values from -1.2 to 1.2
- head_mix: float32 [16, 2], replicated, may hold values from 0.2 to 1
- w_gate: float32 [1536, 4096], P('seq', 'wide'), may hold values from -0.15625 to 0.15625
- w_up: float32 [1536, 4096], P('seq', 'wide'), may hold values from -0.15625 to 0.15625
- w_down: float32 [4096, 1536], P('wide', 'seq'), may hold values from -0.09375 to 0.09375
- cotangent: bfloat16 [8, 512, 1536], P('wide', 'seq'), may hold values from -6 to 6
Outputs:
- output: bfloat16 [8, 512, 1536], P('wide', 'seq')
- grad_tokens: bfloat16 [8, 512, 1536], P('wide', 'seq')
- grad_w_query: float32 [1536, 1536], P(('seq', 'wide'))
- grad_w_key: float32 [1536, 1536], P(('seq', 'wide'))
- grad_w_value: float32 [1536, 1536], P(('seq', 'wide'))
- grad_w_out: float32 [1536, 1536], P(('seq', 'wide'))
- grad_gain_attn: float32 [1536], P(('seq', 'wide'))
- grad_gain_group: float32 [1536], P(('seq', 'wide'))
- grad_gain_ffn: float32 [1536], P(('seq', 'wide'))
- grad_conv_kernel: float32 [16, 6, 11], replicated
- grad_head_mix: float32 [16, 2], replicated
- grad_w_gate: float32 [1536, 4096], P('seq', 'wide')
- grad_w_up: float32 [1536, 4096], P('seq', 'wide')
- grad_w_down: float32 [4096, 1536], P('wide', 'seq')
The draws below stay inside these ranges and needn't reach their ends.
Inputs may be any that keep to these rules, and one draw needn't show every extreme that they name: `segments`: along a pack the segment ids never fall; each of the 4 documents of a pack holds 1 to 256 positions and one holds exactly 256.
All inputs are finite; a program needn't handle non-finite values.
Results may differ from the reference program's by a relative error of at most 0.019.
The reference program's roundings to bfloat16 on the way count: a program that leaves them out, or rounds other values in their place, can miss the bound.
Values may be sent and summed in bfloat16 or wider, within the bound.
No kernel may reach another device: no remote copies, remote signals or barrier semaphores. Data moves between devices by JAX's collectives and lax.ppermute only.
A program may use at most 320 MiB of HBM per device.

```python
import math
import jax
import jax.numpy as jnp
import numpy as np
from jax import lax

D = 1536
HEADS = 16
HEAD_DIM = 96
FF = 4096
CQ = 6
CK = 11
GROUP = 2
TOK_DEV = 128
HD = 1536
PACK_LEN = 512
PACKS = 8
DOCS = 4
DOC_MOST = 256


def block_scale(rng, shape, shards, smallest, largest):
    gain = 1.0
    for dim, parts in shards:
        steps = jax.random.uniform(jax.random.fold_in(jax.random.fold_in(rng, 6), dim), (parts,), jnp.float32, smallest / len(shards), largest / len(shards))
        gain = gain * jnp.repeat(jnp.exp(steps), shape[dim] // parts).reshape((-1,) + (1,) * (len(shape) - 1 - dim))
    return gain


def split_up(amount, total, bound, skew):
    portions = [(1 << 20) // math.isqrt(rank ** skew) + 1 for rank in range(2, amount + 1)]
    surplus, counts = total - bound - (amount - 1), [1] * (amount - 1)
    while surplus > 0:
        free = [i for i in range(amount - 1) if counts[i] < bound]
        mass, remaining = sum([portions[i] for i in free]), surplus
        for i in free:
            addition = min(bound - counts[i], max(1, remaining * portions[i] // mass), surplus)
            counts[i] = counts[i] + addition
            surplus = surplus - addition
    return np.array([bound] + counts)


def ragged(own_key, amount, total, most, lean):
    if amount == 2:
        one = jax.random.randint(own_key, (), max(1, total - most), min(most, total - 1) + 1)
        return jnp.stack([one, total - one])
    sizes = jnp.asarray(split_up(amount, total, most, lean), jnp.int32)
    couples = (amount - 1) // 2
    giver, receiver = sizes[1:1 + 2 * couples:2], sizes[2:2 + 2 * couples:2]
    slack = jnp.minimum(giver - 1, most - receiver)
    passed = jax.random.randint(jax.random.fold_in(own_key, 1), (couples,), 0, 1 << 20) % (slack + 1)
    sizes = sizes.at[1:1 + 2 * couples:2].set(giver - passed).at[2:2 + 2 * couples:2].set(receiver + passed)
    return sizes[jax.random.permutation(jax.random.fold_in(own_key, 2), amount)]


def gaussian(stream_key, extent, scale, reach, shards=(), kind=jnp.bfloat16):
    gain = block_scale(stream_key, extent, shards, -0.22, 0.18) if shards else 1.0
    array = jax.random.normal(stream_key, extent, jnp.float32) * scale * gain
    return jnp.minimum(jnp.maximum(array, -reach), reach).astype(kind)


def setup_inputs(seed: int = 0) -> dict:
    seeds = jax.random.split(jax.random.key(seed), 16)
    tokens = gaussian(seeds[0], (PACKS, PACK_LEN, D), 1.0, 6.0, ((0, 8), (1, 4)))
    segments = jax.vmap(lambda own: jnp.searchsorted(jnp.cumsum(ragged(own, DOCS, PACK_LEN, DOC_MOST, 2)), jnp.arange(PACK_LEN), side="right"))(jax.random.split(seeds[1], PACKS)).reshape((PACKS, PACK_LEN)).astype(jnp.int32)
    w_query = gaussian(seeds[2], (D, HD), D ** -0.5, 0.15625, ((0, 32),), jnp.float32)
    w_key = gaussian(seeds[3], (D, HD), D ** -0.5, 0.15625, ((0, 32),), jnp.float32)
    w_value = gaussian(seeds[4], (D, HD), D ** -0.5, 0.15625, ((0, 32),), jnp.float32)
    w_out = gaussian(seeds[5], (HD, D), HD ** -0.5, 0.15625, ((0, 32),), jnp.float32)
    gain_attn = jnp.clip(1.0 + 0.1 * jax.random.normal(seeds[6], (D,), jnp.float32), 0.5, 1.5)
    gain_group = jnp.clip(1.0 + 0.1 * jax.random.normal(seeds[7], (HD,), jnp.float32), 0.5, 1.5)
    gain_ffn = jnp.clip(1.0 + 0.1 * jax.random.normal(seeds[8], (D,), jnp.float32), 0.5, 1.5)
    conv_kernel = gaussian(seeds[9], (HEADS, CQ, CK), 0.3, 1.2, (), jnp.float32)
    head_mix = jnp.clip(jax.random.uniform(seeds[10], (HEADS, GROUP), jnp.float32, 0.2, 1.0), 0.2, 1.0)
    w_gate = gaussian(seeds[11], (D, FF), D ** -0.5, 0.15625, ((0, 4), (1, 8)), jnp.float32)
    w_up = gaussian(seeds[12], (D, FF), D ** -0.5, 0.15625, ((0, 4), (1, 8)), jnp.float32)
    w_down = gaussian(seeds[13], (FF, D), FF ** -0.5, 0.09375, ((0, 8), (1, 4)), jnp.float32)
    cotangent = gaussian(seeds[14], (PACKS, PACK_LEN, D), 1.0, 6.0, ((0, 8), (1, 4)))
    return {"tokens": tokens, "segments": segments, "w_query": w_query, "w_key": w_key, "w_value": w_value, "w_out": w_out, "gain_attn": gain_attn, "gain_group": gain_group, "gain_ffn": gain_ffn, "conv_kernel": conv_kernel, "head_mix": head_mix, "w_gate": w_gate, "w_up": w_up, "w_down": w_down, "cotangent": cotangent}


precise = lax.Precision.HIGHEST
epsilon = 1e-05

@jax.custom_vjp
def low(v):
    return lax.optimization_barrier(v.astype(jnp.bfloat16)).astype(jnp.float32)

@jax.custom_vjp
def low_back(v):
    return v

def low_keep(v):
    return (low(v), None)

def low_pass(kept, grad):
    return (grad,)

def back_keep(v):
    return (v, None)

def back_low(kept, grad):
    return (low(grad),)
low.defvjp(low_keep, low_pass)
low_back.defvjp(back_keep, back_low)

def matmul(left_op, right_op):
    return jnp.dot(left_op, right_op, precision=precise, preferred_element_type=jnp.float32)

def rms_scaled(values, gain_vec):
    return values * lax.rsqrt(lax.optimization_barrier(jnp.mean(values * values, axis=-1, keepdims=True)) + epsilon) * gain_vec

def group_scaled(values, gain_vec):
    center = values - lax.optimization_barrier(jnp.mean(values, axis=-1, keepdims=True))
    spread = lax.optimization_barrier(jnp.mean(center * center, axis=-1, keepdims=True))
    return center * lax.rsqrt(spread + epsilon) * gain_vec

def tile_masks(seg_query, pos_query, seg_key, pos_key, valid_flag):
    query_rim = CQ - 1
    key_rim = CK // 2
    allowed = (seg_query[:, None] == seg_key[None, :]) & (pos_key[None, :] <= pos_query[:, None]) & valid_flag
    row_count = seg_query.shape[0] - query_rim
    row_masks = jnp.stack([(seg_query[query_rim - shift_q:query_rim - shift_q + row_count] == seg_query[query_rim:]).astype(jnp.float32) for shift_q in range(CQ)])
    final_mask = allowed[query_rim:, key_rim:key_rim + row_count]
    return (allowed, row_masks, final_mask)

def convolve(scores, allowed, row_masks, kernel):
    query_rim = CQ - 1
    key_rim = CK // 2
    row_count = scores.shape[1] - query_rim
    col_count = scores.shape[2] - 2 * key_rim
    masked = jnp.where(allowed[None], scores, 0.0)
    summed = jnp.zeros((scores.shape[0], row_count, col_count), jnp.float32)
    for shift_q in range(CQ):
        inner_sum = jnp.zeros((scores.shape[0], row_count, col_count), jnp.float32)
        for shift_k in range(CK):
            piece_view = masked[:, query_rim - shift_q:query_rim - shift_q + row_count, 2 * key_rim - shift_k:2 * key_rim - shift_k + col_count]
            inner_sum = inner_sum + kernel[:, shift_q, shift_k][:, None, None] * piece_view
        summed = summed + row_masks[shift_q][None, :, None] * inner_sum
    return summed

def mix_heads(probs, head_mix):
    lead_dims = probs.shape[:-3]
    tail_dims = probs.shape[-2:]
    grouped = probs.reshape(lead_dims + (HEADS // GROUP, GROUP) + tail_dims)
    mixing = head_mix.reshape(HEADS // GROUP, GROUP, GROUP)
    summed = jnp.zeros(lead_dims + (HEADS // GROUP, GROUP) + tail_dims, jnp.float32)
    for source in range(GROUP):
        summed = summed + mixing[:, :, source][:, :, None, None] * jnp.expand_dims(grouped[..., :, source, :, :], -3)
    return summed.reshape(probs.shape)

def layer_pack(tokens_f, seg_row, params):
    w_query, w_key, w_value, w_out, gain_attn, gain_group, gain_ffn, conv_kernel, head_mix, w_gate, w_up, w_down = params
    length = tokens_f.shape[0]
    query_rim = CQ - 1
    key_rim = CK // 2
    scaling = HEAD_DIM ** (-0.5)
    normed = low(rms_scaled(tokens_f, gain_attn))
    query_val = low(low_back(matmul(normed, w_query))).reshape(length, HEADS, HEAD_DIM)
    key_val = low(low_back(matmul(normed, w_key))).reshape(length, HEADS, HEAD_DIM)
    value_val = low(low_back(matmul(normed, w_value))).reshape(length, HEADS, HEAD_DIM)
    query_pad = jnp.concatenate([jnp.zeros((query_rim, HEADS, HEAD_DIM), jnp.float32), query_val])
    key_pad = jnp.concatenate([jnp.zeros((key_rim, HEADS, HEAD_DIM), jnp.float32), key_val, jnp.zeros((key_rim, HEADS, HEAD_DIM), jnp.float32)])
    seg_query_pad = jnp.concatenate([jnp.full((query_rim,), -1, jnp.int32), seg_row])
    seg_key_pad = jnp.concatenate([jnp.full((key_rim,), -2, jnp.int32), seg_row, jnp.full((key_rim,), -2, jnp.int32)])
    blocks = length // TOK_DEV

    def query_block(block_index):
        row_start = (block_index * TOK_DEV).astype(jnp.int32)
        query_ext = lax.dynamic_slice_in_dim(query_pad, row_start, TOK_DEV + query_rim)
        seg_query = lax.dynamic_slice_in_dim(seg_query_pad, row_start, TOK_DEV + query_rim)
        pos_query = row_start - query_rim + jnp.arange(TOK_DEV + query_rim, dtype=jnp.int32)

        def key_block(other_index):
            key_start = (other_index * TOK_DEV).astype(jnp.int32)
            key_ext = lax.dynamic_slice_in_dim(key_pad, key_start, TOK_DEV + 2 * key_rim)
            seg_key = lax.dynamic_slice_in_dim(seg_key_pad, key_start, TOK_DEV + 2 * key_rim)
            pos_key = key_start - key_rim + jnp.arange(TOK_DEV + 2 * key_rim, dtype=jnp.int32)
            scores = low_back(scaling * jnp.einsum('qhe,khe->hqk', query_ext, key_ext, precision=precise))
            allowed, row_masks, final_mask = tile_masks(seg_query, pos_query, seg_key, pos_key, True)
            conv_out = convolve(scores, allowed, row_masks, conv_kernel)
            return jnp.where(final_mask[None], conv_out, -jnp.inf)
        tile_stack = lax.map(key_block, jnp.arange(blocks, dtype=jnp.int32))
        logits = jnp.transpose(tile_stack, (1, 2, 0, 3)).reshape(HEADS, TOK_DEV, length)
        probs = jnp.exp(logits - jax.nn.logsumexp(logits, axis=-1, keepdims=True))
        weights = low(mix_heads(probs, head_mix))
        return jnp.einsum('htk,khe->the', weights, value_val, precision=precise)
    attended = lax.map(jax.checkpoint(query_block), jnp.arange(blocks, dtype=jnp.int32))
    attended = low_back(attended.reshape(length, HEADS, HEAD_DIM))
    grouped = low(group_scaled(attended, gain_group.reshape(HEADS, HEAD_DIM))).reshape(length, HEADS * HEAD_DIM)
    branch = low_back(matmul(grouped, w_out))
    middle = tokens_f + branch
    ffn_in = low(rms_scaled(middle, gain_ffn))
    gate_val = low_back(matmul(ffn_in, w_gate))
    up_val = low_back(matmul(ffn_in, w_up))
    hidden = low(jax.nn.silu(gate_val) * up_val)
    block_units = FF // PACKS
    ffn_total = jnp.zeros(middle.shape, jnp.float32)
    for block_number in range(PACKS):
        first_unit = block_number * block_units
        ffn_total = ffn_total + low(matmul(hidden[:, first_unit:first_unit + block_units], w_down[first_unit:first_unit + block_units]))
    return middle + ffn_total

def reference(tokens, segments, w_query, w_key, w_value, w_out, gain_attn, gain_group, gain_ffn, conv_kernel, head_mix, w_gate, w_up, w_down, cotangent):
    params = (w_query, w_key, w_value, w_out, gain_attn, gain_group, gain_ffn, conv_kernel, head_mix, w_gate, w_up, w_down)

    def forward(tokens_f, params):
        wq_m, wk_m, wv_m, wo_m, ga_m, gg_m, gf_m, conv_m, mix_m, wg_m, wu_m, wd_m = params
        rounded = (low(wq_m), low(wk_m), low(wv_m), low(wo_m), low(ga_m), low(gg_m), low(gf_m), conv_m, mix_m, low(wg_m), low(wu_m), low(wd_m))

        def one_pack(pair_args):
            return layer_pack(pair_args[0], pair_args[1], rounded)
        return lax.map(one_pack, (tokens_f, segments))
    layer_out, pull_back = jax.vjp(forward, tokens.astype(jnp.float32), params)
    grad_in, grad_list = pull_back(cotangent.astype(jnp.float32))
    return (layer_out.astype(jnp.bfloat16), grad_in.astype(jnp.bfloat16), grad_list[0], grad_list[1], grad_list[2], grad_list[3], grad_list[4], grad_list[5], grad_list[6], grad_list[7], grad_list[8], grad_list[9], grad_list[10], grad_list[11])
```

```python
import functools

import jax
import jax.numpy as jnp
from jax import lax
from jax.experimental import pallas as pl
from jax.experimental.pallas import tpu as pltpu
from jax.sharding import PartitionSpec as P

HEADS = 16
HEAD_DIM = 96
CQ = 6
CK = 11
GROUP = 2
LANES = 128
BLOCK = 128
RIM = 16


precise = lax.Precision.HIGHEST
epsilon = 1e-05


def passed_along(value, axis, by):
    devices = lax.axis_size(axis)
    pairs = [(i, i + by) for i in range(devices) if 0 <= i + by < devices]
    return lax.ppermute(value, axis, pairs)


def extended(block, sides, width):
    for axis, dim in sides:
        count = lax.axis_size(axis)
        forward = [(i, i + 1) for i in range(count - 1)]
        backward = [(target, source) for source, target in forward]
        low = lax.ppermute(
            lax.slice_in_dim(block, block.shape[dim] - width, None, axis=dim), axis, forward
        )
        high = lax.ppermute(lax.slice_in_dim(block, 0, width, axis=dim), axis, backward)
        block = jnp.concatenate([low, block, high], axis=dim)
    return block


def rms_scaled(values, gain_vec):
    return (
        values * lax.rsqrt(jnp.mean(values * values, axis=-1, keepdims=True) + epsilon) * gain_vec
    )


def group_scaled(values, gain_vec):
    center = values - jnp.mean(values, axis=-1, keepdims=True)
    spread = jnp.mean(center * center, axis=-1, keepdims=True)
    return center * lax.rsqrt(spread + epsilon) * gain_vec


def tile_masks(seg_query, pos_query, seg_key, pos_key, valid_flag):
    query_rim = CQ - 1
    key_rim = CK // 2
    allowed = (
        (seg_query[:, None] == seg_key[None, :])
        & (pos_key[None, :] <= pos_query[:, None])
        & valid_flag
    )
    row_count = seg_query.shape[0] - query_rim
    row_masks = jnp.stack(
        [
            (
                seg_query[query_rim - shift_q : query_rim - shift_q + row_count]
                == seg_query[query_rim:]
            ).astype(jnp.float32)
            for shift_q in range(CQ)
        ]
    )
    final_mask = allowed[query_rim:, key_rim : key_rim + row_count]
    return (allowed, row_masks, final_mask)


def convolve(scores, allowed, row_masks, kernel):
    query_rim = CQ - 1
    key_rim = CK // 2
    row_count = scores.shape[1] - query_rim
    col_count = scores.shape[2] - 2 * key_rim
    masked = jnp.where(allowed[None], scores, 0.0)
    summed = jnp.zeros((scores.shape[0], row_count, col_count), jnp.float32)
    for shift_q in range(CQ):
        inner_sum = jnp.zeros((scores.shape[0], row_count, col_count), jnp.float32)
        for shift_k in range(CK):
            piece_view = masked[
                :,
                query_rim - shift_q : query_rim - shift_q + row_count,
                2 * key_rim - shift_k : 2 * key_rim - shift_k + col_count,
            ]
            inner_sum = inner_sum + kernel[:, shift_q, shift_k][:, None, None] * piece_view
        summed = summed + row_masks[shift_q][None, :, None] * inner_sum
    return summed


def mix_heads(probs, head_mix):
    lead_dims = probs.shape[:-3]
    tail_dims = probs.shape[-2:]
    grouped = probs.reshape(lead_dims + (HEADS // GROUP, GROUP) + tail_dims)
    mixing = head_mix.reshape(HEADS // GROUP, GROUP, GROUP)
    summed = jnp.zeros(lead_dims + (HEADS // GROUP, GROUP) + tail_dims, jnp.float32)
    for source in range(GROUP):
        summed = summed + mixing[:, :, source][:, :, None, None] * jnp.expand_dims(
            grouped[..., :, source, :, :], -3
        )
    return summed.reshape(probs.shape)


def unmix_heads(grads, head_mix):
    lead_dims = grads.shape[:-3]
    tail_dims = grads.shape[-2:]
    grouped = grads.reshape(lead_dims + (HEADS // GROUP, GROUP) + tail_dims)
    mixing = head_mix.reshape(HEADS // GROUP, GROUP, GROUP)
    summed = jnp.zeros(lead_dims + (HEADS // GROUP, GROUP) + tail_dims, jnp.float32)
    for target in range(GROUP):
        summed = summed + mixing[:, target, :][:, :, None, None] * jnp.expand_dims(
            grouped[..., :, target, :, :], -3
        )
    return summed.reshape(grads.shape)


def contract(left_op, right_op, left_dim, right_dim):
    return lax.dot_general(
        left_op,
        right_op,
        (((left_dim,), (right_dim,)), ((), ())),
        preferred_element_type=jnp.float32,
    )


def gather_attention(w_query, w_key, w_value, w_out, gain_attn, gain_group, gain_ffn):
    return (
        lax.all_gather(w_query.astype(jnp.bfloat16), ("seq", "wide"), axis=0, tiled=True),
        lax.all_gather(w_key.astype(jnp.bfloat16), ("seq", "wide"), axis=0, tiled=True),
        lax.all_gather(w_value.astype(jnp.bfloat16), ("seq", "wide"), axis=0, tiled=True),
        lax.all_gather(w_out.astype(jnp.bfloat16), ("seq", "wide"), axis=0, tiled=True),
        lax.all_gather(gain_attn.astype(jnp.bfloat16), ("seq", "wide"), axis=0, tiled=True),
        lax.all_gather(gain_group.astype(jnp.bfloat16), ("seq", "wide"), axis=0, tiled=True),
        lax.all_gather(gain_ffn.astype(jnp.bfloat16), ("seq", "wide"), axis=0, tiled=True),
    )


def collect_packets(own, reach_len):
    stored = jnp.zeros((reach_len,) + own.shape, own.dtype).at[0].set(own)

    def advance(turn_index, state_pair):
        packet, stored_now = state_pair
        packet = passed_along(packet, "seq", 1)
        return (packet, lax.dynamic_update_index_in_dim(stored_now, packet, turn_index, 0))

    return lax.fori_loop(1, reach_len, advance, (own, stored))[1]


def tile_logits(query_ext, packet, seg_query, pos_query, seg_key_pad, other_shard, token_count):
    key_rim = CK // 2
    key_ext = packet[: token_count + 2 * key_rim].reshape(
        token_count + 2 * key_rim, HEADS, HEAD_DIM
    )
    scores = jnp.einsum(
        "qhe,khe->hqk", query_ext, key_ext, preferred_element_type=jnp.float32
    ) * HEAD_DIM ** (-0.5)
    key_start = other_shard * token_count
    seg_key = lax.dynamic_slice_in_dim(
        seg_key_pad, jnp.maximum(key_start, 0), token_count + 2 * key_rim
    )
    pos_key = key_start - key_rim + jnp.arange(token_count + 2 * key_rim, dtype=jnp.int32)
    allowed, row_masks, final_mask = tile_masks(
        seg_query, pos_query, seg_key, pos_key, other_shard >= 0
    )
    return (scores, allowed, row_masks, final_mask, key_ext)


def shards(
    tokens,
    segments,
    w_query,
    w_key,
    w_value,
    w_out,
    gain_attn,
    gain_group,
    gain_ffn,
    conv_kernel,
    head_mix,
    w_gate,
    w_up,
    w_down,
    cotangent,
):
    token_count = tokens.shape[1]
    query_rim = CQ - 1
    key_rim = CK // 2
    width_all = HEADS * HEAD_DIM
    scaling = HEAD_DIM ** (-0.5)
    seq_count = lax.axis_size("seq")
    longest_doc = min(1024, token_count * seq_count // 2)
    reach_len = min(seq_count - 1, (longest_doc - 1) // token_count + 1) + 1
    seq_index = lax.axis_index("seq")
    row_start = seq_index * token_count
    seg_row = segments[0]
    seg_query_pad = jnp.concatenate([jnp.full((query_rim,), -1, jnp.int32), seg_row])
    seg_key_pad = jnp.concatenate(
        [jnp.full((key_rim,), -2, jnp.int32), seg_row, jnp.full((key_rim,), -2, jnp.int32)]
    )
    seg_query = lax.dynamic_slice_in_dim(seg_query_pad, row_start, token_count + query_rim)
    pos_query = row_start - query_rim + jnp.arange(token_count + query_rim, dtype=jnp.int32)
    weights = gather_attention(w_query, w_key, w_value, w_out, gain_attn, gain_group, gain_ffn)
    query_mat, key_mat, value_mat, out_mat, gain_one, gain_mid, gain_two = weights
    inputs = tokens[0].astype(jnp.float32)
    gain_first = gain_one.astype(jnp.float32)
    normed = rms_scaled(inputs, gain_first).astype(jnp.bfloat16)
    queries = jnp.dot(normed, query_mat, preferred_element_type=jnp.float32).astype(jnp.bfloat16)
    keys_loc = jnp.dot(normed, key_mat, preferred_element_type=jnp.float32).astype(jnp.bfloat16)
    values_loc = jnp.dot(normed, value_mat, preferred_element_type=jnp.float32).astype(jnp.bfloat16)
    rimmed = extended(jnp.stack([queries, keys_loc]), (("seq", 1),), key_rim)
    query_ext = rimmed[0, : token_count + query_rim].reshape(
        token_count + query_rim, HEADS, HEAD_DIM
    )
    own = jnp.concatenate([rimmed[1], values_loc], axis=0)
    packets = collect_packets(own, reach_len)

    def all_logits(packet_stack):

        def logits_of(turn_index):
            packet = lax.dynamic_index_in_dim(packet_stack, turn_index, 0, keepdims=False)
            scores, allowed, row_masks, final_mask, key_ext = tile_logits(
                query_ext,
                packet,
                seg_query,
                pos_query,
                seg_key_pad,
                seq_index - turn_index,
                token_count,
            )
            return jnp.where(
                final_mask[None], convolve(scores, allowed, row_masks, conv_kernel), -jnp.inf
            )

        return lax.map(logits_of, jnp.arange(reach_len, dtype=jnp.int32))

    logits = all_logits(packets)
    peak_val = jnp.max(logits, axis=(0, 3))
    log_total = peak_val + jnp.log(
        jnp.sum(jnp.exp(logits - peak_val[None, :, :, None]), axis=(0, 3))
    )
    probs_all = jnp.exp(logits - log_total[None, :, :, None])
    mixed_b = mix_heads(probs_all, head_mix).astype(jnp.bfloat16)
    values_all = packets[:, token_count + 2 * key_rim :].reshape(
        reach_len, token_count, HEADS, HEAD_DIM
    )
    attended = jnp.einsum("rhtk,rkhe->the", mixed_b, values_all, preferred_element_type=jnp.float32)
    gain_middle = gain_mid.astype(jnp.float32).reshape(HEADS, HEAD_DIM)
    grouped = (
        group_scaled(attended, gain_middle).reshape(token_count, width_all).astype(jnp.bfloat16)
    )
    middle = inputs + jnp.dot(grouped, out_mat, preferred_element_type=jnp.float32)
    gain_second = gain_two.astype(jnp.float32)
    ffn_in = rms_scaled(middle, gain_second).astype(jnp.bfloat16)
    ffn_all = lax.all_gather(ffn_in, "wide", axis=0, tiled=True)
    gate_mat, up_mat, down_mat = (
        lax.all_gather(w_gate.astype(jnp.bfloat16), "seq", axis=0, tiled=True),
        lax.all_gather(w_up.astype(jnp.bfloat16), "seq", axis=0, tiled=True),
        lax.all_gather(w_down.astype(jnp.bfloat16), "seq", axis=1, tiled=True),
    )
    gate_val = jnp.dot(ffn_all, gate_mat, preferred_element_type=jnp.float32)
    up_val = jnp.dot(ffn_all, up_mat, preferred_element_type=jnp.float32)
    hidden = (jax.nn.silu(gate_val) * up_val).astype(jnp.bfloat16)
    ffn_out = lax.psum_scatter(
        jnp.dot(hidden, down_mat, preferred_element_type=jnp.float32).astype(jnp.bfloat16),
        "wide",
        scatter_dimension=0,
        tiled=True,
    ).astype(jnp.float32)
    output = (middle + ffn_out).astype(jnp.bfloat16)
    grad_out = cotangent[0]
    grad_all = lax.all_gather(grad_out, "wide", axis=0, tiled=True)
    grad_hidden = contract(grad_all, down_mat, 1, 1)
    grad_down = contract(hidden, grad_all, 0, 0)
    sig_gate = jax.nn.sigmoid(gate_val)
    grad_gate = (grad_hidden * up_val * sig_gate * (1.0 + gate_val * (1.0 - sig_gate))).astype(
        jnp.bfloat16
    )
    grad_up = (grad_hidden * gate_val * sig_gate).astype(jnp.bfloat16)
    grad_gate_w = contract(ffn_all, grad_gate, 0, 0)
    grad_up_w = contract(ffn_all, grad_up, 0, 0)
    grad_ffn_in = lax.psum_scatter(
        (contract(grad_gate, gate_mat, 1, 1) + contract(grad_up, up_mat, 1, 1)).astype(
            jnp.bfloat16
        ),
        "wide",
        scatter_dimension=0,
        tiled=True,
    ).astype(jnp.float32)
    ffn_grads = (
        lax.psum_scatter(
            grad_gate_w.astype(jnp.bfloat16), "seq", scatter_dimension=0, tiled=True
        ).astype(jnp.float32),
        lax.psum_scatter(
            grad_up_w.astype(jnp.bfloat16), "seq", scatter_dimension=0, tiled=True
        ).astype(jnp.float32),
        lax.psum_scatter(
            grad_down.astype(jnp.bfloat16), "seq", scatter_dimension=1, tiled=True
        ).astype(jnp.float32),
    )
    norm_two_back = jax.vjp(rms_scaled, middle, gain_second)[1]
    grad_mid_part, grad_gain_two = norm_two_back(grad_ffn_in)
    grad_middle = grad_out.astype(jnp.float32) + grad_mid_part
    grad_branch = grad_middle.astype(jnp.bfloat16)
    back_weights = gather_attention(w_query, w_key, w_value, w_out, gain_attn, gain_group, gain_ffn)
    query_back, key_back, value_back, out_back = (
        back_weights[0],
        back_weights[1],
        back_weights[2],
        back_weights[3],
    )
    grad_grouped = contract(grad_branch, out_back, 1, 1)
    grad_out_w = contract(grouped, grad_branch, 0, 0)
    group_back = jax.vjp(group_scaled, attended, gain_middle)[1]
    grad_attended, grad_gain_mid = group_back(grad_grouped.reshape(token_count, HEADS, HEAD_DIM))
    grad_att_b = grad_attended.astype(jnp.bfloat16)
    back_packets = collect_packets(own, reach_len)
    logits_again = all_logits(back_packets)
    probs_again = jnp.exp(logits_again - log_total[None, :, :, None])
    mixed_again = mix_heads(probs_again, head_mix).astype(jnp.bfloat16)
    values_back = back_packets[:, token_count + 2 * key_rim :].reshape(
        reach_len, token_count, HEADS, HEAD_DIM
    )
    grad_mixed = jnp.einsum(
        "the,rkhe->rhtk", grad_att_b, values_back, preferred_element_type=jnp.float32
    )
    grad_values = jnp.einsum(
        "rhtk,the->rkhe", mixed_again, grad_att_b, preferred_element_type=jnp.float32
    ).reshape(reach_len, token_count, width_all)
    probs_grouped = probs_again.reshape(reach_len, HEADS // GROUP, GROUP, token_count, token_count)
    mixed_grouped = grad_mixed.reshape(reach_len, HEADS // GROUP, GROUP, token_count, token_count)
    grad_mix = jnp.einsum(
        "rgdtk,rgctk->gcd", probs_grouped, mixed_grouped, precision=precise
    ).reshape(HEADS, GROUP)
    grad_probs = unmix_heads(grad_mixed, head_mix)
    delta_row = jnp.sum(probs_again * grad_probs, axis=(0, 3))
    grad_logits = probs_again * (grad_probs - delta_row[None, :, :, None])

    def tile_grads(turn_index):
        packet = lax.dynamic_index_in_dim(back_packets, turn_index, 0, keepdims=False)
        scores, allowed, row_masks, final_mask, key_ext = tile_logits(
            query_ext,
            packet,
            seg_query,
            pos_query,
            seg_key_pad,
            seq_index - turn_index,
            token_count,
        )
        conv_back = jax.vjp(
            lambda field, weights_k: convolve(field, allowed, row_masks, weights_k),
            scores,
            conv_kernel,
        )[1]
        grad_scores, grad_kernel = conv_back(
            lax.dynamic_index_in_dim(grad_logits, turn_index, 0, keepdims=False)
        )
        grad_scores_b = grad_scores.astype(jnp.bfloat16)
        grad_query_ext = (
            jnp.einsum("hqk,khe->qhe", grad_scores_b, key_ext, preferred_element_type=jnp.float32)
            * scaling
        )
        grad_key_ext = (
            jnp.einsum("hqk,qhe->khe", grad_scores_b, query_ext, preferred_element_type=jnp.float32)
            * scaling
        )
        cycle_term = jnp.concatenate(
            [
                grad_key_ext.reshape(token_count + 2 * key_rim, width_all),
                lax.dynamic_index_in_dim(grad_values, turn_index, 0, keepdims=False),
            ],
            axis=0,
        )
        return (cycle_term, grad_query_ext, grad_kernel)

    start_term, start_query, start_kernel = tile_grads(reach_len - 1)

    def descend(turn_index, state_all):
        cycle_acc, query_acc, kernel_acc = state_all
        cycle_term, query_part, kernel_part = tile_grads(reach_len - 1 - turn_index)
        moved_acc = passed_along(cycle_acc.astype(jnp.bfloat16), "seq", -1).astype(cycle_acc.dtype)
        return (moved_acc + cycle_term, query_acc + query_part, kernel_acc + kernel_part)

    cycle_acc, query_acc, kernel_acc = lax.fori_loop(
        1, reach_len, descend, (start_term, start_query, start_kernel)
    )
    query_flat = query_acc.reshape(token_count + query_rim, width_all)
    key_ext_grad = cycle_acc[: token_count + 2 * key_rim]
    grad_values_own = cycle_acc[token_count + 2 * key_rim :]
    edge_grads = jnp.stack(
        [
            jnp.concatenate([query_flat[:query_rim], jnp.zeros((key_rim, width_all), jnp.float32)]),
            jnp.concatenate([key_ext_grad[:key_rim], key_ext_grad[token_count + key_rim :]]),
        ]
    )
    rim_back = extended(edge_grads.astype(jnp.bfloat16), (("seq", 1),), key_rim).astype(
        edge_grads.dtype
    )
    grad_queries = (
        query_flat[query_rim:].at[token_count - key_rim :].add(rim_back[0, 3 * key_rim :])
    )
    grad_keys = (
        key_ext_grad[key_rim : key_rim + token_count]
        .at[:key_rim]
        .add(rim_back[1, :key_rim])
        .at[token_count - key_rim :]
        .add(rim_back[1, 3 * key_rim :])
    )
    grad_query_b = grad_queries.astype(jnp.bfloat16)
    grad_key_b = grad_keys.astype(jnp.bfloat16)
    grad_value_b = grad_values_own.astype(jnp.bfloat16)
    grad_query_w = contract(normed, grad_query_b, 0, 0)
    grad_key_w = contract(normed, grad_key_b, 0, 0)
    grad_value_w = contract(normed, grad_value_b, 0, 0)
    grad_normed = (
        contract(grad_query_b, query_back, 1, 1)
        + contract(grad_key_b, key_back, 1, 1)
        + contract(grad_value_b, value_back, 1, 1)
    )
    norm_one_back = jax.vjp(rms_scaled, inputs, gain_first)[1]
    grad_in_part, grad_gain_one = norm_one_back(grad_normed)
    grad_input = (grad_middle + grad_in_part).astype(jnp.bfloat16)
    attn_grads = (
        lax.psum_scatter(grad_query_w, ("seq", "wide"), scatter_dimension=0, tiled=True),
        lax.psum_scatter(grad_key_w, ("seq", "wide"), scatter_dimension=0, tiled=True),
        lax.psum_scatter(grad_value_w, ("seq", "wide"), scatter_dimension=0, tiled=True),
        lax.psum_scatter(grad_out_w, ("seq", "wide"), scatter_dimension=0, tiled=True),
        lax.psum_scatter(grad_gain_one, ("seq", "wide"), scatter_dimension=0, tiled=True),
        lax.psum_scatter(
            grad_gain_mid.reshape(width_all), ("seq", "wide"), scatter_dimension=0, tiled=True
        ),
        lax.psum_scatter(grad_gain_two, ("seq", "wide"), scatter_dimension=0, tiled=True),
    )
    small_sums = lax.psum((kernel_acc, grad_mix), ("seq", "wide"))
    return (
        output[None],
        grad_input[None],
        attn_grads[0],
        attn_grads[1],
        attn_grads[2],
        attn_grads[3],
        attn_grads[4],
        attn_grads[5],
        attn_grads[6],
        small_sums[0],
        small_sums[1],
        ffn_grads[0],
        ffn_grads[1],
        ffn_grads[2],
    )


def dot_plain(left, right):
    return lax.dot_general(left, right, (((1,), (0,)), ((), ())), preferred_element_type=jnp.float32)


def dot_nt(left, right):
    return lax.dot_general(left, right, (((1,), (1,)), ((), ())), preferred_element_type=jnp.float32)


def dot_tn(left, right):
    return lax.dot_general(left, right, (((0,), (0,)), ((), ())), preferred_element_type=jnp.float32)


def halves(value):
    high = value.astype(jnp.bfloat16)
    return high, (value - high.astype(jnp.float32)).astype(jnp.bfloat16)


def spread_lanes(tile, count):
    return tile if count == 1 else jnp.concatenate([tile] * count, axis=1)


def allowed_mask(starts, block, first_col, count):
    cols = lax.broadcasted_iota(jnp.int32, (BLOCK, count * LANES), 1) + first_col
    rows = lax.broadcasted_iota(jnp.int32, (BLOCK, count * LANES), 0) + block * BLOCK
    return (cols >= spread_lanes(starts, count)) & (cols <= rows)


def head_stats(values):
    lane = lax.broadcasted_iota(jnp.int32, values.shape, 1)
    mean = jnp.sum(values, axis=-1, keepdims=True) * (1.0 / HEAD_DIM)
    center = jnp.where(lane < HEAD_DIM, values - mean, 0.0)
    spread = jnp.sum(center * center, axis=-1, keepdims=True) * (1.0 / HEAD_DIM)
    inverse = lax.rsqrt(spread + epsilon)
    return center * inverse, inverse


def forward_kernel(
    blocks, reach, mix_ref, q_ref, k_ref, v_ref, start_ref, th_ref, tl_ref, gain_ref,
    probs_ref, high_ref, att_ref, grouped_ref, low_ref, part_ref,
):
    key_rim = CK // 2
    scaling = HEAD_DIM ** (-0.5)
    for h in range(GROUP):
        lanes = slice(h * LANES, (h + 1) * LANES)
        high_ref[0, h, :RIM, :] = jnp.zeros((RIM, high_ref.shape[3]), jnp.bfloat16)
        low_ref[h, :RIM, :] = jnp.zeros((RIM, high_ref.shape[3]), jnp.bfloat16)
        for n in range(blocks):
            first, last = max(0, n - reach), min(n + 3, blocks + 1)
            rows = slice(n * BLOCK, (n + 1) * BLOCK)
            scores = (
                dot_nt(q_ref[0, rows, lanes], k_ref[0, first * BLOCK : last * BLOCK, lanes]) * scaling
            )
            keep = allowed_mask(start_ref[0, rows, :], n, first * BLOCK - key_rim, last - first)
            high, low = halves(jnp.where(keep, scores, 0.0))
            into = slice(RIM + n * BLOCK, RIM + (n + 1) * BLOCK)
            cols = slice(first * LANES, last * LANES)
            high_ref[0, h, into, cols] = high
            low_ref[h, into, cols] = low
    for n in range(blocks):
        first = max(0, n - reach)
        count = n - first + 1
        rows = slice(n * BLOCK, (n + 1) * BLOCK)
        starts = start_ref[0, rows, :]
        offset = lax.broadcasted_iota(jnp.int32, (BLOCK, LANES), 0) + n * BLOCK - starts
        keep = allowed_mask(starts, n, first * BLOCK, count)
        window = slice((reach + 1 - count) * LANES, (reach + 1) * LANES)
        probs = []
        for h in range(GROUP):
            pieces = []
            for m in range(first, n + 1):
                rim_rows = slice(n * BLOCK, (n + 1) * BLOCK + RIM)
                cols = slice(m * LANES, (m + 2) * LANES)
                high = high_ref[0, h, rim_rows, cols]
                low = low_ref[h, rim_rows, cols]
                part = (
                    dot_plain(high, th_ref[h])
                    + dot_plain(low, th_ref[h])
                    + dot_plain(high, tl_ref[h])
                )
                for a in range(CQ):
                    part_ref[a] = part[:, a * LANES : (a + 1) * LANES]
                total = part_ref[0, RIM:, :]
                for a in range(1, CQ):
                    total = total + jnp.where(
                        offset >= a, part_ref[a, RIM - a : RIM - a + BLOCK, :], 0.0
                    )
                pieces.append(total)
            logits = pieces[0] if count == 1 else jnp.concatenate(pieces, axis=1)
            logits = jnp.where(keep, logits, -jnp.inf)
            peak = jnp.max(logits, axis=-1, keepdims=True)
            raised = jnp.exp(logits - peak)
            prob = raised / jnp.sum(raised, axis=-1, keepdims=True)
            probs_ref[0, h, rows, window] = prob
            probs.append(prob)
        keys = slice(first * BLOCK, (n + 1) * BLOCK)
        for h in range(GROUP):
            lanes = slice(h * LANES, (h + 1) * LANES)
            mixed = (mix_ref[h, 0] * probs[0] + mix_ref[h, 1] * probs[1]).astype(jnp.bfloat16)
            attended = dot_plain(mixed, v_ref[0, keys, lanes])
            att_ref[0, rows, lanes] = attended
            normal, _ = head_stats(attended)
            grouped_ref[0, rows, lanes] = (normal * gain_ref[:, lanes]).astype(jnp.bfloat16)


def fold_rows(value):
    return jnp.sum(value.reshape(value.shape[0] // 8, 8, value.shape[1]), axis=0)


def backward_kernel(
    blocks, reach, mix_ref, gg_ref, att_ref, gain_ref, q_ref, k_ref, v_ref, start_ref, stop_ref,
    probs_ref, high_ref, th_ref, tl_ref,
    dq_ref, dk_ref, dv_ref, taps_ref, mixg_ref, gaing_ref,
    grad_ref, cross_ref, keyg_ref, valueg_ref,
):
    key_rim = CK // 2
    scaling = HEAD_DIM ** (-0.5)

    @pl.when(pl.program_id(0) == 0)
    def _():
        cross_ref[...] = jnp.zeros_like(cross_ref)
        mixg_ref[...] = jnp.zeros_like(mixg_ref)
        gaing_ref[...] = jnp.zeros_like(gaing_ref)

    grad_ref[...] = jnp.zeros_like(grad_ref)
    keyg_ref[...] = jnp.zeros_like(keyg_ref)
    valueg_ref[...] = jnp.zeros_like(valueg_ref)
    lane = lax.broadcasted_iota(jnp.int32, (BLOCK, LANES), 1)
    for n in range(blocks):
        first = max(0, n - reach)
        count = n - first + 1
        rows = slice(n * BLOCK, (n + 1) * BLOCK)
        keys = slice(first * BLOCK, (n + 1) * BLOCK)
        window = slice((reach + 1 - count) * LANES, (reach + 1) * LANES)
        probs = [probs_ref[0, h, rows, window] for h in range(GROUP)]
        mixed_grads = []
        for h in range(GROUP):
            lanes = slice(h * LANES, (h + 1) * LANES)
            normal, inverse = head_stats(att_ref[0, rows, lanes])
            grad_grouped = gg_ref[0, rows, lanes]
            gaing_ref[:, lanes] += fold_rows(grad_grouped * normal)
            scaled = jnp.where(lane < HEAD_DIM, grad_grouped * gain_ref[:, lanes], 0.0)
            mean_one = jnp.sum(scaled, axis=-1, keepdims=True) * (1.0 / HEAD_DIM)
            mean_two = jnp.sum(scaled * normal, axis=-1, keepdims=True) * (1.0 / HEAD_DIM)
            grad_att = inverse * (scaled - mean_one - normal * mean_two)
            grad_att = jnp.where(lane < HEAD_DIM, grad_att, 0.0).astype(jnp.bfloat16)
            mixed_grads.append(dot_nt(grad_att, v_ref[0, keys, lanes]))
            mixed = (mix_ref[h, 0] * probs[0] + mix_ref[h, 1] * probs[1]).astype(jnp.bfloat16)
            valueg_ref[keys, lanes] += dot_tn(mixed, grad_att)
        for h in range(GROUP):
            for d in range(GROUP):
                product = fold_rows(probs[d] * mixed_grads[h])
                total = product[:, :LANES]
                for m in range(1, count):
                    total = total + product[:, m * LANES : (m + 1) * LANES]
                mixg_ref[h * GROUP + d] += total
        for d in range(GROUP):
            grad_probs = mix_ref[0, d] * mixed_grads[0] + mix_ref[1, d] * mixed_grads[1]
            delta = jnp.sum(probs[d] * grad_probs, axis=-1, keepdims=True)
            grad_logits = probs[d] * (grad_probs - delta)
            for m in range(count):
                grad_ref[d, first + m, rows, :] = grad_logits[:, m * LANES : (m + 1) * LANES]
    for h in range(GROUP):
        lanes = slice(h * LANES, (h + 1) * LANES)
        for n in range(blocks):
            first, last = max(0, n - reach), min(n + 1, blocks - 1)
            rows = slice(n * BLOCK, (n + 1) * BLOCK)
            room = stop_ref[0, rows, :] - (
                lax.broadcasted_iota(jnp.int32, (BLOCK, LANES), 0) + n * BLOCK
            )
            count = n + 2 - first
            sums = [None] * (count + 1)
            for m in range(first, last + 1):
                highs, lows = [], []
                for a in range(CQ):
                    piece = grad_ref[h, m, n * BLOCK + a : (n + 1) * BLOCK + a, :]
                    if a:
                        piece = jnp.where(room > a, piece, 0.0)
                    high, low = halves(piece)
                    highs.append(high)
                    lows.append(low)
                high = jnp.concatenate(highs, axis=1)
                low = jnp.concatenate(lows, axis=1)
                part = (
                    dot_nt(high, th_ref[h]) + dot_nt(low, th_ref[h]) + dot_nt(high, tl_ref[h])
                )
                for side in range(2):
                    place = m - first + side
                    value = part[:, side * LANES : (side + 1) * LANES]
                    sums[place] = value if sums[place] is None else sums[place] + value
                scores = high_ref[
                    0, h, RIM + n * BLOCK : RIM + (n + 1) * BLOCK, m * LANES : (m + 2) * LANES
                ]
                if m <= n:
                    cross_ref[h] += dot_tn(scores, high)
                else:
                    cross_ref[h, :LANES, :] += dot_tn(scores[:, :LANES], high)
            total = jnp.concatenate(sums[:count], axis=1)
            keep = allowed_mask(start_ref[0, rows, :], n, first * BLOCK - key_rim, count)
            grad_scores = jnp.where(keep, total, 0.0).astype(jnp.bfloat16)
            cols = slice(first * BLOCK, (first + count) * BLOCK)
            dq_ref[0, rows, lanes] = (
                dot_plain(grad_scores, k_ref[0, cols, lanes]) * scaling
            ).astype(jnp.bfloat16)
            keyg_ref[h, cols, :] += dot_tn(grad_scores, q_ref[0, rows, lanes])
        dk_ref[0, :, lanes] = (
            keyg_ref[h, key_rim : key_rim + blocks * BLOCK, :] * scaling
        ).astype(jnp.bfloat16)
    dv_ref[0] = valueg_ref[...].astype(jnp.bfloat16)

    @pl.when(pl.program_id(0) == pl.num_programs(0) - 1)
    def _():
        height = LANES + 2 * 8
        shift = (
            lax.broadcasted_iota(jnp.int32, (height, CQ * LANES), 1) % LANES
            - lax.broadcasted_iota(jnp.int32, (height, CQ * LANES), 0)
            + (CK - 1)
        )
        for h in range(GROUP):
            cross = cross_ref[h, :height, :]
            taps_ref[h] = jnp.zeros(taps_ref.shape[1:], jnp.float32)
            for b in range(CK):
                taps_ref[h, b : b + 1, :] = jnp.sum(
                    jnp.where(shift == b, cross, 0.0), axis=0, keepdims=True
                )


def pack_spec(shape):
    return pl.BlockSpec((1,) + shape, lambda p: (p,) + (0,) * len(shape))


def fixed_spec(shape):
    return pl.BlockSpec(shape, lambda p: (0,) * len(shape))


def attention_forward(mix, q, k, v, starts, table_high, table_low, gain, reach):
    packs, length, width = q.shape
    blocks = length // BLOCK
    padded = k.shape[1]
    return pl.pallas_call(
        functools.partial(forward_kernel, blocks, reach),
        grid=(packs,),
        in_specs=[
            pl.BlockSpec(memory_space=pltpu.SMEM),
            pack_spec((length, width)),
            pack_spec((padded, width)),
            pack_spec((length, width)),
            pack_spec((length, LANES)),
            fixed_spec(table_high.shape),
            fixed_spec(table_low.shape),
            fixed_spec(gain.shape),
        ],
        out_specs=[
            pack_spec((GROUP, length, (reach + 1) * LANES)),
            pack_spec((GROUP, RIM + length, padded)),
            pack_spec((length, width)),
            pack_spec((length, width)),
        ],
        out_shape=[
            jax.ShapeDtypeStruct((packs, GROUP, length, (reach + 1) * LANES), jnp.float32),
            jax.ShapeDtypeStruct((packs, GROUP, RIM + length, padded), jnp.bfloat16),
            jax.ShapeDtypeStruct((packs, length, width), jnp.float32),
            jax.ShapeDtypeStruct((packs, length, width), jnp.bfloat16),
        ],
        scratch_shapes=[
            pltpu.VMEM((GROUP, RIM + length, padded), jnp.bfloat16),
            pltpu.VMEM((CQ, RIM + BLOCK, LANES), jnp.float32),
        ],
        compiler_params=pltpu.CompilerParams(vmem_limit_bytes=48 << 20),
        name="attention_forward",
    )(mix, q, k, v, starts, table_high, table_low, gain)


def attention_backward(
    mix, grad_grouped, attended, gain, q, k, v, starts, stops, probs, high, table_high, table_low, reach
):
    packs, length, width = q.shape
    blocks = length // BLOCK
    padded = k.shape[1]
    return pl.pallas_call(
        functools.partial(backward_kernel, blocks, reach),
        grid=(packs,),
        in_specs=[
            pl.BlockSpec(memory_space=pltpu.SMEM),
            pack_spec((length, width)),
            pack_spec((length, width)),
            fixed_spec(gain.shape),
            pack_spec((length, width)),
            pack_spec((padded, width)),
            pack_spec((length, width)),
            pack_spec((length, LANES)),
            pack_spec((length, LANES)),
            pack_spec((GROUP, length, (reach + 1) * LANES)),
            pack_spec((GROUP, RIM + length, padded)),
            fixed_spec(table_high.shape),
            fixed_spec(table_low.shape),
        ],
        out_specs=[
            pack_spec((length, width)),
            pack_spec((length, width)),
            pack_spec((length, width)),
            fixed_spec((GROUP, 16, CQ * LANES)),
            fixed_spec((GROUP * GROUP, 8, LANES)),
            fixed_spec((8, width)),
        ],
        out_shape=[
            jax.ShapeDtypeStruct((packs, length, width), jnp.bfloat16),
            jax.ShapeDtypeStruct((packs, length, width), jnp.bfloat16),
            jax.ShapeDtypeStruct((packs, length, width), jnp.bfloat16),
            jax.ShapeDtypeStruct((GROUP, 16, CQ * LANES), jnp.float32),
            jax.ShapeDtypeStruct((GROUP * GROUP, 8, LANES), jnp.float32),
            jax.ShapeDtypeStruct((8, width), jnp.float32),
        ],
        scratch_shapes=[
            pltpu.VMEM((GROUP, blocks, length + 8, LANES), jnp.float32),
            pltpu.VMEM((GROUP, 2 * LANES, CQ * LANES), jnp.float32),
            pltpu.VMEM((GROUP, padded, LANES), jnp.float32),
            pltpu.VMEM((length, width), jnp.float32),
        ],
        compiler_params=pltpu.CompilerParams(vmem_limit_bytes=48 << 20),
        name="attention_backward",
    )(mix, grad_grouped, attended, gain, q, k, v, starts, stops, probs, high, table_high, table_low)


def conv_tables(kernel):
    heads = kernel.shape[0]
    u = lax.broadcasted_iota(jnp.int32, (2 * LANES, CQ * LANES), 0)
    j = lax.broadcasted_iota(jnp.int32, (2 * LANES, CQ * LANES), 1) % LANES
    table = jnp.zeros((heads, 2 * LANES, CQ * LANES), jnp.float32)
    for b in range(CK):
        taps = jnp.repeat(kernel[:, :, b], LANES, axis=1)
        table = jnp.where((j - u + CK - 1 == b)[None], taps[:, None, :], table)
    return halves(table)


FLAT = ("seq", "wide")


def swapped(value, flip):
    total = lax.axis_size("seq") * lax.axis_size("wide")
    return lax.ppermute(value, FLAT, [(i, i ^ flip) for i in range(total)])


class Place:
    def __init__(self):
        self.wide_count = lax.axis_size("wide")
        self.depth = self.wide_count // 2
        self.seq = lax.axis_index("seq")
        wide = lax.axis_index("wide")
        self.y = wide % 2
        self.z = wide // 2
        self.plane = 2 * self.seq + self.y
        self.x_flip = 2 * self.wide_count
        self.core_flip = self.wide_count
        self.y_flip = 1
        seqs = range(lax.axis_size("seq"))
        self.plane_groups = [
            [s * self.wide_count + z * 2 + y for s in seqs for y in range(2)] for z in range(self.depth)
        ]
        self.line_groups = [[z * 2 + y for z in range(self.depth)] for y in range(2)]


CHIPS = (0, 4, 1, 5)


def plane_gather(place, value):
    near = [
        value,
        swapped(value, place.x_flip),
        swapped(value, place.y_flip),
        swapped(value, place.x_flip | place.y_flip),
    ]
    far = swapped(jnp.stack(near), place.core_flip)
    parts = [None] * 8
    for slot, k in enumerate(CHIPS):
        parts[k] = near[slot]
        parts[k | 2] = far[slot]
    return jnp.stack(parts)


def plane_scatter(place, terms):
    kept = jnp.stack([terms[k] for k in CHIPS])
    sent = jnp.stack([terms[k | 2] for k in CHIPS]).astype(jnp.bfloat16)
    total = kept + swapped(sent, place.core_flip).astype(jnp.float32)
    rounded = total.astype(jnp.bfloat16)
    flips = (place.x_flip, place.y_flip, place.x_flip | place.y_flip)
    result = total[0]
    for slot, flip in enumerate(flips):
        result = result + swapped(rounded[slot + 1], flip).astype(jnp.float32)
    return result


def plane_order(place, blocks):
    return jnp.concatenate(
        [lax.dynamic_slice_in_dim(blocks, i ^ place.plane, 1) for i in range(8)]
    )


def line_gather(place, value):
    parts = jnp.stack([value] + [swapped(value, 2 * k) for k in range(1, place.depth)])
    return jnp.concatenate(
        [lax.dynamic_slice_in_dim(parts, i ^ place.z, 1) for i in range(place.depth)]
    )


def line_scatter(place, blocks):
    total = lax.dynamic_index_in_dim(blocks, place.z, 0, keepdims=False)
    sent = [
        swapped(
            lax.dynamic_index_in_dim(blocks, place.z ^ k, 0, keepdims=False).astype(jnp.bfloat16),
            2 * k,
        )
        for k in range(1, place.depth)
    ]
    for part in sent:
        total = total + part.astype(jnp.float32)
    return total


def plane_exchange(place, blocks):
    return lax.all_to_all(blocks, FLAT, 0, 0, axis_index_groups=place.plane_groups)


def out_rows_gathered(place, rows):
    other = swapped(rows, place.y_flip)
    pair = jnp.where(
        place.y == 0, jnp.concatenate([rows, other]), jnp.concatenate([other, rows])
    )
    holds = place.z // 2 == place.y
    moved = {}
    for k in range(1, place.depth):
        pairs = [
            (s * place.wide_count + z * 2 + y, s * place.wide_count + (z ^ k) * 2 + y)
            for s in range(lax.axis_size("seq"))
            for z in range(place.depth)
            for y in range(2)
            if z // 2 == y
        ]
        moved[k] = lax.ppermute(pair, FLAT, pairs)
    first = jnp.where(holds, pair, moved[2])
    second = jnp.where(holds, moved[1], moved[3])
    return jnp.where(place.z % 2 == 0, jnp.stack([first, second]), jnp.stack([second, first]))


def out_rows_scattered(place, terms):
    half = terms.shape[1] // 2
    total = lax.dynamic_index_in_dim(terms, place.z % 2, 0, keepdims=False)
    for k in range(1, place.depth):
        pairs = [
            (s * place.wide_count + z * 2 + y, s * place.wide_count + (z ^ k) * 2 + y)
            for s in range(lax.axis_size("seq"))
            for z in range(place.depth)
            for y in range(2)
            if (z ^ k) // 2 == y
        ]
        sent = lax.dynamic_index_in_dim(terms, (place.z ^ k) % 2, 0, keepdims=False)
        total = total + lax.ppermute(sent.astype(jnp.bfloat16), FLAT, pairs).astype(jnp.float32)
    holds = place.z // 2 == place.y
    away = lax.dynamic_slice_in_dim(total, (1 - place.y) * half, half).astype(jnp.bfloat16)
    pairs = [
        (s * place.wide_count + z * 2 + z // 2, s * place.wide_count + z * 2 + 1 - z // 2)
        for s in range(lax.axis_size("seq"))
        for z in range(place.depth)
    ]
    got = lax.ppermute(away, FLAT, pairs).astype(jnp.float32)
    return jnp.where(holds, lax.dynamic_slice_in_dim(total, place.y * half, half), got)


def head_pad(count):
    rows = jnp.arange(HEAD_DIM * count)
    return jax.nn.one_hot(
        rows // HEAD_DIM * LANES + rows % HEAD_DIM, LANES * count, dtype=jnp.bfloat16
    )


def split_columns(value):
    half = value.shape[-2] // 2
    rest = value[..., 4 * LANES :]
    return value[..., : 4 * LANES], jnp.concatenate(
        [rest[..., :half, :], rest[..., half:, :]], axis=-1
    )


def join_columns(main, rest):
    half = LANES // 2
    return jnp.concatenate(
        [main, jnp.concatenate([rest[..., :half], rest[..., half:]], axis=-2)], axis=-1
    )


def plane_shards(
    tokens, segments, w_query, w_key, w_value, w_out, gain_attn, gain_group, gain_ffn,
    conv_kernel, head_mix, w_gate, w_up, w_down, cotangent,
):
    place = Place()
    seq_count = lax.axis_size("seq")
    depth = place.depth
    count = tokens.shape[1]
    length = count * seq_count
    width = tokens.shape[2]
    slab = w_query.shape[0]
    reach = (length // 2 - 1) // BLOCK + 1
    heads_width = GROUP * LANES
    cols = GROUP * HEAD_DIM
    bf16 = jnp.bfloat16
    f32 = jnp.float32

    stacked = jnp.stack([w_query, w_key, w_value]).astype(bf16)
    stacked = stacked.reshape(3, slab, 8, cols).transpose(2, 1, 0, 3).reshape(8, slab, 3 * cols)
    main, rest = split_columns(stacked)
    gains_own = jnp.stack([gain_attn, gain_group, gain_ffn]).astype(bf16)
    gains_own = jnp.pad(gains_own, ((0, 5), (0, LANES - slab)))
    rest = jnp.concatenate([rest, jnp.broadcast_to(gains_own[None], (8, 8, LANES))], axis=1)
    main, rest = plane_exchange(place, main), plane_exchange(place, rest)
    main, rest = line_gather(place, main), line_gather(place, rest)

    def by_rows(value):
        tail = value.shape[2:]
        value = value.reshape((depth, seq_count, 2) + tail)
        return jnp.swapaxes(value, 0, 1)

    main, rest = by_rows(main), by_rows(rest)
    gains = rest[:, :, :, slab // 2 :, :]
    gains = gains[..., :3, :slab].transpose(3, 0, 1, 2, 4).reshape(3, width).astype(f32)
    table = join_columns(main, rest[:, :, :, : slab // 2, :]).reshape(width, 3 * cols)
    w_attn = jnp.dot(table, head_pad(3 * GROUP), preferred_element_type=f32).astype(bf16)

    own_tokens = tokens[0]
    token_blocks = plane_order(place, plane_gather(place, own_tokens))

    def by_pack(blocks):
        return jnp.swapaxes(blocks.reshape((seq_count, 2) + blocks.shape[1:]), 0, 1)

    def by_plane(value):
        blocks = value.reshape((2, seq_count, count) + value.shape[2:])
        return jnp.swapaxes(blocks, 0, 1).reshape((8, count) + value.shape[2:])

    token_all = by_pack(token_blocks).reshape(2 * length, width)
    inputs_all = token_all.astype(f32)
    scale_all = lax.rsqrt(jnp.mean(inputs_all * inputs_all, axis=-1, keepdims=True) + epsilon)
    normed = (inputs_all * scale_all * gains[0]).astype(bf16)

    other_row = swapped(segments, place.y_flip)
    seg = jnp.where(
        place.y == 0,
        jnp.concatenate([segments, other_row]),
        jnp.concatenate([other_row, segments]),
    )
    starts = jnp.sum(seg[:, None, :] < seg[:, :, None], axis=-1, dtype=jnp.int32)
    stops = jnp.sum(seg[:, None, :] <= seg[:, :, None], axis=-1, dtype=jnp.int32)
    starts = jnp.broadcast_to(starts[:, :, None], (2, length, LANES))
    stops = jnp.broadcast_to(stops[:, :, None], (2, length, LANES))
    taps = lax.dynamic_slice_in_dim(conv_kernel, place.plane * GROUP, GROUP)
    mix = lax.dynamic_slice_in_dim(head_mix, place.plane * GROUP, GROUP)
    table_high, table_low = conv_tables(taps)
    gain_heads = lax.dynamic_slice_in_dim(gains[1], place.plane * cols, cols)
    gain_heads = jnp.pad(gain_heads.reshape(GROUP, HEAD_DIM), ((0, 0), (0, LANES - HEAD_DIM)))
    gain_heads = gain_heads.reshape(1, heads_width)

    sub = w_gate.shape[1] // seq_count
    deep = w_gate.shape[0]
    parts = deep // LANES
    ffn_own = jnp.stack(
        [
            w_gate.astype(bf16).reshape(deep, seq_count, sub).swapaxes(0, 1),
            w_up.astype(bf16).reshape(deep, seq_count, sub).swapaxes(0, 1),
            w_down.astype(bf16)
            .reshape(seq_count, sub, parts, LANES)
            .swapaxes(1, 2)
            .reshape(seq_count, deep, sub),
        ],
        axis=1,
    )
    ffn_own = lax.all_to_all(ffn_own, "seq", 0, 0)
    ffn_w = lax.all_gather(
        ffn_own, "wide", axis=0, tiled=False, axis_index_groups=place.line_groups
    )
    hidden_units = depth * sub
    w_gate_up = (
        ffn_w[:, :, :2].transpose(1, 3, 2, 0, 4).reshape(width, 2 * hidden_units)
    )
    w_down_all = (
        ffn_w[:, :, 2]
        .reshape(depth, seq_count, parts, sub, LANES)
        .transpose(0, 3, 1, 2, 4)
        .reshape(hidden_units, width)
    )
    w_out_heads = out_rows_gathered(place, w_out.astype(bf16))
    w_out_heads = jnp.pad(w_out_heads, ((0, 0), (0, LANES - HEAD_DIM), (0, 0)))
    w_out_heads = w_out_heads.reshape(heads_width, width)
    grad_out = cotangent[0]
    cot_all = plane_gather(place, grad_out).reshape(8 * count, width)

    qkv = jnp.dot(normed, w_attn, preferred_element_type=f32).astype(bf16)
    qkv = qkv.reshape(2, length, 3 * heads_width)
    queries = qkv[..., :heads_width]
    keys = jnp.pad(
        qkv[..., heads_width : 2 * heads_width], ((0, 0), (CK // 2, LANES - CK // 2), (0, 0))
    )
    values = qkv[..., 2 * heads_width :]
    probs, high, attended, grouped = attention_forward(
        mix, queries, keys, values, starts, table_high, table_low, gain_heads, reach
    )
    grouped_rel = plane_order(place, by_plane(grouped)).reshape(8 * count, heads_width)
    branch = jnp.dot(grouped_rel, w_out_heads, preferred_element_type=f32)
    middle = own_tokens.astype(f32) + plane_scatter(place, branch.reshape(8, count, width))

    scale_mid = lax.rsqrt(jnp.mean(middle * middle, axis=-1, keepdims=True) + epsilon)
    ffn_in = (middle * scale_mid * gains[2]).astype(bf16)
    ffn_all = plane_gather(place, ffn_in).reshape(8 * count, width)
    gate_up = jnp.dot(ffn_all, w_gate_up, preferred_element_type=f32)
    gate, up = gate_up[:, :hidden_units], gate_up[:, hidden_units:]
    grad_hidden = contract(cot_all, w_down_all, 1, 1)
    sig = jax.nn.sigmoid(gate)
    hidden = (gate * sig * up).astype(bf16)
    grad_gate = (grad_hidden * up * sig * (1.0 + gate * (1.0 - sig))).astype(bf16)
    grad_up = (grad_hidden * gate * sig).astype(bf16)
    grad_gate_up = jnp.concatenate([grad_gate, grad_up], axis=1)
    grad_ffn_in = plane_scatter(
        place, contract(grad_gate_up, w_gate_up, 1, 1).reshape(8, count, width)
    )
    ffn_out = plane_scatter(
        place, jnp.dot(hidden, w_down_all, preferred_element_type=f32).reshape(8, count, width)
    )
    output = (middle + ffn_out).astype(bf16)
    grad_gain_ffn = jnp.sum(grad_ffn_in * middle * scale_mid, axis=0)
    scaled = grad_ffn_in * gains[2]
    grad_middle = grad_out.astype(f32) + (
        scale_mid * scaled
        - middle
        * (scale_mid * scale_mid * scale_mid)
        * jnp.mean(scaled * middle, axis=-1, keepdims=True)
    )
    grad_branch = grad_middle.astype(bf16)

    grad_gu_w = contract(ffn_all, grad_gate_up, 0, 0).astype(bf16)
    grad_gu_w = grad_gu_w.reshape(seq_count, deep, 2, depth, sub).transpose(3, 0, 2, 1, 4)
    grad_down_w = contract(hidden, cot_all, 0, 0).astype(bf16)
    grad_down_w = (
        grad_down_w.reshape(depth, sub, seq_count, parts, LANES)
        .transpose(0, 2, 3, 1, 4)
        .reshape(depth, seq_count, 1, deep, sub)
    )
    ffn_g = lax.psum_scatter(
        jnp.concatenate([grad_gu_w, grad_down_w], axis=2),
        "wide",
        scatter_dimension=0,
        axis_index_groups=place.line_groups,
    )
    ffn_g = lax.all_to_all(ffn_g, "seq", 0, 0).astype(f32)
    grad_w_gate = ffn_g[:, 0].swapaxes(0, 1).reshape(deep, seq_count * sub)
    grad_w_up = ffn_g[:, 1].swapaxes(0, 1).reshape(deep, seq_count * sub)
    grad_w_down = (
        ffn_g[:, 2]
        .reshape(seq_count, parts, sub, LANES)
        .swapaxes(1, 2)
        .reshape(seq_count * sub, deep)
    )

    branch_blocks = plane_order(place, plane_gather(place, grad_branch))
    branch_all = by_pack(branch_blocks).reshape(2 * length, width)
    grad_grouped = contract(branch_all, w_out_heads, 1, 1).reshape(2, length, heads_width)
    grad_w_out = contract(grouped.reshape(2 * length, heads_width), branch_all, 0, 0)
    grad_w_out = out_rows_scattered(
        place, grad_w_out.reshape(GROUP, LANES, width)[:, :HEAD_DIM]
    )
    grad_q, grad_k, grad_v, grad_taps, grad_mix, grad_gain_group = attention_backward(
        mix, grad_grouped, attended, gain_heads, queries, keys, values, starts, stops,
        probs, high, table_high, table_low, reach,
    )
    grad_qkv = jnp.concatenate([grad_q, grad_k, grad_v], axis=-1)
    grad_rel = plane_order(place, by_plane(grad_qkv)).reshape(8 * count, 3 * heads_width)
    normed_part = contract(grad_rel, w_attn, 1, 1)
    grad_normed = plane_scatter(place, normed_part.reshape(8, count, width))

    grad_table = contract(normed, grad_qkv.reshape(2 * length, 3 * heads_width), 0, 0)
    grad_table = contract(grad_table.astype(bf16), head_pad(3 * GROUP), 1, 1).astype(bf16)
    grad_table = jnp.swapaxes(
        grad_table.reshape(seq_count, depth, 2, slab, 3 * cols), 0, 1
    ).reshape(depth, 8, slab, 3 * cols)
    main, rest = split_columns(grad_table)
    main = line_scatter(place, main.astype(f32)).astype(bf16)
    rest = line_scatter(place, rest.astype(f32)).astype(bf16)
    main, rest = plane_exchange(place, main), plane_exchange(place, rest)
    grad_rows = join_columns(main, rest).reshape(8, slab, 3, cols).transpose(2, 1, 0, 3)
    grad_rows = grad_rows.reshape(3, slab, width).astype(f32)

    inputs = own_tokens.astype(f32)
    scale_in = lax.rsqrt(jnp.mean(inputs * inputs, axis=-1, keepdims=True) + epsilon)
    grad_gain_attn = jnp.sum(grad_normed * inputs * scale_in, axis=0)
    scaled_in = grad_normed * gains[0]
    grad_tokens = (
        grad_middle
        + scale_in * scaled_in
        - inputs
        * (scale_in * scale_in * scale_in)
        * jnp.mean(scaled_in * inputs, axis=-1, keepdims=True)
    ).astype(bf16)

    tap_sums = grad_taps[:, :CK].reshape(GROUP, CK, CQ, LANES).sum(-1).swapaxes(1, 2)
    mix_sums = grad_mix.sum((1, 2)).reshape(GROUP, GROUP)
    group_sums = grad_gain_group.sum(0).reshape(GROUP, LANES)[:, :HEAD_DIM].reshape(cols)

    def placed(value, full, start):
        return lax.dynamic_update_slice_in_dim(jnp.zeros(full, f32), value, start, 0)

    small = [
        grad_gain_attn,
        grad_gain_ffn,
        placed(group_sums, (width,), place.plane * cols),
        placed(tap_sums, (HEADS, CQ, CK), place.plane * GROUP).reshape(-1),
        placed(mix_sums, (HEADS, GROUP), place.plane * GROUP).reshape(-1),
    ]
    sizes = [value.shape[0] for value in small]
    flat = jnp.concatenate(small)
    padded = -flat.shape[0] % (8 * LANES)
    flat = jnp.pad(flat, (0, padded)).reshape(-1, LANES)
    for flip in (place.core_flip, place.x_flip, place.y_flip, 2, 4):
        flat = flat + swapped(flat, flip)
    flat = flat.reshape(-1)
    row = (place.seq * place.wide_count + lax.axis_index("wide")) * slab
    gain_grads = [
        lax.dynamic_slice_in_dim(flat, i * width + row, slab) for i in range(3)
    ]
    at = 3 * width
    grad_conv = flat[at : at + sizes[3]].reshape(HEADS, CQ, CK)
    grad_head_mix = flat[at + sizes[3] : at + sizes[3] + sizes[4]].reshape(HEADS, GROUP)
    return (
        output[None],
        grad_tokens[None],
        grad_rows[0],
        grad_rows[1],
        grad_rows[2],
        grad_w_out,
        gain_grads[0],
        gain_grads[2],
        gain_grads[1],
        grad_conv,
        grad_head_mix,
        grad_w_gate,
        grad_w_up,
        grad_w_down,
    )


def solution(mesh):
    planes = mesh.shape["seq"] == 4 and mesh.shape["wide"] == 8
    return jax.shard_map(
        plane_shards if planes else shards,
        mesh=mesh,
        in_specs=(
            P("wide", "seq", None),
            P("wide", None),
            P(("seq", "wide"), None),
            P(("seq", "wide"), None),
            P(("seq", "wide"), None),
            P(("seq", "wide"), None),
            P(("seq", "wide")),
            P(("seq", "wide")),
            P(("seq", "wide")),
            P(),
            P(),
            P("seq", "wide"),
            P("seq", "wide"),
            P("wide", "seq"),
            P("wide", "seq", None),
        ),
        out_specs=(
            P("wide", "seq", None),
            P("wide", "seq", None),
            P(("seq", "wide"), None),
            P(("seq", "wide"), None),
            P(("seq", "wide"), None),
            P(("seq", "wide"), None),
            P(("seq", "wide")),
            P(("seq", "wide")),
            P(("seq", "wide")),
            P(),
            P(),
            P("seq", "wide"),
            P("seq", "wide"),
            P("wide", "seq"),
        ),
        check_vma=False,
    )
```

```python
import functools

import jax
import jax.numpy as jnp
from jax import lax
from jax.experimental import pallas as pl
from jax.experimental.pallas import tpu as pltpu
from jax.sharding import PartitionSpec as P

HEADS = 16
HEAD_DIM = 96
CQ = 6
CK = 11
GROUP = 2
LANES = 128
BLOCK = 128
RIM = 16


precise = lax.Precision.HIGHEST
epsilon = 1e-05


def passed_along(value, axis, by):
    devices = lax.axis_size(axis)
    pairs = [(i, i + by) for i in range(devices) if 0 <= i + by < devices]
    return lax.ppermute(value, axis, pairs)


def extended(block, sides, width):
    for axis, dim in sides:
        count = lax.axis_size(axis)
        forward = [(i, i + 1) for i in range(count - 1)]
        backward = [(target, source) for source, target in forward]
        low = lax.ppermute(
            lax.slice_in_dim(block, block.shape[dim] - width, None, axis=dim), axis, forward
        )
        high = lax.ppermute(lax.slice_in_dim(block, 0, width, axis=dim), axis, backward)
        block = jnp.concatenate([low, block, high], axis=dim)
    return block


def rms_scaled(values, gain_vec):
    return (
        values * lax.rsqrt(jnp.mean(values * values, axis=-1, keepdims=True) + epsilon) * gain_vec
    )


def group_scaled(values, gain_vec):
    center = values - jnp.mean(values, axis=-1, keepdims=True)
    spread = jnp.mean(center * center, axis=-1, keepdims=True)
    return center * lax.rsqrt(spread + epsilon) * gain_vec


def tile_masks(seg_query, pos_query, seg_key, pos_key, valid_flag):
    query_rim = CQ - 1
    key_rim = CK // 2
    allowed = (
        (seg_query[:, None] == seg_key[None, :])
        & (pos_key[None, :] <= pos_query[:, None])
        & valid_flag
    )
    row_count = seg_query.shape[0] - query_rim
    row_masks = jnp.stack(
        [
            (
                seg_query[query_rim - shift_q : query_rim - shift_q + row_count]
                == seg_query[query_rim:]
            ).astype(jnp.float32)
            for shift_q in range(CQ)
        ]
    )
    final_mask = allowed[query_rim:, key_rim : key_rim + row_count]
    return (allowed, row_masks, final_mask)


def convolve(scores, allowed, row_masks, kernel):
    query_rim = CQ - 1
    key_rim = CK // 2
    row_count = scores.shape[1] - query_rim
    col_count = scores.shape[2] - 2 * key_rim
    masked = jnp.where(allowed[None], scores, 0.0)
    summed = jnp.zeros((scores.shape[0], row_count, col_count), jnp.float32)
    for shift_q in range(CQ):
        inner_sum = jnp.zeros((scores.shape[0], row_count, col_count), jnp.float32)
        for shift_k in range(CK):
            piece_view = masked[
                :,
                query_rim - shift_q : query_rim - shift_q + row_count,
                2 * key_rim - shift_k : 2 * key_rim - shift_k + col_count,
            ]
            inner_sum = inner_sum + kernel[:, shift_q, shift_k][:, None, None] * piece_view
        summed = summed + row_masks[shift_q][None, :, None] * inner_sum
    return summed


def mix_heads(probs, head_mix):
    lead_dims = probs.shape[:-3]
    tail_dims = probs.shape[-2:]
    grouped = probs.reshape(lead_dims + (HEADS // GROUP, GROUP) + tail_dims)
    mixing = head_mix.reshape(HEADS // GROUP, GROUP, GROUP)
    summed = jnp.zeros(lead_dims + (HEADS // GROUP, GROUP) + tail_dims, jnp.float32)
    for source in range(GROUP):
        summed = summed + mixing[:, :, source][:, :, None, None] * jnp.expand_dims(
            grouped[..., :, source, :, :], -3
        )
    return summed.reshape(probs.shape)


def unmix_heads(grads, head_mix):
    lead_dims = grads.shape[:-3]
    tail_dims = grads.shape[-2:]
    grouped = grads.reshape(lead_dims + (HEADS // GROUP, GROUP) + tail_dims)
    mixing = head_mix.reshape(HEADS // GROUP, GROUP, GROUP)
    summed = jnp.zeros(lead_dims + (HEADS // GROUP, GROUP) + tail_dims, jnp.float32)
    for target in range(GROUP):
        summed = summed + mixing[:, target, :][:, :, None, None] * jnp.expand_dims(
            grouped[..., :, target, :, :], -3
        )
    return summed.reshape(grads.shape)


def contract(left_op, right_op, left_dim, right_dim):
    return lax.dot_general(
        left_op,
        right_op,
        (((left_dim,), (right_dim,)), ((), ())),
        preferred_element_type=jnp.float32,
    )


def gather_attention(w_query, w_key, w_value, w_out, gain_attn, gain_group, gain_ffn):
    return (
        lax.all_gather(w_query.astype(jnp.bfloat16), ("seq", "wide"), axis=0, tiled=True),
        lax.all_gather(w_key.astype(jnp.bfloat16), ("seq", "wide"), axis=0, tiled=True),
        lax.all_gather(w_value.astype(jnp.bfloat16), ("seq", "wide"), axis=0, tiled=True),
        lax.all_gather(w_out.astype(jnp.bfloat16), ("seq", "wide"), axis=0, tiled=True),
        lax.all_gather(gain_attn.astype(jnp.bfloat16), ("seq", "wide"), axis=0, tiled=True),
        lax.all_gather(gain_group.astype(jnp.bfloat16), ("seq", "wide"), axis=0, tiled=True),
        lax.all_gather(gain_ffn.astype(jnp.bfloat16), ("seq", "wide"), axis=0, tiled=True),
    )


def collect_packets(own, reach_len):
    stored = jnp.zeros((reach_len,) + own.shape, own.dtype).at[0].set(own)

    def advance(turn_index, state_pair):
        packet, stored_now = state_pair
        packet = passed_along(packet, "seq", 1)
        return (packet, lax.dynamic_update_index_in_dim(stored_now, packet, turn_index, 0))

    return lax.fori_loop(1, reach_len, advance, (own, stored))[1]


def tile_logits(query_ext, packet, seg_query, pos_query, seg_key_pad, other_shard, token_count):
    key_rim = CK // 2
    key_ext = packet[: token_count + 2 * key_rim].reshape(
        token_count + 2 * key_rim, HEADS, HEAD_DIM
    )
    scores = jnp.einsum(
        "qhe,khe->hqk", query_ext, key_ext, preferred_element_type=jnp.float32
    ) * HEAD_DIM ** (-0.5)
    key_start = other_shard * token_count
    seg_key = lax.dynamic_slice_in_dim(
        seg_key_pad, jnp.maximum(key_start, 0), token_count + 2 * key_rim
    )
    pos_key = key_start - key_rim + jnp.arange(token_count + 2 * key_rim, dtype=jnp.int32)
    allowed, row_masks, final_mask = tile_masks(
        seg_query, pos_query, seg_key, pos_key, other_shard >= 0
    )
    return (scores, allowed, row_masks, final_mask, key_ext)


def shards(
    tokens,
    segments,
    w_query,
    w_key,
    w_value,
    w_out,
    gain_attn,
    gain_group,
    gain_ffn,
    conv_kernel,
    head_mix,
    w_gate,
    w_up,
    w_down,
    cotangent,
):
    token_count = tokens.shape[1]
    query_rim = CQ - 1
    key_rim = CK // 2
    width_all = HEADS * HEAD_DIM
    scaling = HEAD_DIM ** (-0.5)
    seq_count = lax.axis_size("seq")
    longest_doc = min(1024, token_count * seq_count // 2)
    reach_len = min(seq_count - 1, (longest_doc - 1) // token_count + 1) + 1
    seq_index = lax.axis_index("seq")
    row_start = seq_index * token_count
    seg_row = segments[0]
    seg_query_pad = jnp.concatenate([jnp.full((query_rim,), -1, jnp.int32), seg_row])
    seg_key_pad = jnp.concatenate(
        [jnp.full((key_rim,), -2, jnp.int32), seg_row, jnp.full((key_rim,), -2, jnp.int32)]
    )
    seg_query = lax.dynamic_slice_in_dim(seg_query_pad, row_start, token_count + query_rim)
    pos_query = row_start - query_rim + jnp.arange(token_count + query_rim, dtype=jnp.int32)
    weights = gather_attention(w_query, w_key, w_value, w_out, gain_attn, gain_group, gain_ffn)
    query_mat, key_mat, value_mat, out_mat, gain_one, gain_mid, gain_two = weights
    inputs = tokens[0].astype(jnp.float32)
    gain_first = gain_one.astype(jnp.float32)
    normed = rms_scaled(inputs, gain_first).astype(jnp.bfloat16)
    queries = jnp.dot(normed, query_mat, preferred_element_type=jnp.float32).astype(jnp.bfloat16)
    keys_loc = jnp.dot(normed, key_mat, preferred_element_type=jnp.float32).astype(jnp.bfloat16)
    values_loc = jnp.dot(normed, value_mat, preferred_element_type=jnp.float32).astype(jnp.bfloat16)
    rimmed = extended(jnp.stack([queries, keys_loc]), (("seq", 1),), key_rim)
    query_ext = rimmed[0, : token_count + query_rim].reshape(
        token_count + query_rim, HEADS, HEAD_DIM
    )
    own = jnp.concatenate([rimmed[1], values_loc], axis=0)
    packets = collect_packets(own, reach_len)

    def all_logits(packet_stack):

        def logits_of(turn_index):
            packet = lax.dynamic_index_in_dim(packet_stack, turn_index, 0, keepdims=False)
            scores, allowed, row_masks, final_mask, key_ext = tile_logits(
                query_ext,
                packet,
                seg_query,
                pos_query,
                seg_key_pad,
                seq_index - turn_index,
                token_count,
            )
            return jnp.where(
                final_mask[None], convolve(scores, allowed, row_masks, conv_kernel), -jnp.inf
            )

        return lax.map(logits_of, jnp.arange(reach_len, dtype=jnp.int32))

    logits = all_logits(packets)
    peak_val = jnp.max(logits, axis=(0, 3))
    log_total = peak_val + jnp.log(
        jnp.sum(jnp.exp(logits - peak_val[None, :, :, None]), axis=(0, 3))
    )
    probs_all = jnp.exp(logits - log_total[None, :, :, None])
    mixed_b = mix_heads(probs_all, head_mix).astype(jnp.bfloat16)
    values_all = packets[:, token_count + 2 * key_rim :].reshape(
        reach_len, token_count, HEADS, HEAD_DIM
    )
    attended = jnp.einsum("rhtk,rkhe->the", mixed_b, values_all, preferred_element_type=jnp.float32)
    gain_middle = gain_mid.astype(jnp.float32).reshape(HEADS, HEAD_DIM)
    grouped = (
        group_scaled(attended, gain_middle).reshape(token_count, width_all).astype(jnp.bfloat16)
    )
    middle = inputs + jnp.dot(grouped, out_mat, preferred_element_type=jnp.float32)
    gain_second = gain_two.astype(jnp.float32)
    ffn_in = rms_scaled(middle, gain_second).astype(jnp.bfloat16)
    ffn_all = lax.all_gather(ffn_in, "wide", axis=0, tiled=True)
    gate_mat, up_mat, down_mat = (
        lax.all_gather(w_gate.astype(jnp.bfloat16), "seq", axis=0, tiled=True),
        lax.all_gather(w_up.astype(jnp.bfloat16), "seq", axis=0, tiled=True),
        lax.all_gather(w_down.astype(jnp.bfloat16), "seq", axis=1, tiled=True),
    )
    gate_val = jnp.dot(ffn_all, gate_mat, preferred_element_type=jnp.float32)
    up_val = jnp.dot(ffn_all, up_mat, preferred_element_type=jnp.float32)
    hidden = (jax.nn.silu(gate_val) * up_val).astype(jnp.bfloat16)
    ffn_out = lax.psum_scatter(
        jnp.dot(hidden, down_mat, preferred_element_type=jnp.float32).astype(jnp.bfloat16),
        "wide",
        scatter_dimension=0,
        tiled=True,
    ).astype(jnp.float32)
    output = (middle + ffn_out).astype(jnp.bfloat16)
    grad_out = cotangent[0]
    grad_all = lax.all_gather(grad_out, "wide", axis=0, tiled=True)
    grad_hidden = contract(grad_all, down_mat, 1, 1)
    grad_down = contract(hidden, grad_all, 0, 0)
    sig_gate = jax.nn.sigmoid(gate_val)
    grad_gate = (grad_hidden * up_val * sig_gate * (1.0 + gate_val * (1.0 - sig_gate))).astype(
        jnp.bfloat16
    )
    grad_up = (grad_hidden * gate_val * sig_gate).astype(jnp.bfloat16)
    grad_gate_w = contract(ffn_all, grad_gate, 0, 0)
    grad_up_w = contract(ffn_all, grad_up, 0, 0)
    grad_ffn_in = lax.psum_scatter(
        (contract(grad_gate, gate_mat, 1, 1) + contract(grad_up, up_mat, 1, 1)).astype(
            jnp.bfloat16
        ),
        "wide",
        scatter_dimension=0,
        tiled=True,
    ).astype(jnp.float32)
    ffn_grads = (
        lax.psum_scatter(
            grad_gate_w.astype(jnp.bfloat16), "seq", scatter_dimension=0, tiled=True
        ).astype(jnp.float32),
        lax.psum_scatter(
            grad_up_w.astype(jnp.bfloat16), "seq", scatter_dimension=0, tiled=True
        ).astype(jnp.float32),
        lax.psum_scatter(
            grad_down.astype(jnp.bfloat16), "seq", scatter_dimension=1, tiled=True
        ).astype(jnp.float32),
    )
    norm_two_back = jax.vjp(rms_scaled, middle, gain_second)[1]
    grad_mid_part, grad_gain_two = norm_two_back(grad_ffn_in)
    grad_middle = grad_out.astype(jnp.float32) + grad_mid_part
    grad_branch = grad_middle.astype(jnp.bfloat16)
    back_weights = gather_attention(w_query, w_key, w_value, w_out, gain_attn, gain_group, gain_ffn)
    query_back, key_back, value_back, out_back = (
        back_weights[0],
        back_weights[1],
        back_weights[2],
        back_weights[3],
    )
    grad_grouped = contract(grad_branch, out_back, 1, 1)
    grad_out_w = contract(grouped, grad_branch, 0, 0)
    group_back = jax.vjp(group_scaled, attended, gain_middle)[1]
    grad_attended, grad_gain_mid = group_back(grad_grouped.reshape(token_count, HEADS, HEAD_DIM))
    grad_att_b = grad_attended.astype(jnp.bfloat16)
    back_packets = collect_packets(own, reach_len)
    logits_again = all_logits(back_packets)
    probs_again = jnp.exp(logits_again - log_total[None, :, :, None])
    mixed_again = mix_heads(probs_again, head_mix).astype(jnp.bfloat16)
    values_back = back_packets[:, token_count + 2 * key_rim :].reshape(
        reach_len, token_count, HEADS, HEAD_DIM
    )
    grad_mixed = jnp.einsum(
        "the,rkhe->rhtk", grad_att_b, values_back, preferred_element_type=jnp.float32
    )
    grad_values = jnp.einsum(
        "rhtk,the->rkhe", mixed_again, grad_att_b, preferred_element_type=jnp.float32
    ).reshape(reach_len, token_count, width_all)
    probs_grouped = probs_again.reshape(reach_len, HEADS // GROUP, GROUP, token_count, token_count)
    mixed_grouped = grad_mixed.reshape(reach_len, HEADS // GROUP, GROUP, token_count, token_count)
    grad_mix = jnp.einsum(
        "rgdtk,rgctk->gcd", probs_grouped, mixed_grouped, precision=precise
    ).reshape(HEADS, GROUP)
    grad_probs = unmix_heads(grad_mixed, head_mix)
    delta_row = jnp.sum(probs_again * grad_probs, axis=(0, 3))
    grad_logits = probs_again * (grad_probs - delta_row[None, :, :, None])

    def tile_grads(turn_index):
        packet = lax.dynamic_index_in_dim(back_packets, turn_index, 0, keepdims=False)
        scores, allowed, row_masks, final_mask, key_ext = tile_logits(
            query_ext,
            packet,
            seg_query,
            pos_query,
            seg_key_pad,
            seq_index - turn_index,
            token_count,
        )
        conv_back = jax.vjp(
            lambda field, weights_k: convolve(field, allowed, row_masks, weights_k),
            scores,
            conv_kernel,
        )[1]
        grad_scores, grad_kernel = conv_back(
            lax.dynamic_index_in_dim(grad_logits, turn_index, 0, keepdims=False)
        )
        grad_scores_b = grad_scores.astype(jnp.bfloat16)
        grad_query_ext = (
            jnp.einsum("hqk,khe->qhe", grad_scores_b, key_ext, preferred_element_type=jnp.float32)
            * scaling
        )
        grad_key_ext = (
            jnp.einsum("hqk,qhe->khe", grad_scores_b, query_ext, preferred_element_type=jnp.float32)
            * scaling
        )
        cycle_term = jnp.concatenate(
            [
                grad_key_ext.reshape(token_count + 2 * key_rim, width_all),
                lax.dynamic_index_in_dim(grad_values, turn_index, 0, keepdims=False),
            ],
            axis=0,
        )
        return (cycle_term, grad_query_ext, grad_kernel)

    start_term, start_query, start_kernel = tile_grads(reach_len - 1)

    def descend(turn_index, state_all):
        cycle_acc, query_acc, kernel_acc = state_all
        cycle_term, query_part, kernel_part = tile_grads(reach_len - 1 - turn_index)
        moved_acc = passed_along(cycle_acc.astype(jnp.bfloat16), "seq", -1).astype(cycle_acc.dtype)
        return (moved_acc + cycle_term, query_acc + query_part, kernel_acc + kernel_part)

    cycle_acc, query_acc, kernel_acc = lax.fori_loop(
        1, reach_len, descend, (start_term, start_query, start_kernel)
    )
    query_flat = query_acc.reshape(token_count + query_rim, width_all)
    key_ext_grad = cycle_acc[: token_count + 2 * key_rim]
    grad_values_own = cycle_acc[token_count + 2 * key_rim :]
    edge_grads = jnp.stack(
        [
            jnp.concatenate([query_flat[:query_rim], jnp.zeros((key_rim, width_all), jnp.float32)]),
            jnp.concatenate([key_ext_grad[:key_rim], key_ext_grad[token_count + key_rim :]]),
        ]
    )
    rim_back = extended(edge_grads.astype(jnp.bfloat16), (("seq", 1),), key_rim).astype(
        edge_grads.dtype
    )
    grad_queries = (
        query_flat[query_rim:].at[token_count - key_rim :].add(rim_back[0, 3 * key_rim :])
    )
    grad_keys = (
        key_ext_grad[key_rim : key_rim + token_count]
        .at[:key_rim]
        .add(rim_back[1, :key_rim])
        .at[token_count - key_rim :]
        .add(rim_back[1, 3 * key_rim :])
    )
    grad_query_b = grad_queries.astype(jnp.bfloat16)
    grad_key_b = grad_keys.astype(jnp.bfloat16)
    grad_value_b = grad_values_own.astype(jnp.bfloat16)
    grad_query_w = contract(normed, grad_query_b, 0, 0)
    grad_key_w = contract(normed, grad_key_b, 0, 0)
    grad_value_w = contract(normed, grad_value_b, 0, 0)
    grad_normed = (
        contract(grad_query_b, query_back, 1, 1)
        + contract(grad_key_b, key_back, 1, 1)
        + contract(grad_value_b, value_back, 1, 1)
    )
    norm_one_back = jax.vjp(rms_scaled, inputs, gain_first)[1]
    grad_in_part, grad_gain_one = norm_one_back(grad_normed)
    grad_input = (grad_middle + grad_in_part).astype(jnp.bfloat16)
    attn_grads = (
        lax.psum_scatter(grad_query_w, ("seq", "wide"), scatter_dimension=0, tiled=True),
        lax.psum_scatter(grad_key_w, ("seq", "wide"), scatter_dimension=0, tiled=True),
        lax.psum_scatter(grad_value_w, ("seq", "wide"), scatter_dimension=0, tiled=True),
        lax.psum_scatter(grad_out_w, ("seq", "wide"), scatter_dimension=0, tiled=True),
        lax.psum_scatter(grad_gain_one, ("seq", "wide"), scatter_dimension=0, tiled=True),
        lax.psum_scatter(
            grad_gain_mid.reshape(width_all), ("seq", "wide"), scatter_dimension=0, tiled=True
        ),
        lax.psum_scatter(grad_gain_two, ("seq", "wide"), scatter_dimension=0, tiled=True),
    )
    small_sums = lax.psum((kernel_acc, grad_mix), ("seq", "wide"))
    return (
        output[None],
        grad_input[None],
        attn_grads[0],
        attn_grads[1],
        attn_grads[2],
        attn_grads[3],
        attn_grads[4],
        attn_grads[5],
        attn_grads[6],
        small_sums[0],
        small_sums[1],
        ffn_grads[0],
        ffn_grads[1],
        ffn_grads[2],
    )


def dot_plain(left, right):
    return contract(left, right, 1, 0)


def dot_nt(left, right):
    return contract(left, right, 1, 1)


def dot_tn(left, right):
    return contract(left, right, 0, 0)


def halves(value):
    high = value.astype(jnp.bfloat16)
    return high, (value - high.astype(jnp.float32)).astype(jnp.bfloat16)


def iota(shape, dim):
    return lax.broadcasted_iota(jnp.int32, shape, dim)


def spread_lanes(tile, count):
    return tile if count == 1 else jnp.concatenate([tile] * count, axis=1)


def allowed_mask(starts, block, first_col, count):
    cols = iota((BLOCK, count * LANES), 1) + first_col
    rows = iota((BLOCK, count * LANES), 0) + block * BLOCK
    return (cols >= spread_lanes(starts, count)) & (cols <= rows)


def head_stats(values):
    lane = iota(values.shape, 1)
    mean = jnp.sum(values, axis=-1, keepdims=True) * (1.0 / HEAD_DIM)
    center = jnp.where(lane < HEAD_DIM, values - mean, 0.0)
    spread = jnp.sum(center * center, axis=-1, keepdims=True) * (1.0 / HEAD_DIM)
    inverse = lax.rsqrt(spread + epsilon)
    return center * inverse, inverse


def fold_rows(value):
    return jnp.sum(value.reshape(value.shape[0] // 8, 8, value.shape[1]), axis=0)


def full_spec():
    return pl.BlockSpec(memory_space=pltpu.VMEM)


def smem_spec():
    return pl.BlockSpec(memory_space=pltpu.SMEM)


def shape_of(shape, dtype=jnp.bfloat16):
    return jax.ShapeDtypeStruct(shape, dtype)


def kernel_call(body, name, outs, ins, scratch=(), flops=0, smem=0, vmem=40, lazy=0):
    moved = sum(v.size * v.dtype.itemsize for v in ins) + sum(
        o.size * o.dtype.itemsize for o in outs
    )
    return pl.pallas_call(
        body,
        in_specs=[smem_spec()] * smem
        + [full_spec()] * (len(ins) - smem - lazy)
        + [pl.BlockSpec(memory_space=pl.ANY)] * lazy,
        out_specs=[full_spec()] * len(outs),
        out_shape=list(outs),
        scratch_shapes=[pltpu.VMEM(v.shape, v.dtype) for v in ins[len(ins) - lazy :]]
        + [pltpu.SemaphoreType.DMA((lazy,))] * min(lazy, 1)
        + list(scratch),
        compiler_params=pltpu.CompilerParams(vmem_limit_bytes=vmem << 20),
        cost_estimate=pl.CostEstimate(flops=flops, bytes_accessed=moved, transcendentals=0),
        name=name,
    )(*ins)


ORDER = (0, 4, 1, 5, 2, 6, 3, 7)


def slot_place(plane, slot):
    other = plane ^ ORDER[slot]
    return other & 1, pl.multiple_of((other >> 1) * BLOCK, BLOCK)


def half_tile(tiles, index):
    tile = tiles[index // 2]
    return tile, pltpu.roll(tile, LANES // 2, 1), index % 2


def joined(first, second):
    low = first[1] if first[2] else first[0]
    high = second[0] if second[2] else second[1]
    lane = iota(low.shape, 1)
    return jnp.where(lane < LANES // 2, low, high)


def pack_kernel(slab, q_ref, k_ref, v_ref, gains_ref, rows_ref, out_ref, rows_out_ref):
    tiles = [
        [ref[:, t * LANES : (t + 1) * LANES] for t in range(ref.shape[1] // LANES)]
        for ref in (q_ref, k_ref, v_ref)
    ]
    per = GROUP * HEAD_DIM // (LANES // 2)
    for g in range(8):
        parts = [half_tile(tiles[w], per * g + i) for w in range(3) for i in range(per)]
        for t in range(4):
            out_ref[g, t * slab : (t + 1) * slab, :] = joined(
                parts[2 * t], parts[2 * t + 1]
            ).astype(jnp.bfloat16)
        tile, turned, side = parts[8]
        first, second = (turned, tile) if side else (tile, turned)
        half = slab // 2
        lane = iota((half, LANES), 1)
        out_ref[g, 4 * slab : 4 * slab + half, :] = jnp.where(
            lane < LANES // 2, first[:half], second[half:]
        ).astype(jnp.bfloat16)
        out_ref[g, 4 * slab + half :, :] = gains_ref[...]
    for t in range(rows_ref.shape[1] // LANES):
        rows_out_ref[t * slab : (t + 1) * slab, :] = rows_ref[
            :, t * LANES : (t + 1) * LANES
        ].astype(jnp.bfloat16)


def unpack_kernel(slab, in_ref, rows_ref, q_ref, k_ref, v_ref, out_ref):
    per = GROUP * HEAD_DIM // (LANES // 2)
    pieces = [[], [], []]
    half = slab // 2
    lane = iota((half, LANES), 1)
    for g in range(8):
        tiles = [
            in_ref[g, t * slab : (t + 1) * slab, :].astype(jnp.float32) for t in range(4)
        ]
        rest = in_ref[g, 4 * slab : 4 * slab + half, :].astype(jnp.float32)
        turned = pltpu.roll(rest, LANES // 2, 1)
        tiles.append(jnp.concatenate([rest, turned], axis=0))
        for i in range(3 * per):
            pieces[i // per].append(half_tile(tiles, i))
    for ref, parts in zip((q_ref, k_ref, v_ref), pieces):
        for t in range(len(parts) // 2):
            ref[:, t * LANES : (t + 1) * LANES] = joined(parts[2 * t], parts[2 * t + 1])
    for t in range(out_ref.shape[1] // LANES):
        out_ref[:, t * LANES : (t + 1) * LANES] = rows_ref[t * slab : (t + 1) * slab, :].astype(
            jnp.float32
        )


def attend_pack(p, blocks, reach, mix_ref, q_ref, k_ref, v_ref, start_ref, th_ref, tl_ref, gain,
                probs_ref, high_ref, att_ref, grouped_ref, low_ref, part_ref):
    key_rim = CK // 2
    scaling = HEAD_DIM ** (-0.5)
    for h in range(GROUP):
        lanes = slice(h * LANES, (h + 1) * LANES)
        high_ref[p, h, :RIM, :] = jnp.zeros((RIM, high_ref.shape[3]), jnp.bfloat16)
        low_ref[h, :RIM, :] = jnp.zeros((RIM, high_ref.shape[3]), jnp.bfloat16)
        for n in range(blocks):
            first, last = max(0, n - reach), min(n + 3, blocks + 1)
            rows = slice(n * BLOCK, (n + 1) * BLOCK)
            scores = (
                dot_nt(q_ref[p, rows, lanes], k_ref[p, first * BLOCK : last * BLOCK, lanes]) * scaling
            )
            keep = allowed_mask(start_ref[p, rows, :], n, first * BLOCK - key_rim, last - first)
            high, low = halves(jnp.where(keep, scores, 0.0))
            into = slice(RIM + n * BLOCK, RIM + (n + 1) * BLOCK)
            cols = slice(first * LANES, last * LANES)
            high_ref[p, h, into, cols] = high
            low_ref[h, into, cols] = low
    for n in range(blocks):
        first = max(0, n - reach)
        count = n - first + 1
        rows = slice(n * BLOCK, (n + 1) * BLOCK)
        starts = start_ref[p, rows, :]
        offset = iota((BLOCK, LANES), 0) + n * BLOCK - starts
        keep = allowed_mask(starts, n, first * BLOCK, count)
        window = slice((reach + 1 - count) * LANES, (reach + 1) * LANES)
        probs = []
        for h in range(GROUP):
            pieces = []
            for m in range(first, n + 1):
                rim_rows = slice(n * BLOCK, (n + 1) * BLOCK + RIM)
                cols = slice(m * LANES, (m + 2) * LANES)
                high = high_ref[p, h, rim_rows, cols]
                low = low_ref[h, rim_rows, cols]
                part = (
                    dot_plain(high, th_ref[h])
                    + dot_plain(low, th_ref[h])
                    + dot_plain(high, tl_ref[h])
                )
                for a in range(CQ):
                    part_ref[a] = part[:, a * LANES : (a + 1) * LANES]
                total = part_ref[0, RIM:, :]
                for a in range(1, CQ):
                    total = total + jnp.where(
                        offset >= a, part_ref[a, RIM - a : RIM - a + BLOCK, :], 0.0
                    )
                pieces.append(total)
            logits = pieces[0] if count == 1 else jnp.concatenate(pieces, axis=1)
            logits = jnp.where(keep, logits, -jnp.inf)
            peak = jnp.max(logits, axis=-1, keepdims=True)
            raised = jnp.exp(logits - peak)
            prob = raised / jnp.sum(raised, axis=-1, keepdims=True)
            probs_ref[p, h, rows, window] = prob
            probs.append(prob)
        keys = slice(first * BLOCK, (n + 1) * BLOCK)
        for h in range(GROUP):
            lanes = slice(h * LANES, (h + 1) * LANES)
            mixed = (mix_ref[h, 0] * probs[0] + mix_ref[h, 1] * probs[1]).astype(jnp.bfloat16)
            attended = dot_plain(mixed, v_ref[p, keys, lanes])
            att_ref[p, rows, lanes] = attended
            normal, _ = head_stats(attended)
            grouped_ref[p, rows, lanes] = (normal * gain[:, lanes]).astype(jnp.bfloat16)


def forward_kernel(
    blocks, reach, slab, at_ref, mix_ref, w_ref, t0, t1, t2, t3, t4, t5, t6, t7,
    start_ref, th_ref, tl_ref, spread_ref, rest_ref,
    normed_ref, wide_ref, q_ref, k_ref, v_ref, probs_ref, high_ref, att_ref, near_ref,
    far_ref, gains_ref, gain_ref,
    grp_ref, shift_ref, low_ref, part_ref,
):
    plane = at_ref[0]
    half = slab // 2
    block = 4 * slab + half + 8
    gains_ref[...] = jnp.zeros_like(gains_ref)
    span = gains_ref.shape[1] // 4
    for zz in range(w_ref.shape[0]):
        ref = w_ref.at[zz]
        main = jnp.concatenate(
            [
                jnp.concatenate(
                    [ref[g * block + t * slab : g * block + (t + 1) * slab, :] for t in range(4)],
                    axis=1,
                )
                for g in range(8)
            ],
            axis=0,
        )
        rest = jnp.concatenate(
            [ref[g * block + 4 * slab : g * block + 4 * slab + half, :] for g in range(8)], axis=0
        )
        table = dot_plain(main, spread_ref[...])
        early = dot_plain(rest, rest_ref[0])
        late = dot_plain(rest, rest_ref[1])
        for g in range(8):
            row = (g // 2 * 8 + g % 2 + 2 * zz) * slab
            tail = jnp.concatenate(
                [early[g * half : (g + 1) * half], late[g * half : (g + 1) * half]], axis=0
            )
            wide_ref[row : row + slab, :] = (table[g * slab : (g + 1) * slab] + tail).astype(
                jnp.bfloat16
            )
        lane = iota((LANES, span), 0)
        for y in range(2):
            place = (iota((LANES, span), 1) == lane + (zz * 2 + y) * slab) & (lane < slab)
            place = jnp.where(place, 1.0, 0.0).astype(jnp.bfloat16)
            for s in range(4):
                gains_ref[:, s * span : (s + 1) * span] += dot_plain(
                    ref[(2 * s + y + 1) * block - 8 : (2 * s + y + 1) * block, :], place
                )
    cols = GROUP * HEAD_DIM
    width = gains_ref.shape[1]
    lane = iota((width, GROUP * LANES), 1)
    from_row = iota((width, GROUP * LANES), 0) - plane * cols
    select = (from_row == lane // LANES * HEAD_DIM + lane % LANES) & (lane % LANES < HEAD_DIM)
    gain_ref[...] = dot_plain(
        gains_ref[...].astype(jnp.bfloat16), jnp.where(select, 1.0, 0.0).astype(jnp.bfloat16)
    )[1:2]
    gain = gain_ref[...]
    for slot, ref in enumerate((t0, t1, t2, t3, t4, t5, t6, t7)):
        value = ref[...].astype(jnp.float32)
        scale = lax.rsqrt(jnp.mean(value * value, axis=-1, keepdims=True) + epsilon)
        normed_ref[slot * BLOCK : (slot + 1) * BLOCK, :] = (
            value * scale * gains_ref[0:1, :]
        ).astype(jnp.bfloat16)
    lanes = GROUP * LANES
    shift_ref[...] = jnp.zeros_like(shift_ref)
    for slots in (range(4), range(4, 8)):
        rows = slice(slots[0] * BLOCK, (slots[-1] + 1) * BLOCK)
        qkv = dot_plain(normed_ref[rows, :], wide_ref[...])
        for i, slot in enumerate(slots):
            pack, row = slot_place(plane, slot)
            part = qkv[i * BLOCK : (i + 1) * BLOCK]
            q_ref[pack, pl.ds(row, BLOCK), :] = part[:, :lanes].astype(jnp.bfloat16)
            shift_ref[pack, pl.ds(row, BLOCK), :] = part[:, lanes : 2 * lanes]
            v_ref[pack, pl.ds(row, BLOCK), :] = part[:, 2 * lanes :].astype(jnp.bfloat16)
    key_rim = CK // 2
    length = q_ref.shape[1]
    for p in range(2):
        moved = jnp.concatenate(
            [
                jnp.zeros((8, lanes), jnp.float32),
                shift_ref[p],
                jnp.zeros((LANES - 8, lanes), jnp.float32),
            ],
            axis=0,
        )
        moved = pltpu.roll(moved, length + LANES - (8 - key_rim), 0)
        k_ref[p] = moved.astype(jnp.bfloat16)
        attend_pack(
            p, blocks, reach, mix_ref, q_ref, k_ref, v_ref, start_ref, th_ref, tl_ref, gain,
            probs_ref, high_ref, att_ref, grp_ref, low_ref, part_ref,
        )
    for slot in range(8):
        pack, row = slot_place(plane, slot)
        into = near_ref if slot < 4 else far_ref
        into[slot % 4 * BLOCK : (slot % 4 + 1) * BLOCK, :] = grp_ref[pack, pl.ds(row, BLOCK), :]


def pair_product(transposed, own_ref, got_ref, w_ref, other_ref):
    dot = dot_nt if transposed else dot_plain
    return dot(own_ref[...], w_ref[...]) + dot(got_ref[...], other_ref[...])


def store_blocks(value, refs):
    for i, ref in enumerate(refs):
        ref[...] = value[i * BLOCK : (i + 1) * BLOCK].astype(ref.dtype)


def pair_kernel(transposed, own_ref, got_ref, w_ref, other_ref, total_ref, r1, r2, r3):
    value = pair_product(transposed, own_ref, got_ref, w_ref, other_ref)
    store_blocks(value, (total_ref, r1, r2, r3))


def pair_gain_kernel(
    own_ref, got_ref, w_ref, other_ref, t0, t1, t2, t3, total_ref, r1, r2, r3, gain_ref
):
    value = pair_product(True, own_ref, got_ref, w_ref, other_ref)
    store_blocks(value, (total_ref, r1, r2, r3))
    total = jnp.zeros(gain_ref.shape, jnp.float32)
    for i, ref in enumerate((t0, t1, t2, t3)):
        token = ref[...].astype(jnp.float32)
        scale = lax.rsqrt(jnp.mean(token * token, axis=-1, keepdims=True) + epsilon)
        total = total + fold_rows(value[i * BLOCK : (i + 1) * BLOCK] * (token * scale))
    gain_ref[...] = total


def small_kernel(at_ref, attn_ref, ffn_ref, taps_ref, mix_ref, group_ref, out_ref):
    plane = at_ref[0]
    out_ref[...] = jnp.zeros_like(out_ref)
    tiles = attn_ref.shape[1] // LANES
    for i, ref in enumerate((attn_ref, ffn_ref)):
        row = jnp.sum(ref[...], axis=0, keepdims=True)
        for t in range(tiles):
            out_ref[i * tiles + t : i * tiles + t + 1, :] = row[:, t * LANES : (t + 1) * LANES]
    group = jnp.sum(group_ref[...], axis=0, keepdims=True)
    lane = iota((16, LANES), 1)
    place = iota((16, LANES), 0)
    first = iota((1, LANES), 1)
    for h in range(GROUP):
        head = GROUP * plane + h
        out_ref[pl.ds(2 * tiles + head, 1), :] = group[:, h * LANES : (h + 1) * LANES]
        total = jnp.zeros((16, LANES), jnp.float32)
        for a in range(CQ):
            sums = jnp.sum(taps_ref[h, :, a * LANES : (a + 1) * LANES], axis=-1, keepdims=True)
            total = total + jnp.where(lane == 16 * a + place, sums, 0.0)
        row = jnp.sum(total, axis=0, keepdims=True)
        for d in range(GROUP):
            value = jnp.sum(mix_ref[h * GROUP + d], axis=0, keepdims=True)
            value = jnp.sum(value, axis=1, keepdims=True)
            row = row + jnp.where(first == 16 * CQ + d, value, 0.0)
        out_ref[pl.ds(2 * tiles + HEADS + head, 1), :] = row


def backward_pack(p, blocks, reach, mix_ref, gg_ref, att_ref, gain_ref, q_ref, k_ref, v_ref,
                  start_ref, stop_ref, probs_ref, high_ref, th_ref, tl_ref,
                  dqkv_ref, mixg_ref, gaing_ref, grad_ref, cross_ref, keyg_ref, valueg_ref, ready):
    key_rim = CK // 2
    scaling = HEAD_DIM ** (-0.5)
    all_lanes = GROUP * LANES
    grad_ref[...] = jnp.zeros_like(grad_ref)
    keyg_ref[...] = jnp.zeros_like(keyg_ref)
    valueg_ref[...] = jnp.zeros_like(valueg_ref)
    lane = iota((BLOCK, LANES), 1)
    for n in range(blocks):
        first = max(0, n - reach)
        count = n - first + 1
        rows = slice(n * BLOCK, (n + 1) * BLOCK)
        keys = slice(first * BLOCK, (n + 1) * BLOCK)
        window = slice((reach + 1 - count) * LANES, (reach + 1) * LANES)
        probs = [probs_ref[p, h, rows, window] for h in range(GROUP)]
        mixed_grads = []
        for h in range(GROUP):
            lanes = slice(h * LANES, (h + 1) * LANES)
            normal, inverse = head_stats(att_ref[p, rows, lanes])
            grad_grouped = gg_ref[p, rows, lanes]
            gaing_ref[:, lanes] += fold_rows(grad_grouped * normal)
            scaled = jnp.where(lane < HEAD_DIM, grad_grouped * gain_ref[:, lanes], 0.0)
            mean_one = jnp.sum(scaled, axis=-1, keepdims=True) * (1.0 / HEAD_DIM)
            mean_two = jnp.sum(scaled * normal, axis=-1, keepdims=True) * (1.0 / HEAD_DIM)
            grad_att = inverse * (scaled - mean_one - normal * mean_two)
            grad_att = jnp.where(lane < HEAD_DIM, grad_att, 0.0).astype(jnp.bfloat16)
            mixed_grads.append(dot_nt(grad_att, v_ref[p, keys, lanes]))
            mixed = (mix_ref[h, 0] * probs[0] + mix_ref[h, 1] * probs[1]).astype(jnp.bfloat16)
            valueg_ref[keys, lanes] += dot_tn(mixed, grad_att)
        for h in range(GROUP):
            for d in range(GROUP):
                product = fold_rows(probs[d] * mixed_grads[h])
                total = product[:, :LANES]
                for m in range(1, count):
                    total = total + product[:, m * LANES : (m + 1) * LANES]
                mixg_ref[h * GROUP + d] += total
        for d in range(GROUP):
            grad_probs = mix_ref[0, d] * mixed_grads[0] + mix_ref[1, d] * mixed_grads[1]
            delta = jnp.sum(probs[d] * grad_probs, axis=-1, keepdims=True)
            grad_logits = probs[d] * (grad_probs - delta)
            for m in range(count):
                grad_ref[d, first + m, rows, :] = grad_logits[:, m * LANES : (m + 1) * LANES]
    ready()
    for h in range(GROUP):
        lanes = slice(h * LANES, (h + 1) * LANES)
        for n in range(blocks):
            first, last = max(0, n - reach), min(n + 1, blocks - 1)
            rows = slice(n * BLOCK, (n + 1) * BLOCK)
            room = stop_ref[p, rows, :] - (iota((BLOCK, LANES), 0) + n * BLOCK)
            count = n + 2 - first
            sums = [None] * (count + 1)
            for m in range(first, last + 1):
                highs, lows = [], []
                for a in range(CQ):
                    piece = grad_ref[h, m, n * BLOCK + a : (n + 1) * BLOCK + a, :]
                    if a:
                        piece = jnp.where(room > a, piece, 0.0)
                    high, low = halves(piece)
                    highs.append(high)
                    lows.append(low)
                high = jnp.concatenate(highs, axis=1)
                low = jnp.concatenate(lows, axis=1)
                part = (
                    dot_nt(high, th_ref[h]) + dot_nt(low, th_ref[h]) + dot_nt(high, tl_ref[h])
                )
                for side in range(2):
                    place = m - first + side
                    value = part[:, side * LANES : (side + 1) * LANES]
                    sums[place] = value if sums[place] is None else sums[place] + value
                scores = high_ref[
                    p, h, RIM + n * BLOCK : RIM + (n + 1) * BLOCK, m * LANES : (m + 2) * LANES
                ]
                if m <= n:
                    cross_ref[h] += dot_tn(scores, high)
                else:
                    cross_ref[h, :LANES, :] += dot_tn(scores[:, :LANES], high)
            total = jnp.concatenate(sums[:count], axis=1)
            keep = allowed_mask(start_ref[p, rows, :], n, first * BLOCK - key_rim, count)
            grad_scores = jnp.where(keep, total, 0.0).astype(jnp.bfloat16)
            cols = slice(first * BLOCK, (first + count) * BLOCK)
            dqkv_ref[p, rows, lanes] = (
                dot_plain(grad_scores, k_ref[p, cols, lanes]) * scaling
            ).astype(jnp.bfloat16)
            keyg_ref[h, cols, :] += dot_tn(grad_scores, q_ref[p, rows, lanes])
        key_lanes = slice(all_lanes + h * LANES, all_lanes + (h + 1) * LANES)
        dqkv_ref[p, :, key_lanes] = (
            keyg_ref[h, key_rim : key_rim + blocks * BLOCK, :] * scaling
        ).astype(jnp.bfloat16)
    dqkv_ref[p, :, 2 * all_lanes :] = valueg_ref[...].astype(jnp.bfloat16)


def backward_kernel(
    blocks, reach, at_ref, mix_ref, b0, b1, b2, b3, b4, b5, b6, b7, out_w_ref, gain_ref,
    att_from, v_from, probs_from, start_from, stop_from, th_from, tl_from, high_from, k_from, q_from,
    near_ref, far_ref, taps_ref, mixg_ref, gaing_ref,
    att_ref, v_ref, probs_ref, start_ref, stop_ref, th_ref, tl_ref, high_ref, k_ref, q_ref, sems,
    gg_ref, abs_ref, grad_ref, cross_ref, keyg_ref, valueg_ref,
):
    plane = at_ref[0]
    sources = (
        att_from, v_from, probs_from, start_from, stop_from, th_from, tl_from, high_from, k_from, q_from
    )
    targets = (
        att_ref, v_ref, probs_ref, start_ref, stop_ref, th_ref, tl_ref, high_ref, k_ref, q_ref
    )
    copies = [
        pltpu.make_async_copy(source, target, sems.at[i])
        for i, (source, target) in enumerate(zip(sources, targets))
    ]
    for copy in copies:
        copy.start()
    pieces = (b0, b1, b2, b3, b4, b5, b6, b7)
    for slots in (range(4), range(4, 8)):
        branch = jnp.concatenate([pieces[slot][...] for slot in slots], axis=0)
        part = dot_nt(branch, out_w_ref[...])
        for i, slot in enumerate(slots):
            pack, row = slot_place(plane, slot)
            gg_ref[pack, pl.ds(row, BLOCK), :] = part[i * BLOCK : (i + 1) * BLOCK]
    cross_ref[...] = jnp.zeros_like(cross_ref)
    mixg_ref[...] = jnp.zeros_like(mixg_ref)
    gaing_ref[...] = jnp.zeros_like(gaing_ref)
    for copy in copies[:3]:
        copy.wait()

    def ready():
        for copy in copies[3:]:
            copy.wait()

    for p in range(2):
        backward_pack(
            p, blocks, reach, mix_ref, gg_ref, att_ref, gain_ref, q_ref, k_ref, v_ref,
            start_ref, stop_ref, probs_ref, high_ref, th_ref, tl_ref,
            abs_ref, mixg_ref, gaing_ref, grad_ref, cross_ref, keyg_ref, valueg_ref,
            ready if p == 0 else lambda: None,
        )
    for slot in range(8):
        pack, row = slot_place(plane, slot)
        into = near_ref if slot < 4 else far_ref
        into[slot % 4 * BLOCK : (slot % 4 + 1) * BLOCK, :] = abs_ref[pack, pl.ds(row, BLOCK), :]
    height = LANES + 2 * 8
    shift = iota((height, CQ * LANES), 1) % LANES - iota((height, CQ * LANES), 0) + (CK - 1)
    for h in range(GROUP):
        cross = cross_ref[h, :height, :]
        taps_ref[h] = jnp.zeros(taps_ref.shape[1:], jnp.float32)
        for b in range(CK):
            taps_ref[h, b : b + 1, :] = jnp.sum(
                jnp.where(shift == b, cross, 0.0), axis=0, keepdims=True
            )


def out_rows_kernel(slab, w_ref, out_ref):
    width = out_ref.shape[1]
    base = w_ref.shape[1] - width // LANES * slab
    fill = jnp.zeros((LANES - HEAD_DIM, width), jnp.bfloat16)
    for k in range(w_ref.shape[0]):
        row = k // 2 * LANES + k % 2 * slab
        for t in range(width // LANES):
            out_ref[row : row + slab, t * LANES : (t + 1) * LANES] = w_ref[
                k, base + t * slab : base + (t + 1) * slab, :
            ]
    for h in range(GROUP):
        out_ref[h * LANES + HEAD_DIM : (h + 1) * LANES, :] = fill


def weight_grads_kernel(
    slab, normed_ref, near_ref, far_ref, spread_ref, rest_ref, group_near, group_far,
    b0, b1, b2, b3, b4, b5, b6, b7, all_ref,
):
    pieces = (b0, b1, b2, b3, b4, b5, b6, b7)
    near = jnp.concatenate([ref[...] for ref in pieces[:4]], axis=0)
    grad = dot_tn(group_near[...], near)
    far = jnp.concatenate([ref[...] for ref in pieces[4:]], axis=0)
    grad = (grad + dot_tn(group_far[...], far)).astype(jnp.bfloat16)
    base = all_ref.shape[1] - grad.shape[1] // LANES * slab
    for k in range(all_ref.shape[0]):
        row = k // 2 * LANES + k % 2 * slab
        for t in range(grad.shape[1] // LANES):
            all_ref[k, base + t * slab : base + (t + 1) * slab, :] = grad[
                row : row + slab, t * LANES : (t + 1) * LANES
            ]
    block = base // 8
    half = slab // 2
    span = normed_ref.shape[1] // 4
    for s in range(4):
        rows = near_ref.shape[0]
        cols = slice(s * span, (s + 1) * span)
        table = (
            dot_tn(normed_ref[:rows, cols], near_ref[...])
            + dot_tn(normed_ref[rows:, cols], far_ref[...])
        ).astype(jnp.bfloat16)
        main = dot_nt(table, spread_ref[...])
        early = dot_nt(table, rest_ref[0])
        late = dot_nt(table, rest_ref[1])
        for zz in range(4):
            for y in range(2):
                g = 2 * s + y
                row = (zz * 2 + y) * slab
                for t in range(4):
                    at = g * block + t * slab
                    all_ref[zz, at : at + slab, :] = main[
                        row : row + slab, t * LANES : (t + 1) * LANES
                    ].astype(jnp.bfloat16)
                rest = early[row : row + half] + late[row + half : row + slab]
                all_ref[zz, g * block + 4 * slab : (g + 1) * block, :] = jnp.concatenate(
                    [rest, jnp.zeros((8, LANES), jnp.float32)], axis=0
                ).astype(jnp.bfloat16)


def assemble_kernel(sub, w_ref, gu_ref, down_ref):
    deep = w_ref.shape[3]
    units = w_ref.shape[0] * sub
    parts = deep // LANES
    for zz in range(w_ref.shape[0]):
        for s in range(w_ref.shape[1]):
            for m in range(2):
                at = m * units + zz * sub
                gu_ref[s * deep : (s + 1) * deep, at : at + sub] = w_ref[zz, s, m]
            for c in range(parts):
                at = (s * parts + c) * LANES
                down_ref[zz * sub : (zz + 1) * sub, at : at + LANES] = w_ref[
                    zz, s, 2, c * sub : (c + 1) * sub, :
                ]


def hidden_kernel(
    x0, x1, x2, x3, x4, x5, x6, x7, c0, c1, c2, c3, c4, c5, c6, c7, gu_ref, down_ref,
    hidden_near, hidden_far, grad_near, grad_far,
):
    units = down_ref.shape[0]
    xs = (x0, x1, x2, x3, x4, x5, x6, x7)
    cs = (c0, c1, c2, c3, c4, c5, c6, c7)
    for part in (2, 3, 0, 1):
        pair = (2 * part, 2 * part + 1)
        value = jnp.concatenate([xs[i][...] for i in pair], axis=0)
        gate_up = dot_plain(value, gu_ref[...])
        gate, up = gate_up[:, :units], gate_up[:, units:]
        cot = jnp.concatenate([cs[i][...] for i in pair], axis=0)
        grad_hidden = dot_nt(cot, down_ref[...])
        sig = 1.0 / (1.0 + jnp.exp(-gate))
        silu = gate * sig
        hidden_ref, grad_ref = (hidden_near, grad_near) if part < 2 else (hidden_far, grad_far)
        rows = slice(part % 2 * 2 * BLOCK, (part % 2 + 1) * 2 * BLOCK)
        hidden_ref[rows, :] = (silu * up).astype(jnp.bfloat16)
        grad_ref[rows, :units] = (
            grad_hidden * up * sig * (1.0 + gate * (1.0 - sig))
        ).astype(jnp.bfloat16)
        grad_ref[rows, units:] = (grad_hidden * silu).astype(jnp.bfloat16)


def hidden_grad_kernel(
    sub, x0, x1, x2, x3, x4, x5, x6, x7, c0, c1, c2, c3, c4, c5, c6, c7,
    hidden_near, hidden_far, grad_near, grad_far, out_ref, x_ref, c_ref,
):
    deep = out_ref.shape[3]
    depth = out_ref.shape[0]
    units = depth * sub
    xs = (x0, x1, x2, x3, x4, x5, x6, x7)
    cs = (c0, c1, c2, c3, c4, c5, c6, c7)
    for slot in range(8):
        rows = slice(slot * BLOCK, (slot + 1) * BLOCK)
        x_ref[rows, :] = xs[slot][...]
        c_ref[rows, :] = cs[slot][...]
    half = 4 * BLOCK
    for s in range(out_ref.shape[1]):
        cols = slice(s * deep, (s + 1) * deep)
        table = (
            dot_tn(x_ref[:half, cols], grad_near[...]) + dot_tn(x_ref[half:, cols], grad_far[...])
        ).astype(jnp.bfloat16)
        for zz in range(depth):
            for m in range(2):
                at = m * units + zz * sub
                out_ref[zz, s, m] = table[:, at : at + sub]
        down = (
            dot_tn(hidden_near[...], c_ref[:half, cols])
            + dot_tn(hidden_far[...], c_ref[half:, cols])
        ).astype(jnp.bfloat16)
        for zz in range(depth):
            for c in range(deep // LANES):
                out_ref[zz, s, 2, c * sub : (c + 1) * sub, :] = down[
                    zz * sub : (zz + 1) * sub, c * LANES : (c + 1) * LANES
                ]


def pack_hidden_kernel(sub, gate_ref, up_ref, down_ref, out_ref):
    deep = gate_ref.shape[0]
    for s in range(out_ref.shape[0]):
        for m, ref in enumerate((gate_ref, up_ref)):
            out_ref[s, m] = ref[:, s * sub : (s + 1) * sub].astype(jnp.bfloat16)
        for c in range(deep // LANES):
            out_ref[s, 2, c * sub : (c + 1) * sub, :] = down_ref[
                s * sub : (s + 1) * sub, c * LANES : (c + 1) * LANES
            ].astype(jnp.bfloat16)


def unpack_hidden_kernel(sub, in_ref, gate_ref, up_ref, down_ref):
    deep = gate_ref.shape[0]
    for s in range(in_ref.shape[0]):
        for m, ref in enumerate((gate_ref, up_ref)):
            ref[:, s * sub : (s + 1) * sub] = in_ref[s, m].astype(jnp.float32)
        for c in range(deep // LANES):
            down_ref[s * sub : (s + 1) * sub, c * LANES : (c + 1) * LANES] = in_ref[
                s, 2, c * sub : (c + 1) * sub, :
            ].astype(jnp.float32)


def total_of(refs):
    total = refs[0][...]
    for ref in refs[1:]:
        total = total + ref[...].astype(jnp.float32)
    return total


def middle_kernel(s0, s1, s2, s3, token_ref, gains_ref, middle_ref, in_ref):
    middle = token_ref[...].astype(jnp.float32) + total_of((s0, s1, s2, s3))
    middle_ref[...] = middle
    scale = lax.rsqrt(jnp.mean(middle * middle, axis=-1, keepdims=True) + epsilon)
    in_ref[...] = (middle * scale * gains_ref[2:3, :]).astype(jnp.bfloat16)


def norm_back(row, grad, value, gains_ref, first):
    scale = lax.rsqrt(jnp.mean(value * value, axis=-1, keepdims=True) + epsilon)
    scaled = grad * gains_ref[row : row + 1, :]
    mean = jnp.mean(scaled * value, axis=-1, keepdims=True)
    return first + (scale * scaled - value * (scale * scale * scale) * mean)


def middle_back_kernel(
    s0, s1, s2, s3, middle_ref, cot_ref, gains_ref, grad_ref, branch_ref, gain_ref
):
    value = middle_ref[...]
    total = total_of((s0, s1, s2, s3))
    grad = norm_back(2, total, value, gains_ref, cot_ref[...].astype(jnp.float32))
    grad_ref[...] = grad
    branch_ref[...] = grad.astype(jnp.bfloat16)
    scale = lax.rsqrt(jnp.mean(value * value, axis=-1, keepdims=True) + epsilon)
    gain_ref[...] = fold_rows(total * value * scale)


def input_back_kernel(s0, s1, s2, s3, token_ref, middle_ref, gains_ref, grad_ref):
    token = token_ref[...].astype(jnp.float32)
    grad_ref[...] = norm_back(
        0, total_of((s0, s1, s2, s3)), token, gains_ref, middle_ref[...]
    ).astype(jnp.bfloat16)


def output_kernel(s0, s1, s2, s3, middle_ref, out_ref):
    out_ref[...] = (middle_ref[...] + total_of((s0, s1, s2, s3))).astype(jnp.bfloat16)


def conv_tables(kernel):
    heads = kernel.shape[0]
    u = iota((2 * LANES, CQ * LANES), 0)
    j = iota((2 * LANES, CQ * LANES), 1) % LANES
    table = jnp.zeros((heads, 2 * LANES, CQ * LANES), jnp.float32)
    for b in range(CK):
        taps = jnp.repeat(kernel[:, :, b], LANES, axis=1)
        table = jnp.where((j - u + CK - 1 == b)[None], taps[:, None, :], table)
    return halves(table)


FLAT = ("seq", "wide")


def swapped(value, flip):
    total = lax.axis_size("seq") * lax.axis_size("wide")
    return lax.ppermute(value, FLAT, [(i, i ^ flip) for i in range(total)])


class Place:
    def __init__(self):
        self.wide_count = lax.axis_size("wide")
        self.depth = self.wide_count // 2
        self.seq = lax.axis_index("seq")
        wide = lax.axis_index("wide")
        self.y = wide % 2
        self.z = wide // 2
        self.plane = 2 * self.seq + self.y
        self.x_flip = 2 * self.wide_count
        self.core_flip = self.wide_count
        self.y_flip = 1
        self.chip_flips = (self.x_flip, self.y_flip, self.x_flip | self.y_flip)
        seqs = range(lax.axis_size("seq"))
        self.plane_groups = [
            [s * self.wide_count + z * 2 + y for s in seqs for y in range(2)] for z in range(self.depth)
        ]
        self.line_groups = [[z * 2 + y for z in range(self.depth)] for y in range(2)]


def chip_gather(place, value):
    return [value] + [swapped(value, flip) for flip in place.chip_flips]


def core_gather(place, near):
    return near + [swapped(part, place.core_flip) for part in near]


def plane_gather(place, value):
    return core_gather(place, chip_gather(place, value))


def plane_terms(place, near, far, weight, other, transposed, name, tokens=None):
    width = weight.shape[0] if transposed else weight.shape[1]
    flat = (BLOCK, width)
    got = swapped(far, place.core_flip)
    return list(
        kernel_call(
            functools.partial(pair_kernel, transposed) if tokens is None else pair_gain_kernel,
            name,
            [shape_of(flat, jnp.float32)]
            + [shape_of(flat)] * 3
            + ([] if tokens is None else [shape_of((8, width), jnp.float32)]),
            (near, got, weight, other) + (tokens or ()),
            flops=16 * BLOCK * weight.size,
            vmem=32,
        )
    )


def chip_scatter(place, terms):
    return [terms[0]] + [
        swapped(part, flip) for part, flip in zip(terms[1:], place.chip_flips)
    ]


def line_gather(place, value):
    return lax.all_gather(value, "wide", axis=0, axis_index_groups=place.line_groups)


def line_scatter(place, blocks):
    return lax.psum_scatter(
        blocks, "wide", scatter_dimension=0, axis_index_groups=place.line_groups
    )


def plane_exchange(place, blocks):
    return lax.all_to_all(blocks, FLAT, 0, 0, axis_index_groups=place.plane_groups)


def out_pairs(place):
    return [
        (s * place.wide_count + 4 * y + z, s * place.wide_count + 2 * z + y)
        for s in range(lax.axis_size("seq"))
        for z in range(place.depth)
        for y in range(2)
    ]


def spread_tables():
    target = iota((4 * LANES, 3 * GROUP * LANES), 1)
    column = target // LANES * HEAD_DIM + target % LANES
    real = target % LANES < HEAD_DIM
    source = iota(target.shape, 0)
    main = jnp.where(real & (column == source), 1.0, 0.0).astype(jnp.bfloat16)
    source, column, real = source[:LANES], column[:LANES], real[:LANES]
    rest = [
        jnp.where(
            real & (column >= 4 * LANES) & (column - 4 * LANES + side * (LANES // 2) == source), 1.0, 0.0
        ).astype(jnp.bfloat16)
        for side in range(2)
    ]
    return main, jnp.stack(rest)


def after(done, *values):
    return lax.optimization_barrier((done,) + values)[1:]


def plane_shards(
    tokens, segments, w_query, w_key, w_value, w_out, gain_attn, gain_group, gain_ffn,
    conv_kernel, head_mix, w_gate, w_up, w_down, cotangent,
):
    place = Place()
    seq_count = lax.axis_size("seq")
    depth = place.depth
    count = tokens.shape[1]
    length = count * seq_count
    width = tokens.shape[2]
    slab = w_query.shape[0]
    blocks = length // BLOCK
    reach = (length // 2 - 1) // BLOCK + 1
    lanes = GROUP * LANES
    cols = GROUP * HEAD_DIM
    bf16 = jnp.bfloat16
    f32 = jnp.float32
    at = jnp.stack([place.plane, place.z, place.y]).astype(jnp.int32)
    own_tokens = tokens[0]
    own_cot = cotangent[0]

    gains_own = jnp.stack([gain_attn, gain_group, gain_ffn]).astype(bf16)
    gains_own = jnp.pad(gains_own, ((0, 5), (0, LANES - slab)))
    pack_rows = 4 * slab + slab // 2 + 8
    out_rows = width // LANES * slab
    packed, w_out_rows = kernel_call(
        functools.partial(pack_kernel, slab),
        "pack_projections",
        [shape_of((8, pack_rows, LANES)), shape_of((out_rows, LANES))],
        (w_query, w_key, w_value, gains_own, w_out),
        vmem=16,
    )
    sub = w_gate.shape[1] // seq_count
    deep = w_gate.shape[0]
    (ffn_own,) = kernel_call(
        functools.partial(pack_hidden_kernel, sub),
        "pack_hidden",
        [shape_of((seq_count, 3, deep, sub))],
        (w_gate, w_up, w_down),
        vmem=16,
    )
    packed, ffn_own, own_tokens, w_out_rows, segments, conv_kernel = lax.optimization_barrier(
        (packed, ffn_own, own_tokens, w_out_rows, segments, conv_kernel)
    )
    w_out_rows = lax.ppermute(w_out_rows, FLAT, out_pairs(place))
    packed = plane_exchange(place, packed)
    token_near = chip_gather(place, own_tokens)
    packed, ffn_own, own_cot = lax.optimization_barrier((packed, ffn_own, own_cot))
    w_all = line_gather(
        place, jnp.concatenate([packed.reshape(8 * pack_rows, LANES), w_out_rows])
    )
    ffn_own = lax.all_to_all(ffn_own, "seq", 0, 0)
    cot_near = chip_gather(place, own_cot)
    token_parts = core_gather(place, token_near)

    other_row = swapped(segments, place.y_flip)
    seg = jnp.where(
        place.y == 0,
        jnp.concatenate([segments, other_row]),
        jnp.concatenate([other_row, segments]),
    )
    starts = jnp.sum(seg[:, None, :] < seg[:, :, None], axis=-1, dtype=jnp.int32)
    stops = jnp.sum(seg[:, None, :] <= seg[:, :, None], axis=-1, dtype=jnp.int32)
    starts = jnp.broadcast_to(starts[:, :, None], (2, length, LANES))
    stops = jnp.broadcast_to(stops[:, :, None], (2, length, LANES))
    taps = lax.dynamic_slice_in_dim(conv_kernel, place.plane * GROUP, GROUP)
    mix = lax.dynamic_slice_in_dim(head_mix, place.plane * GROUP, GROUP)
    table_high, table_low = conv_tables(taps)
    spread_main, spread_rest = spread_tables()

    ffn_w = line_gather(place, ffn_own)
    units = depth * sub
    w_gate_up, w_down_all = kernel_call(
        functools.partial(assemble_kernel, sub),
        "assemble_feed_forward",
        [shape_of((width, 2 * units)), shape_of((units, width))],
        (ffn_w,),
        vmem=24,
    )
    gate_up_other = swapped(w_gate_up, place.core_flip)
    down_other = swapped(w_down_all, place.core_flip)
    w_all, starts, stops, *cot_near = lax.optimization_barrier(
        (w_all, starts, stops, *cot_near)
    )
    (w_out_heads,) = kernel_call(
        functools.partial(out_rows_kernel, slab),
        "out_rows",
        [shape_of((lanes, width))],
        (w_all,),
        vmem=16,
    )
    w_out_other = swapped(w_out_heads, place.core_flip)
    cot_parts = core_gather(place, cot_near)

    padded = length + LANES
    half = 4 * count
    (
        normed, w_wide, queries, keys, values, probs, high, attended, grouped_near, grouped_far,
        gains, gain_heads,
    ) = kernel_call(
        functools.partial(forward_kernel, blocks, reach, slab),
        "attention_forward",
        [
            shape_of((8 * count, width)),
            shape_of((width, 3 * lanes)),
            shape_of((2, length, lanes)),
            shape_of((2, padded, lanes)),
            shape_of((2, length, lanes)),
            shape_of((2, GROUP, length, (reach + 1) * LANES), f32),
            shape_of((2, GROUP, RIM + length, padded)),
            shape_of((2, length, lanes), f32),
            shape_of((half, lanes)),
            shape_of((half, lanes)),
            shape_of((8, width), f32),
            shape_of((1, lanes), f32),
        ],
        (
            at, mix, w_all, *token_parts, starts, table_high, table_low, spread_main, spread_rest,
        ),
        [
            pltpu.VMEM((2, length, lanes), bf16),
            pltpu.VMEM((2, length, lanes), f32),
            pltpu.VMEM((GROUP, RIM + length, padded), bf16),
            pltpu.VMEM((CQ, RIM + BLOCK, LANES), f32),
        ],
        flops=25 * 10**9,
        smem=2,
    )
    w_wide_other = swapped(w_wide, place.core_flip)
    terms = chip_scatter(
        place,
        plane_terms(place, grouped_near, grouped_far, w_out_heads, w_out_other, False, "branch"),
    )
    flat = (count, width)
    middle, ffn_in = kernel_call(
        middle_kernel,
        "middle",
        [shape_of(flat, f32), shape_of(flat)],
        (*terms, own_tokens, gains),
        vmem=16,
    )

    ffn_parts = plane_gather(place, ffn_in)
    hidden_near, hidden_far, grad_near, grad_far = kernel_call(
        hidden_kernel,
        "feed_forward",
        [
            shape_of((half, units)),
            shape_of((half, units)),
            shape_of((half, 2 * units)),
            shape_of((half, 2 * units)),
        ],
        (*ffn_parts, *cot_parts, w_gate_up, w_down_all),
        flops=10 * 10**9,
        vmem=32,
    )
    terms = plane_terms(
        place, grad_near, grad_far, w_gate_up, gate_up_other, True, "feed_forward_back"
    )
    held = lax.optimization_barrier((terms[0], hidden_near, hidden_far, grad_near, grad_far))
    terms[0], *held = held
    terms = chip_scatter(place, terms)
    (ffn_g,) = kernel_call(
        functools.partial(hidden_grad_kernel, sub),
        "feed_forward_weights",
        [shape_of((depth, seq_count, 3, deep, sub))],
        (*ffn_parts, *cot_parts, *held),
        [pltpu.VMEM((8 * count, width), bf16), pltpu.VMEM((8 * count, width), bf16)],
        flops=5 * 10**9,
        vmem=40,
    )
    grad_middle, grad_branch, gain_ffn_sum = kernel_call(
        middle_back_kernel,
        "middle_back",
        [shape_of(flat, f32), shape_of(flat), shape_of((8, width), f32)],
        (*terms, middle, own_cot, gains),
        vmem=16,
    )
    terms[1], ffn_g = lax.optimization_barrier((terms[1], ffn_g))
    ffn_g = line_scatter(place, ffn_g)
    ffn_g = lax.all_to_all(ffn_g, "seq", 0, 0)

    hidden_near, hidden_far = after(terms[1], hidden_near, hidden_far)
    out_terms = plane_terms(
        place, hidden_near, hidden_far, w_down_all, down_other, False, "feed_forward_out"
    )
    out_terms[0], grad_branch = lax.optimization_barrier((out_terms[0], grad_branch))
    branch_parts = plane_gather(place, grad_branch)
    branch_parts[3], *out_terms = lax.optimization_barrier((branch_parts[3], *out_terms))
    out_terms = chip_scatter(place, out_terms)
    dqkv_near, dqkv_far, grad_taps, grad_mix, grad_gain_group = kernel_call(
        functools.partial(backward_kernel, blocks, reach),
        "attention_backward",
        [
            shape_of((half, 3 * lanes)),
            shape_of((half, 3 * lanes)),
            shape_of((GROUP, 16, CQ * LANES), f32),
            shape_of((GROUP * GROUP, 8, LANES), f32),
            shape_of((8, lanes), f32),
        ],
        (
            at, mix, *branch_parts, w_out_heads, gain_heads,
            attended, values, probs, starts, stops, table_high, table_low, high, keys, queries,
        ),
        [
            pltpu.VMEM((2, length, lanes), f32),
            pltpu.VMEM((2, length, 3 * lanes), bf16),
            pltpu.VMEM((GROUP, blocks, length + 8, LANES), f32),
            pltpu.VMEM((GROUP, 2 * LANES, CQ * LANES), f32),
            pltpu.VMEM((GROUP, padded, LANES), f32),
            pltpu.VMEM((length, lanes), f32),
        ],
        flops=30 * 10**9,
        smem=2,
        lazy=10,
    )
    dqkv_near, dqkv_far, *out_terms = lax.optimization_barrier(
        (dqkv_near, dqkv_far, *out_terms)
    )
    (table,) = kernel_call(
        functools.partial(weight_grads_kernel, slab),
        "attention_weights",
        [shape_of((depth, 8 * pack_rows + out_rows, LANES))],
        (
            normed, dqkv_near, dqkv_far, spread_main, spread_rest,
            grouped_near, grouped_far, *branch_parts,
        ),
        flops=5 * 10**9,
        vmem=32,
    )
    table, dqkv_near = lax.optimization_barrier((table, dqkv_near))
    table = line_scatter(place, table)
    *terms, gain_attn_sum = plane_terms(
        place, dqkv_near, dqkv_far, w_wide, w_wide_other, True, "project_back",
        tuple(token_parts[:4]),
    )
    (small,) = kernel_call(
        small_kernel,
        "small_sums",
        [shape_of((2 * (width // LANES) + 2 * HEADS, LANES), f32)],
        (at, gain_attn_sum, gain_ffn_sum, grad_taps, grad_mix, grad_gain_group),
        smem=1,
        vmem=16,
    )
    terms = chip_scatter(place, terms)
    for flip in (place.core_flip, place.x_flip, place.y_flip, 2, 4):
        small = small + swapped(small, flip)
    (grad_tokens,) = kernel_call(
        input_back_kernel,
        "input_back",
        [shape_of(flat)],
        (*terms, own_tokens, grad_middle, gains),
        vmem=16,
    )
    (output,) = kernel_call(
        output_kernel, "output", [shape_of(flat)], (*out_terms, middle), vmem=16
    )
    grad_w_gate, grad_w_up, grad_w_down = kernel_call(
        functools.partial(unpack_hidden_kernel, sub),
        "unpack_hidden",
        [
            shape_of((deep, seq_count * sub), f32),
            shape_of((deep, seq_count * sub), f32),
            shape_of((seq_count * sub, deep), f32),
        ],
        (ffn_g,),
        vmem=16,
    )
    output, grad_w_gate, grad_tokens, small, table = lax.optimization_barrier(
        (output, grad_w_gate, grad_tokens, small, table)
    )
    back = [(target, source) for source, target in out_pairs(place)]
    out_table = lax.ppermute(table[8 * pack_rows :], FLAT, back)
    table = plane_exchange(place, table[: 8 * pack_rows].reshape(8, pack_rows, LANES))
    grad_rows = kernel_call(
        functools.partial(unpack_kernel, slab),
        "unpack_projections",
        [shape_of((slab, width), f32)] * 4,
        (table, out_table),
        vmem=16,
    )
    small_flat = small.reshape(-1)
    row = (place.seq * place.wide_count + lax.axis_index("wide")) * slab
    tiles = width // LANES
    gain_grads = [lax.dynamic_slice_in_dim(small_flat, i * width + row, slab) for i in range(2)]
    head, side = row // HEAD_DIM, row % HEAD_DIM
    gain_grads.append(
        lax.dynamic_slice_in_dim(small_flat, (2 * tiles + head) * LANES + side, slab)
    )
    heads = small[2 * tiles + HEADS :]
    grad_conv = heads[:, : 16 * CQ].reshape(HEADS, CQ, 16)[:, :, :CK]
    grad_head_mix = heads[:, 16 * CQ : 16 * CQ + GROUP]
    return (
        output[None],
        grad_tokens[None],
        grad_rows[0],
        grad_rows[1],
        grad_rows[2],
        grad_rows[3],
        gain_grads[0],
        gain_grads[2],
        gain_grads[1],
        grad_conv,
        grad_head_mix,
        grad_w_gate,
        grad_w_up,
        grad_w_down,
    )


def solution(mesh):
    planes = mesh.shape["seq"] == 4 and mesh.shape["wide"] == 8
    return jax.shard_map(
        plane_shards if planes else shards,
        mesh=mesh,
        in_specs=(
            P("wide", "seq", None),
            P("wide", None),
            P(("seq", "wide"), None),
            P(("seq", "wide"), None),
            P(("seq", "wide"), None),
            P(("seq", "wide"), None),
            P(("seq", "wide")),
            P(("seq", "wide")),
            P(("seq", "wide")),
            P(),
            P(),
            P("seq", "wide"),
            P("seq", "wide"),
            P("wide", "seq"),
            P("wide", "seq", None),
        ),
        out_specs=(
            P("wide", "seq", None),
            P("wide", "seq", None),
            P(("seq", "wide"), None),
            P(("seq", "wide"), None),
            P(("seq", "wide"), None),
            P(("seq", "wide"), None),
            P(("seq", "wide")),
            P(("seq", "wide")),
            P(("seq", "wide")),
            P(),
            P(),
            P("seq", "wide"),
            P("seq", "wide"),
            P("wide", "seq"),
        ),
        check_vma=False,
    )
```

```python
import functools

import jax
import jax.numpy as jnp
from jax import lax
from jax.experimental import pallas as pl
from jax.experimental.pallas import tpu as pltpu
from jax.sharding import PartitionSpec as P

HEADS = 16
HEAD_DIM = 96
CQ = 6
CK = 11
GROUP = 2
LANES = 128
BLOCK = 128
RIM = 16


precise = lax.Precision.HIGHEST
epsilon = 1e-05


def passed_along(value, axis, by):
    devices = lax.axis_size(axis)
    pairs = [(i, i + by) for i in range(devices) if 0 <= i + by < devices]
    return lax.ppermute(value, axis, pairs)


def extended(block, sides, width):
    for axis, dim in sides:
        count = lax.axis_size(axis)
        forward = [(i, i + 1) for i in range(count - 1)]
        backward = [(target, source) for source, target in forward]
        low = lax.ppermute(
            lax.slice_in_dim(block, block.shape[dim] - width, None, axis=dim), axis, forward
        )
        high = lax.ppermute(lax.slice_in_dim(block, 0, width, axis=dim), axis, backward)
        block = jnp.concatenate([low, block, high], axis=dim)
    return block


def rms_scaled(values, gain_vec):
    return (
        values * lax.rsqrt(jnp.mean(values * values, axis=-1, keepdims=True) + epsilon) * gain_vec
    )


def group_scaled(values, gain_vec):
    center = values - jnp.mean(values, axis=-1, keepdims=True)
    spread = jnp.mean(center * center, axis=-1, keepdims=True)
    return center * lax.rsqrt(spread + epsilon) * gain_vec


def tile_masks(seg_query, pos_query, seg_key, pos_key, valid_flag):
    query_rim = CQ - 1
    key_rim = CK // 2
    allowed = (
        (seg_query[:, None] == seg_key[None, :])
        & (pos_key[None, :] <= pos_query[:, None])
        & valid_flag
    )
    row_count = seg_query.shape[0] - query_rim
    row_masks = jnp.stack(
        [
            (
                seg_query[query_rim - shift_q : query_rim - shift_q + row_count]
                == seg_query[query_rim:]
            ).astype(jnp.float32)
            for shift_q in range(CQ)
        ]
    )
    final_mask = allowed[query_rim:, key_rim : key_rim + row_count]
    return (allowed, row_masks, final_mask)


def convolve(scores, allowed, row_masks, kernel):
    query_rim = CQ - 1
    key_rim = CK // 2
    row_count = scores.shape[1] - query_rim
    col_count = scores.shape[2] - 2 * key_rim
    masked = jnp.where(allowed[None], scores, 0.0)
    summed = jnp.zeros((scores.shape[0], row_count, col_count), jnp.float32)
    for shift_q in range(CQ):
        inner_sum = jnp.zeros((scores.shape[0], row_count, col_count), jnp.float32)
        for shift_k in range(CK):
            piece_view = masked[
                :,
                query_rim - shift_q : query_rim - shift_q + row_count,
                2 * key_rim - shift_k : 2 * key_rim - shift_k + col_count,
            ]
            inner_sum = inner_sum + kernel[:, shift_q, shift_k][:, None, None] * piece_view
        summed = summed + row_masks[shift_q][None, :, None] * inner_sum
    return summed


def mix_heads(probs, head_mix):
    lead_dims = probs.shape[:-3]
    tail_dims = probs.shape[-2:]
    grouped = probs.reshape(lead_dims + (HEADS // GROUP, GROUP) + tail_dims)
    mixing = head_mix.reshape(HEADS // GROUP, GROUP, GROUP)
    summed = jnp.zeros(lead_dims + (HEADS // GROUP, GROUP) + tail_dims, jnp.float32)
    for source in range(GROUP):
        summed = summed + mixing[:, :, source][:, :, None, None] * jnp.expand_dims(
            grouped[..., :, source, :, :], -3
        )
    return summed.reshape(probs.shape)


def unmix_heads(grads, head_mix):
    lead_dims = grads.shape[:-3]
    tail_dims = grads.shape[-2:]
    grouped = grads.reshape(lead_dims + (HEADS // GROUP, GROUP) + tail_dims)
    mixing = head_mix.reshape(HEADS // GROUP, GROUP, GROUP)
    summed = jnp.zeros(lead_dims + (HEADS // GROUP, GROUP) + tail_dims, jnp.float32)
    for target in range(GROUP):
        summed = summed + mixing[:, target, :][:, :, None, None] * jnp.expand_dims(
            grouped[..., :, target, :, :], -3
        )
    return summed.reshape(grads.shape)


def contract(left_op, right_op, left_dim, right_dim):
    return lax.dot_general(
        left_op,
        right_op,
        (((left_dim,), (right_dim,)), ((), ())),
        preferred_element_type=jnp.float32,
    )


def gather_attention(w_query, w_key, w_value, w_out, gain_attn, gain_group, gain_ffn):
    return (
        lax.all_gather(w_query.astype(jnp.bfloat16), ("seq", "wide"), axis=0, tiled=True),
        lax.all_gather(w_key.astype(jnp.bfloat16), ("seq", "wide"), axis=0, tiled=True),
        lax.all_gather(w_value.astype(jnp.bfloat16), ("seq", "wide"), axis=0, tiled=True),
        lax.all_gather(w_out.astype(jnp.bfloat16), ("seq", "wide"), axis=0, tiled=True),
        lax.all_gather(gain_attn.astype(jnp.bfloat16), ("seq", "wide"), axis=0, tiled=True),
        lax.all_gather(gain_group.astype(jnp.bfloat16), ("seq", "wide"), axis=0, tiled=True),
        lax.all_gather(gain_ffn.astype(jnp.bfloat16), ("seq", "wide"), axis=0, tiled=True),
    )


def collect_packets(own, reach_len):
    stored = jnp.zeros((reach_len,) + own.shape, own.dtype).at[0].set(own)

    def advance(turn_index, state_pair):
        packet, stored_now = state_pair
        packet = passed_along(packet, "seq", 1)
        return (packet, lax.dynamic_update_index_in_dim(stored_now, packet, turn_index, 0))

    return lax.fori_loop(1, reach_len, advance, (own, stored))[1]


def tile_logits(query_ext, packet, seg_query, pos_query, seg_key_pad, other_shard, token_count):
    key_rim = CK // 2
    key_ext = packet[: token_count + 2 * key_rim].reshape(
        token_count + 2 * key_rim, HEADS, HEAD_DIM
    )
    scores = jnp.einsum(
        "qhe,khe->hqk", query_ext, key_ext, preferred_element_type=jnp.float32
    ) * HEAD_DIM ** (-0.5)
    key_start = other_shard * token_count
    seg_key = lax.dynamic_slice_in_dim(
        seg_key_pad, jnp.maximum(key_start, 0), token_count + 2 * key_rim
    )
    pos_key = key_start - key_rim + jnp.arange(token_count + 2 * key_rim, dtype=jnp.int32)
    allowed, row_masks, final_mask = tile_masks(
        seg_query, pos_query, seg_key, pos_key, other_shard >= 0
    )
    return (scores, allowed, row_masks, final_mask, key_ext)


def shards(
    tokens,
    segments,
    w_query,
    w_key,
    w_value,
    w_out,
    gain_attn,
    gain_group,
    gain_ffn,
    conv_kernel,
    head_mix,
    w_gate,
    w_up,
    w_down,
    cotangent,
):
    token_count = tokens.shape[1]
    query_rim = CQ - 1
    key_rim = CK // 2
    width_all = HEADS * HEAD_DIM
    scaling = HEAD_DIM ** (-0.5)
    seq_count = lax.axis_size("seq")
    longest_doc = min(1024, token_count * seq_count // 2)
    reach_len = min(seq_count - 1, (longest_doc - 1) // token_count + 1) + 1
    seq_index = lax.axis_index("seq")
    row_start = seq_index * token_count
    seg_row = segments[0]
    seg_query_pad = jnp.concatenate([jnp.full((query_rim,), -1, jnp.int32), seg_row])
    seg_key_pad = jnp.concatenate(
        [jnp.full((key_rim,), -2, jnp.int32), seg_row, jnp.full((key_rim,), -2, jnp.int32)]
    )
    seg_query = lax.dynamic_slice_in_dim(seg_query_pad, row_start, token_count + query_rim)
    pos_query = row_start - query_rim + jnp.arange(token_count + query_rim, dtype=jnp.int32)
    weights = gather_attention(w_query, w_key, w_value, w_out, gain_attn, gain_group, gain_ffn)
    query_mat, key_mat, value_mat, out_mat, gain_one, gain_mid, gain_two = weights
    inputs = tokens[0].astype(jnp.float32)
    gain_first = gain_one.astype(jnp.float32)
    normed = rms_scaled(inputs, gain_first).astype(jnp.bfloat16)
    queries = jnp.dot(normed, query_mat, preferred_element_type=jnp.float32).astype(jnp.bfloat16)
    keys_loc = jnp.dot(normed, key_mat, preferred_element_type=jnp.float32).astype(jnp.bfloat16)
    values_loc = jnp.dot(normed, value_mat, preferred_element_type=jnp.float32).astype(jnp.bfloat16)
    rimmed = extended(jnp.stack([queries, keys_loc]), (("seq", 1),), key_rim)
    query_ext = rimmed[0, : token_count + query_rim].reshape(
        token_count + query_rim, HEADS, HEAD_DIM
    )
    own = jnp.concatenate([rimmed[1], values_loc], axis=0)
    packets = collect_packets(own, reach_len)

    def all_logits(packet_stack):

        def logits_of(turn_index):
            packet = lax.dynamic_index_in_dim(packet_stack, turn_index, 0, keepdims=False)
            scores, allowed, row_masks, final_mask, key_ext = tile_logits(
                query_ext,
                packet,
                seg_query,
                pos_query,
                seg_key_pad,
                seq_index - turn_index,
                token_count,
            )
            return jnp.where(
                final_mask[None], convolve(scores, allowed, row_masks, conv_kernel), -jnp.inf
            )

        return lax.map(logits_of, jnp.arange(reach_len, dtype=jnp.int32))

    logits = all_logits(packets)
    peak_val = jnp.max(logits, axis=(0, 3))
    log_total = peak_val + jnp.log(
        jnp.sum(jnp.exp(logits - peak_val[None, :, :, None]), axis=(0, 3))
    )
    probs_all = jnp.exp(logits - log_total[None, :, :, None])
    mixed_b = mix_heads(probs_all, head_mix).astype(jnp.bfloat16)
    values_all = packets[:, token_count + 2 * key_rim :].reshape(
        reach_len, token_count, HEADS, HEAD_DIM
    )
    attended = jnp.einsum("rhtk,rkhe->the", mixed_b, values_all, preferred_element_type=jnp.float32)
    gain_middle = gain_mid.astype(jnp.float32).reshape(HEADS, HEAD_DIM)
    grouped = (
        group_scaled(attended, gain_middle).reshape(token_count, width_all).astype(jnp.bfloat16)
    )
    middle = inputs + jnp.dot(grouped, out_mat, preferred_element_type=jnp.float32)
    gain_second = gain_two.astype(jnp.float32)
    ffn_in = rms_scaled(middle, gain_second).astype(jnp.bfloat16)
    ffn_all = lax.all_gather(ffn_in, "wide", axis=0, tiled=True)
    gate_mat, up_mat, down_mat = (
        lax.all_gather(w_gate.astype(jnp.bfloat16), "seq", axis=0, tiled=True),
        lax.all_gather(w_up.astype(jnp.bfloat16), "seq", axis=0, tiled=True),
        lax.all_gather(w_down.astype(jnp.bfloat16), "seq", axis=1, tiled=True),
    )
    gate_val = jnp.dot(ffn_all, gate_mat, preferred_element_type=jnp.float32)
    up_val = jnp.dot(ffn_all, up_mat, preferred_element_type=jnp.float32)
    hidden = (jax.nn.silu(gate_val) * up_val).astype(jnp.bfloat16)
    ffn_out = lax.psum_scatter(
        jnp.dot(hidden, down_mat, preferred_element_type=jnp.float32).astype(jnp.bfloat16),
        "wide",
        scatter_dimension=0,
        tiled=True,
    ).astype(jnp.float32)
    output = (middle + ffn_out).astype(jnp.bfloat16)
    grad_out = cotangent[0]
    grad_all = lax.all_gather(grad_out, "wide", axis=0, tiled=True)
    grad_hidden = contract(grad_all, down_mat, 1, 1)
    grad_down = contract(hidden, grad_all, 0, 0)
    sig_gate = jax.nn.sigmoid(gate_val)
    grad_gate = (grad_hidden * up_val * sig_gate * (1.0 + gate_val * (1.0 - sig_gate))).astype(
        jnp.bfloat16
    )
    grad_up = (grad_hidden * gate_val * sig_gate).astype(jnp.bfloat16)
    grad_gate_w = contract(ffn_all, grad_gate, 0, 0)
    grad_up_w = contract(ffn_all, grad_up, 0, 0)
    grad_ffn_in = lax.psum_scatter(
        (contract(grad_gate, gate_mat, 1, 1) + contract(grad_up, up_mat, 1, 1)).astype(
            jnp.bfloat16
        ),
        "wide",
        scatter_dimension=0,
        tiled=True,
    ).astype(jnp.float32)
    ffn_grads = (
        lax.psum_scatter(
            grad_gate_w.astype(jnp.bfloat16), "seq", scatter_dimension=0, tiled=True
        ).astype(jnp.float32),
        lax.psum_scatter(
            grad_up_w.astype(jnp.bfloat16), "seq", scatter_dimension=0, tiled=True
        ).astype(jnp.float32),
        lax.psum_scatter(
            grad_down.astype(jnp.bfloat16), "seq", scatter_dimension=1, tiled=True
        ).astype(jnp.float32),
    )
    norm_two_back = jax.vjp(rms_scaled, middle, gain_second)[1]
    grad_mid_part, grad_gain_two = norm_two_back(grad_ffn_in)
    grad_middle = grad_out.astype(jnp.float32) + grad_mid_part
    grad_branch = grad_middle.astype(jnp.bfloat16)
    back_weights = gather_attention(w_query, w_key, w_value, w_out, gain_attn, gain_group, gain_ffn)
    query_back, key_back, value_back, out_back = (
        back_weights[0],
        back_weights[1],
        back_weights[2],
        back_weights[3],
    )
    grad_grouped = contract(grad_branch, out_back, 1, 1)
    grad_out_w = contract(grouped, grad_branch, 0, 0)
    group_back = jax.vjp(group_scaled, attended, gain_middle)[1]
    grad_attended, grad_gain_mid = group_back(grad_grouped.reshape(token_count, HEADS, HEAD_DIM))
    grad_att_b = grad_attended.astype(jnp.bfloat16)
    back_packets = collect_packets(own, reach_len)
    logits_again = all_logits(back_packets)
    probs_again = jnp.exp(logits_again - log_total[None, :, :, None])
    mixed_again = mix_heads(probs_again, head_mix).astype(jnp.bfloat16)
    values_back = back_packets[:, token_count + 2 * key_rim :].reshape(
        reach_len, token_count, HEADS, HEAD_DIM
    )
    grad_mixed = jnp.einsum(
        "the,rkhe->rhtk", grad_att_b, values_back, preferred_element_type=jnp.float32
    )
    grad_values = jnp.einsum(
        "rhtk,the->rkhe", mixed_again, grad_att_b, preferred_element_type=jnp.float32
    ).reshape(reach_len, token_count, width_all)
    probs_grouped = probs_again.reshape(reach_len, HEADS // GROUP, GROUP, token_count, token_count)
    mixed_grouped = grad_mixed.reshape(reach_len, HEADS // GROUP, GROUP, token_count, token_count)
    grad_mix = jnp.einsum(
        "rgdtk,rgctk->gcd", probs_grouped, mixed_grouped, precision=precise
    ).reshape(HEADS, GROUP)
    grad_probs = unmix_heads(grad_mixed, head_mix)
    delta_row = jnp.sum(probs_again * grad_probs, axis=(0, 3))
    grad_logits = probs_again * (grad_probs - delta_row[None, :, :, None])

    def tile_grads(turn_index):
        packet = lax.dynamic_index_in_dim(back_packets, turn_index, 0, keepdims=False)
        scores, allowed, row_masks, final_mask, key_ext = tile_logits(
            query_ext,
            packet,
            seg_query,
            pos_query,
            seg_key_pad,
            seq_index - turn_index,
            token_count,
        )
        conv_back = jax.vjp(
            lambda field, weights_k: convolve(field, allowed, row_masks, weights_k),
            scores,
            conv_kernel,
        )[1]
        grad_scores, grad_kernel = conv_back(
            lax.dynamic_index_in_dim(grad_logits, turn_index, 0, keepdims=False)
        )
        grad_scores_b = grad_scores.astype(jnp.bfloat16)
        grad_query_ext = (
            jnp.einsum("hqk,khe->qhe", grad_scores_b, key_ext, preferred_element_type=jnp.float32)
            * scaling
        )
        grad_key_ext = (
            jnp.einsum("hqk,qhe->khe", grad_scores_b, query_ext, preferred_element_type=jnp.float32)
            * scaling
        )
        cycle_term = jnp.concatenate(
            [
                grad_key_ext.reshape(token_count + 2 * key_rim, width_all),
                lax.dynamic_index_in_dim(grad_values, turn_index, 0, keepdims=False),
            ],
            axis=0,
        )
        return (cycle_term, grad_query_ext, grad_kernel)

    start_term, start_query, start_kernel = tile_grads(reach_len - 1)

    def descend(turn_index, state_all):
        cycle_acc, query_acc, kernel_acc = state_all
        cycle_term, query_part, kernel_part = tile_grads(reach_len - 1 - turn_index)
        moved_acc = passed_along(cycle_acc.astype(jnp.bfloat16), "seq", -1).astype(cycle_acc.dtype)
        return (moved_acc + cycle_term, query_acc + query_part, kernel_acc + kernel_part)

    cycle_acc, query_acc, kernel_acc = lax.fori_loop(
        1, reach_len, descend, (start_term, start_query, start_kernel)
    )
    query_flat = query_acc.reshape(token_count + query_rim, width_all)
    key_ext_grad = cycle_acc[: token_count + 2 * key_rim]
    grad_values_own = cycle_acc[token_count + 2 * key_rim :]
    edge_grads = jnp.stack(
        [
            jnp.concatenate([query_flat[:query_rim], jnp.zeros((key_rim, width_all), jnp.float32)]),
            jnp.concatenate([key_ext_grad[:key_rim], key_ext_grad[token_count + key_rim :]]),
        ]
    )
    rim_back = extended(edge_grads.astype(jnp.bfloat16), (("seq", 1),), key_rim).astype(
        edge_grads.dtype
    )
    grad_queries = (
        query_flat[query_rim:].at[token_count - key_rim :].add(rim_back[0, 3 * key_rim :])
    )
    grad_keys = (
        key_ext_grad[key_rim : key_rim + token_count]
        .at[:key_rim]
        .add(rim_back[1, :key_rim])
        .at[token_count - key_rim :]
        .add(rim_back[1, 3 * key_rim :])
    )
    grad_query_b = grad_queries.astype(jnp.bfloat16)
    grad_key_b = grad_keys.astype(jnp.bfloat16)
    grad_value_b = grad_values_own.astype(jnp.bfloat16)
    grad_query_w = contract(normed, grad_query_b, 0, 0)
    grad_key_w = contract(normed, grad_key_b, 0, 0)
    grad_value_w = contract(normed, grad_value_b, 0, 0)
    grad_normed = (
        contract(grad_query_b, query_back, 1, 1)
        + contract(grad_key_b, key_back, 1, 1)
        + contract(grad_value_b, value_back, 1, 1)
    )
    norm_one_back = jax.vjp(rms_scaled, inputs, gain_first)[1]
    grad_in_part, grad_gain_one = norm_one_back(grad_normed)
    grad_input = (grad_middle + grad_in_part).astype(jnp.bfloat16)
    attn_grads = (
        lax.psum_scatter(grad_query_w, ("seq", "wide"), scatter_dimension=0, tiled=True),
        lax.psum_scatter(grad_key_w, ("seq", "wide"), scatter_dimension=0, tiled=True),
        lax.psum_scatter(grad_value_w, ("seq", "wide"), scatter_dimension=0, tiled=True),
        lax.psum_scatter(grad_out_w, ("seq", "wide"), scatter_dimension=0, tiled=True),
        lax.psum_scatter(grad_gain_one, ("seq", "wide"), scatter_dimension=0, tiled=True),
        lax.psum_scatter(
            grad_gain_mid.reshape(width_all), ("seq", "wide"), scatter_dimension=0, tiled=True
        ),
        lax.psum_scatter(grad_gain_two, ("seq", "wide"), scatter_dimension=0, tiled=True),
    )
    small_sums = lax.psum((kernel_acc, grad_mix), ("seq", "wide"))
    return (
        output[None],
        grad_input[None],
        attn_grads[0],
        attn_grads[1],
        attn_grads[2],
        attn_grads[3],
        attn_grads[4],
        attn_grads[5],
        attn_grads[6],
        small_sums[0],
        small_sums[1],
        ffn_grads[0],
        ffn_grads[1],
        ffn_grads[2],
    )


def dot_plain(left, right):
    return contract(left, right, 1, 0)


def dot_nt(left, right):
    return contract(left, right, 1, 1)


def dot_tn(left, right):
    return contract(left, right, 0, 0)


def halves(value):
    high = value.astype(jnp.bfloat16)
    return high, (value - high.astype(jnp.float32)).astype(jnp.bfloat16)


def iota(shape, dim):
    return lax.broadcasted_iota(jnp.int32, shape, dim)


def spread_lanes(tile, count):
    return tile if count == 1 else jnp.concatenate([tile] * count, axis=1)


def allowed_mask(starts, block, first_col, count):
    cols = iota((BLOCK, count * LANES), 1) + first_col
    rows = iota((BLOCK, count * LANES), 0) + block * BLOCK
    return (cols >= spread_lanes(starts, count)) & (cols <= rows)


def head_stats(values):
    lane = iota(values.shape, 1)
    mean = jnp.sum(values, axis=-1, keepdims=True) * (1.0 / HEAD_DIM)
    center = jnp.where(lane < HEAD_DIM, values - mean, 0.0)
    spread = jnp.sum(center * center, axis=-1, keepdims=True) * (1.0 / HEAD_DIM)
    inverse = lax.rsqrt(spread + epsilon)
    return center * inverse, inverse


def fold_rows(value):
    return jnp.sum(value.reshape(value.shape[0] // 8, 8, value.shape[1]), axis=0)


def full_spec():
    return pl.BlockSpec(memory_space=pltpu.VMEM)


def smem_spec():
    return pl.BlockSpec(memory_space=pltpu.SMEM)


def shape_of(shape, dtype=jnp.bfloat16):
    return jax.ShapeDtypeStruct(shape, dtype)


def in_hbm(value):
    return pltpu.with_memory_space_constraint(value, pltpu.HBM)


def kernel_call(body, name, outs, ins, scratch=(), flops=0, smem=0, vmem=40, lazy=0, hbm=0):
    still = lazy + hbm
    moved = sum(v.size * v.dtype.itemsize for v in ins) + sum(
        o.size * o.dtype.itemsize for o in outs
    )
    return pl.pallas_call(
        body,
        in_specs=[smem_spec()] * smem
        + [full_spec()] * (len(ins) - smem - still)
        + [pl.BlockSpec(memory_space=pltpu.HBM)] * still,
        out_specs=[full_spec()] * len(outs),
        out_shape=list(outs),
        scratch_shapes=[pltpu.VMEM(v.shape, v.dtype) for v in ins[len(ins) - lazy :]]
        + [pltpu.SemaphoreType.DMA((lazy,))] * min(lazy, 1)
        + list(scratch),
        compiler_params=pltpu.CompilerParams(vmem_limit_bytes=vmem << 20),
        cost_estimate=pl.CostEstimate(flops=flops, bytes_accessed=moved, transcendentals=0),
        name=name,
    )(*ins[: len(ins) - still], *(in_hbm(v) for v in ins[len(ins) - still :]))


def started(sources, targets, sems):
    copies = [
        pltpu.make_async_copy(source, target, sems.at[i])
        for i, (source, target) in enumerate(zip(sources, targets))
    ]
    for copy in copies:
        copy.start()

    def wait(first, last):
        for copy in copies[first:last]:
            copy.wait()

    return wait


ORDER = (0, 4, 1, 5, 2, 6, 3, 7)


def slot_place(plane, slot):
    other = plane ^ ORDER[slot]
    return other & 1, pl.multiple_of((other >> 1) * BLOCK, BLOCK)


def half_tile(tiles, index):
    tile = tiles[index // 2]
    return tile, pltpu.roll(tile, LANES // 2, 1), index % 2


def joined(first, second):
    low = first[1] if first[2] else first[0]
    high = second[0] if second[2] else second[1]
    lane = iota(low.shape, 1)
    return jnp.where(lane < LANES // 2, low, high)


def pack_kernel(slab, q_ref, k_ref, v_ref, gains_ref, rows_ref, out_ref, rows_out_ref):
    tiles = [
        [ref[:, t * LANES : (t + 1) * LANES] for t in range(ref.shape[1] // LANES)]
        for ref in (q_ref, k_ref, v_ref)
    ]
    per = GROUP * HEAD_DIM // (LANES // 2)
    for g in range(8):
        parts = [half_tile(tiles[w], per * g + i) for w in range(3) for i in range(per)]
        for t in range(4):
            out_ref[g, t * slab : (t + 1) * slab, :] = joined(
                parts[2 * t], parts[2 * t + 1]
            ).astype(jnp.bfloat16)
        tile, turned, side = parts[8]
        first, second = (turned, tile) if side else (tile, turned)
        half = slab // 2
        lane = iota((half, LANES), 1)
        out_ref[g, 4 * slab : 4 * slab + half, :] = jnp.where(
            lane < LANES // 2, first[:half], second[half:]
        ).astype(jnp.bfloat16)
        out_ref[g, 4 * slab + half :, :] = gains_ref[...]
    for t in range(rows_ref.shape[1] // LANES):
        rows_out_ref[t * slab : (t + 1) * slab, :] = rows_ref[
            :, t * LANES : (t + 1) * LANES
        ].astype(jnp.bfloat16)


def unpack_kernel(slab, in_ref, rows_ref, q_ref, k_ref, v_ref, out_ref):
    per = GROUP * HEAD_DIM // (LANES // 2)
    pieces = [[], [], []]
    half = slab // 2
    lane = iota((half, LANES), 1)
    for g in range(8):
        tiles = [
            in_ref[g, t * slab : (t + 1) * slab, :].astype(jnp.float32) for t in range(4)
        ]
        rest = in_ref[g, 4 * slab : 4 * slab + half, :].astype(jnp.float32)
        turned = pltpu.roll(rest, LANES // 2, 1)
        tiles.append(jnp.concatenate([rest, turned], axis=0))
        for i in range(3 * per):
            pieces[i // per].append(half_tile(tiles, i))
    for ref, parts in zip((q_ref, k_ref, v_ref), pieces):
        for t in range(len(parts) // 2):
            ref[:, t * LANES : (t + 1) * LANES] = joined(parts[2 * t], parts[2 * t + 1])
    for t in range(out_ref.shape[1] // LANES):
        out_ref[:, t * LANES : (t + 1) * LANES] = rows_ref[t * slab : (t + 1) * slab, :].astype(
            jnp.float32
        )


def attend_pack(p, blocks, reach, mix_ref, q_ref, k_ref, v_ref, start_ref, th_ref, tl_ref, gain,
                probs_ref, high_ref, att_ref, grouped_ref, low_ref, part_ref):
    key_rim = CK // 2
    scaling = HEAD_DIM ** (-0.5)
    for h in range(GROUP):
        lanes = slice(h * LANES, (h + 1) * LANES)
        high_ref[p, h, :RIM, :] = jnp.zeros((RIM, high_ref.shape[3]), jnp.bfloat16)
        low_ref[h, :RIM, :] = jnp.zeros((RIM, high_ref.shape[3]), jnp.bfloat16)
        for n in range(blocks):
            first, last = max(0, n - reach), min(n + 3, blocks + 1)
            rows = slice(n * BLOCK, (n + 1) * BLOCK)
            scores = (
                dot_nt(q_ref[p, rows, lanes], k_ref[p, first * BLOCK : last * BLOCK, lanes]) * scaling
            )
            keep = allowed_mask(start_ref[p, rows, :], n, first * BLOCK - key_rim, last - first)
            high, low = halves(jnp.where(keep, scores, 0.0))
            into = slice(RIM + n * BLOCK, RIM + (n + 1) * BLOCK)
            cols = slice(first * LANES, last * LANES)
            high_ref[p, h, into, cols] = high
            low_ref[h, into, cols] = low
    for n in range(blocks):
        first = max(0, n - reach)
        count = n - first + 1
        rows = slice(n * BLOCK, (n + 1) * BLOCK)
        starts = start_ref[p, rows, :]
        offset = iota((BLOCK, LANES), 0) + n * BLOCK - starts
        keep = allowed_mask(starts, n, first * BLOCK, count)
        window = slice((reach + 1 - count) * LANES, (reach + 1) * LANES)
        probs = []
        for h in range(GROUP):
            pieces = []
            for m in range(first, n + 1):
                rim_rows = slice(n * BLOCK, (n + 1) * BLOCK + RIM)
                cols = slice(m * LANES, (m + 2) * LANES)
                high = high_ref[p, h, rim_rows, cols]
                low = low_ref[h, rim_rows, cols]
                part = (
                    dot_plain(high, th_ref[h])
                    + dot_plain(low, th_ref[h])
                    + dot_plain(high, tl_ref[h])
                )
                for a in range(CQ):
                    part_ref[a] = part[:, a * LANES : (a + 1) * LANES]
                total = part_ref[0, RIM:, :]
                for a in range(1, CQ):
                    total = total + jnp.where(
                        offset >= a, part_ref[a, RIM - a : RIM - a + BLOCK, :], 0.0
                    )
                pieces.append(total)
            logits = pieces[0] if count == 1 else jnp.concatenate(pieces, axis=1)
            logits = jnp.where(keep, logits, -jnp.inf)
            peak = jnp.max(logits, axis=-1, keepdims=True)
            raised = jnp.exp(logits - peak)
            prob = raised / jnp.sum(raised, axis=-1, keepdims=True)
            probs_ref[p, h, rows, window] = prob
            probs.append(prob)
        keys = slice(first * BLOCK, (n + 1) * BLOCK)
        for h in range(GROUP):
            lanes = slice(h * LANES, (h + 1) * LANES)
            mixed = (mix_ref[h, 0] * probs[0] + mix_ref[h, 1] * probs[1]).astype(jnp.bfloat16)
            attended = dot_plain(mixed, v_ref[p, keys, lanes])
            att_ref[p, rows, lanes] = attended
            normal, _ = head_stats(attended)
            grouped_ref[p, rows, lanes] = (normal * gain[:, lanes]).astype(jnp.bfloat16)


def forward_kernel(
    blocks, reach, slab, at_ref, mix_ref, w_ref, t0, t1, t2, t3, t4, t5, t6, t7,
    start_ref, th_ref, tl_ref, spread_ref, rest_ref,
    normed_ref, wide_ref, q_ref, k_ref, v_ref, probs_ref, high_ref, att_ref, near_ref,
    far_ref, gains_ref, gain_ref,
    grp_ref, shift_ref, low_ref, part_ref,
):
    plane = at_ref[0]
    half = slab // 2
    block = 4 * slab + half + 8
    gains_ref[...] = jnp.zeros_like(gains_ref)
    span = gains_ref.shape[1] // 4
    for zz in range(w_ref.shape[0]):
        ref = w_ref.at[zz]
        main = jnp.concatenate(
            [
                jnp.concatenate(
                    [ref[g * block + t * slab : g * block + (t + 1) * slab, :] for t in range(4)],
                    axis=1,
                )
                for g in range(8)
            ],
            axis=0,
        )
        rest = jnp.concatenate(
            [ref[g * block + 4 * slab : g * block + 4 * slab + half, :] for g in range(8)], axis=0
        )
        table = dot_plain(main, spread_ref[...])
        early = dot_plain(rest, rest_ref[0])
        late = dot_plain(rest, rest_ref[1])
        for g in range(8):
            row = (g // 2 * 8 + g % 2 + 2 * zz) * slab
            tail = jnp.concatenate(
                [early[g * half : (g + 1) * half], late[g * half : (g + 1) * half]], axis=0
            )
            wide_ref[row : row + slab, :] = (table[g * slab : (g + 1) * slab] + tail).astype(
                jnp.bfloat16
            )
        lane = iota((LANES, span), 0)
        for y in range(2):
            place = (iota((LANES, span), 1) == lane + (zz * 2 + y) * slab) & (lane < slab)
            place = jnp.where(place, 1.0, 0.0).astype(jnp.bfloat16)
            for s in range(4):
                gains_ref[:, s * span : (s + 1) * span] += dot_plain(
                    ref[(2 * s + y + 1) * block - 8 : (2 * s + y + 1) * block, :], place
                )
    cols = GROUP * HEAD_DIM
    width = gains_ref.shape[1]
    lane = iota((width, GROUP * LANES), 1)
    from_row = iota((width, GROUP * LANES), 0) - plane * cols
    select = (from_row == lane // LANES * HEAD_DIM + lane % LANES) & (lane % LANES < HEAD_DIM)
    gain_ref[...] = dot_plain(
        gains_ref[...].astype(jnp.bfloat16), jnp.where(select, 1.0, 0.0).astype(jnp.bfloat16)
    )[1:2]
    gain = gain_ref[...]
    for slot, ref in enumerate((t0, t1, t2, t3, t4, t5, t6, t7)):
        value = ref[...].astype(jnp.float32)
        scale = lax.rsqrt(jnp.mean(value * value, axis=-1, keepdims=True) + epsilon)
        normed_ref[slot * BLOCK : (slot + 1) * BLOCK, :] = (
            value * scale * gains_ref[0:1, :]
        ).astype(jnp.bfloat16)
    lanes = GROUP * LANES
    shift_ref[...] = jnp.zeros_like(shift_ref)
    for slots in (range(4), range(4, 8)):
        rows = slice(slots[0] * BLOCK, (slots[-1] + 1) * BLOCK)
        qkv = dot_plain(normed_ref[rows, :], wide_ref[...])
        for i, slot in enumerate(slots):
            pack, row = slot_place(plane, slot)
            part = qkv[i * BLOCK : (i + 1) * BLOCK]
            q_ref[pack, pl.ds(row, BLOCK), :] = part[:, :lanes].astype(jnp.bfloat16)
            shift_ref[pack, pl.ds(row, BLOCK), :] = part[:, lanes : 2 * lanes]
            v_ref[pack, pl.ds(row, BLOCK), :] = part[:, 2 * lanes :].astype(jnp.bfloat16)
    key_rim = CK // 2
    length = q_ref.shape[1]
    @pl.loop(0, 2)
    def _(p):
        moved = jnp.concatenate(
            [
                jnp.zeros((8, lanes), jnp.float32),
                shift_ref[p],
                jnp.zeros((LANES - 8, lanes), jnp.float32),
            ],
            axis=0,
        )
        moved = pltpu.roll(moved, length + LANES - (8 - key_rim), 0)
        k_ref[p] = moved.astype(jnp.bfloat16)
        attend_pack(
            p, blocks, reach, mix_ref, q_ref, k_ref, v_ref, start_ref, th_ref, tl_ref, gain,
            probs_ref, high_ref, att_ref, grp_ref, low_ref, part_ref,
        )

    for slot in range(8):
        pack, row = slot_place(plane, slot)
        into = near_ref if slot < 4 else far_ref
        into[slot % 4 * BLOCK : (slot % 4 + 1) * BLOCK, :] = grp_ref[pack, pl.ds(row, BLOCK), :]


def store_blocks(value, refs):
    for i, ref in enumerate(refs):
        ref[...] = value[i * BLOCK : (i + 1) * BLOCK].astype(ref.dtype)


def pair_kernel(
    transposed, own_ref, got_ref, w_from, other_from, total_ref, r1, r2, r3, w_ref, other_ref, sems
):
    wait = started((w_from, other_from), (w_ref, other_ref), sems)
    dot = dot_nt if transposed else dot_plain
    wait(0, 1)
    value = dot(own_ref[...], w_ref[...])
    wait(1, 2)
    value = value + dot(got_ref[...], other_ref[...])
    store_blocks(value, (total_ref, r1, r2, r3))


def pair_gain_kernel(
    own_ref, got_ref, w_from, other_from, t0_from, t1_from, t2_from, t3_from,
    total_ref, r1, r2, r3, gain_ref,
    w_ref, other_ref, t0, t1, t2, t3, sems,
):
    wait = started(
        (w_from, other_from, t0_from, t1_from, t2_from, t3_from),
        (w_ref, other_ref, t0, t1, t2, t3),
        sems,
    )
    wait(0, 1)
    value = dot_nt(own_ref[...], w_ref[...])
    wait(1, 6)
    value = value + dot_nt(got_ref[...], other_ref[...])
    store_blocks(value, (total_ref, r1, r2, r3))
    total = jnp.zeros(gain_ref.shape, jnp.float32)
    for i, ref in enumerate((t0, t1, t2, t3)):
        token = ref[...].astype(jnp.float32)
        scale = lax.rsqrt(jnp.mean(token * token, axis=-1, keepdims=True) + epsilon)
        total = total + fold_rows(value[i * BLOCK : (i + 1) * BLOCK] * (token * scale))
    gain_ref[...] = total


def small_kernel(at_ref, attn_ref, ffn_ref, taps_ref, mix_ref, group_ref, out_ref):
    plane = at_ref[0]
    out_ref[...] = jnp.zeros_like(out_ref)
    tiles = attn_ref.shape[1] // LANES
    for i, ref in enumerate((attn_ref, ffn_ref)):
        row = jnp.sum(ref[...], axis=0, keepdims=True)
        for t in range(tiles):
            out_ref[i * tiles + t : i * tiles + t + 1, :] = row[:, t * LANES : (t + 1) * LANES]
    group = jnp.sum(group_ref[...], axis=0, keepdims=True)
    lane = iota((16, LANES), 1)
    place = iota((16, LANES), 0)
    first = iota((1, LANES), 1)
    for h in range(GROUP):
        head = GROUP * plane + h
        out_ref[pl.ds(2 * tiles + head, 1), :] = group[:, h * LANES : (h + 1) * LANES]
        total = jnp.zeros((16, LANES), jnp.float32)
        for a in range(CQ):
            sums = jnp.sum(taps_ref[h, :, a * LANES : (a + 1) * LANES], axis=-1, keepdims=True)
            total = total + jnp.where(lane == 16 * a + place, sums, 0.0)
        row = jnp.sum(total, axis=0, keepdims=True)
        for d in range(GROUP):
            value = jnp.sum(mix_ref[h * GROUP + d], axis=0, keepdims=True)
            value = jnp.sum(value, axis=1, keepdims=True)
            row = row + jnp.where(first == 16 * CQ + d, value, 0.0)
        out_ref[pl.ds(2 * tiles + HEADS + head, 1), :] = row


def backward_pack(p, blocks, reach, mix_ref, gg_ref, att_ref, gain_ref, q_ref, k_ref, v_ref,
                  start_ref, stop_ref, probs_ref, high_ref, th_ref,
                  dqkv_ref, mixg_ref, gaing_ref, grad_ref, cross_ref, keyg_ref, valueg_ref, ready):
    key_rim = CK // 2
    scaling = HEAD_DIM ** (-0.5)
    all_lanes = GROUP * LANES
    grad_ref[...] = jnp.zeros_like(grad_ref)
    keyg_ref[...] = jnp.zeros_like(keyg_ref)
    valueg_ref[...] = jnp.zeros_like(valueg_ref)
    lane = iota((BLOCK, LANES), 1)
    for n in range(blocks):
        first = max(0, n - reach)
        count = n - first + 1
        rows = slice(n * BLOCK, (n + 1) * BLOCK)
        keys = slice(first * BLOCK, (n + 1) * BLOCK)
        window = slice((reach + 1 - count) * LANES, (reach + 1) * LANES)
        probs = [probs_ref[p, h, rows, window] for h in range(GROUP)]
        mixed_grads = []
        for h in range(GROUP):
            lanes = slice(h * LANES, (h + 1) * LANES)
            normal, inverse = head_stats(att_ref[p, rows, lanes])
            grad_grouped = gg_ref[p, rows, lanes]
            gaing_ref[:, lanes] += fold_rows(grad_grouped * normal)
            scaled = jnp.where(lane < HEAD_DIM, grad_grouped * gain_ref[:, lanes], 0.0)
            mean_one = jnp.sum(scaled, axis=-1, keepdims=True) * (1.0 / HEAD_DIM)
            mean_two = jnp.sum(scaled * normal, axis=-1, keepdims=True) * (1.0 / HEAD_DIM)
            grad_att = inverse * (scaled - mean_one - normal * mean_two)
            grad_att = jnp.where(lane < HEAD_DIM, grad_att, 0.0).astype(jnp.bfloat16)
            mixed_grads.append(dot_nt(grad_att, v_ref[p, keys, lanes]))
            mixed = (mix_ref[h, 0] * probs[0] + mix_ref[h, 1] * probs[1]).astype(jnp.bfloat16)
            valueg_ref[keys, lanes] += dot_tn(mixed, grad_att)
        for h in range(GROUP):
            for d in range(GROUP):
                product = fold_rows(probs[d] * mixed_grads[h])
                total = product[:, :LANES]
                for m in range(1, count):
                    total = total + product[:, m * LANES : (m + 1) * LANES]
                mixg_ref[h * GROUP + d] += total
        for d in range(GROUP):
            grad_probs = mix_ref[0, d] * mixed_grads[0] + mix_ref[1, d] * mixed_grads[1]
            delta = jnp.sum(probs[d] * grad_probs, axis=-1, keepdims=True)
            grad_logits = probs[d] * (grad_probs - delta)
            for m in range(count):
                grad_ref[d, first + m, rows, :] = grad_logits[:, m * LANES : (m + 1) * LANES]
    ready()
    for h in range(GROUP):
        lanes = slice(h * LANES, (h + 1) * LANES)
        for n in range(blocks):
            first, last = max(0, n - reach), min(n + 1, blocks - 1)
            rows = slice(n * BLOCK, (n + 1) * BLOCK)
            room = stop_ref[p, rows, :] - (iota((BLOCK, LANES), 0) + n * BLOCK)
            count = n + 2 - first
            sums = [None] * (count + 1)
            for m in range(first, last + 1):
                pieces = []
                for a in range(CQ):
                    piece = grad_ref[h, m, n * BLOCK + a : (n + 1) * BLOCK + a, :]
                    if a:
                        piece = jnp.where(room > a, piece, 0.0)
                    pieces.append(piece.astype(jnp.bfloat16))
                high = jnp.concatenate(pieces, axis=1)
                part = dot_nt(high, th_ref[h])
                for side in range(2):
                    place = m - first + side
                    value = part[:, side * LANES : (side + 1) * LANES]
                    sums[place] = value if sums[place] is None else sums[place] + value
                scores = high_ref[
                    p, h, RIM + n * BLOCK : RIM + (n + 1) * BLOCK, m * LANES : (m + 2) * LANES
                ]
                if m <= n:
                    cross_ref[h] += dot_tn(scores, high)
                else:
                    cross_ref[h, :LANES, :] += dot_tn(scores[:, :LANES], high)
            total = jnp.concatenate(sums[:count], axis=1)
            keep = allowed_mask(start_ref[p, rows, :], n, first * BLOCK - key_rim, count)
            grad_scores = jnp.where(keep, total, 0.0).astype(jnp.bfloat16)
            cols = slice(first * BLOCK, (first + count) * BLOCK)
            dqkv_ref[p, rows, lanes] = (
                dot_plain(grad_scores, k_ref[p, cols, lanes]) * scaling
            ).astype(jnp.bfloat16)
            keyg_ref[h, cols, :] += dot_tn(grad_scores, q_ref[p, rows, lanes])
        key_lanes = slice(all_lanes + h * LANES, all_lanes + (h + 1) * LANES)
        dqkv_ref[p, :, key_lanes] = (
            keyg_ref[h, key_rim : key_rim + blocks * BLOCK, :] * scaling
        ).astype(jnp.bfloat16)
    dqkv_ref[p, :, 2 * all_lanes :] = valueg_ref[...].astype(jnp.bfloat16)


def backward_kernel(
    blocks, reach, at_ref, mix_ref, b0, b1, b2, b3, b4, b5, b6, b7, out_w_ref, gain_ref,
    att_from, v_from, probs_from, start_from, stop_from, th_from, high_from, k_from, q_from,
    near_ref, far_ref, taps_ref, mixg_ref, gaing_ref,
    att_ref, v_ref, probs_ref, start_ref, stop_ref, th_ref, high_ref, k_ref, q_ref, sems,
    gg_ref, abs_ref, grad_ref, cross_ref, keyg_ref, valueg_ref,
):
    plane = at_ref[0]
    sources = (
        att_from, v_from, probs_from, start_from, stop_from, th_from, high_from, k_from, q_from
    )
    targets = (
        att_ref, v_ref, probs_ref, start_ref, stop_ref, th_ref, high_ref, k_ref, q_ref
    )
    wait = started(sources, targets, sems)
    pieces = (b0, b1, b2, b3, b4, b5, b6, b7)
    for slots in (range(4), range(4, 8)):
        branch = jnp.concatenate([pieces[slot][...] for slot in slots], axis=0)
        part = dot_nt(branch, out_w_ref[...])
        for i, slot in enumerate(slots):
            pack, row = slot_place(plane, slot)
            gg_ref[pack, pl.ds(row, BLOCK), :] = part[i * BLOCK : (i + 1) * BLOCK]
    cross_ref[...] = jnp.zeros_like(cross_ref)
    mixg_ref[...] = jnp.zeros_like(mixg_ref)
    gaing_ref[...] = jnp.zeros_like(gaing_ref)
    wait(0, 3)

    for p in range(2):
        backward_pack(
            p, blocks, reach, mix_ref, gg_ref, att_ref, gain_ref, q_ref, k_ref, v_ref,
            start_ref, stop_ref, probs_ref, high_ref, th_ref,
            abs_ref, mixg_ref, gaing_ref, grad_ref, cross_ref, keyg_ref, valueg_ref,
            (lambda: wait(3, 9)) if p == 0 else lambda: None,
        )
    for slot in range(8):
        pack, row = slot_place(plane, slot)
        into = near_ref if slot < 4 else far_ref
        into[slot % 4 * BLOCK : (slot % 4 + 1) * BLOCK, :] = abs_ref[pack, pl.ds(row, BLOCK), :]
    height = LANES + 2 * 8
    shift = iota((height, CQ * LANES), 1) % LANES - iota((height, CQ * LANES), 0) + (CK - 1)
    for h in range(GROUP):
        cross = cross_ref[h, :height, :]
        taps_ref[h] = jnp.zeros(taps_ref.shape[1:], jnp.float32)
        for b in range(CK):
            taps_ref[h, b : b + 1, :] = jnp.sum(
                jnp.where(shift == b, cross, 0.0), axis=0, keepdims=True
            )


def out_rows_kernel(slab, w_ref, out_ref):
    width = out_ref.shape[1]
    base = w_ref.shape[1] - width // LANES * slab
    fill = jnp.zeros((LANES - HEAD_DIM, width), jnp.bfloat16)
    for k in range(w_ref.shape[0]):
        row = k // 2 * LANES + k % 2 * slab
        for t in range(width // LANES):
            out_ref[row : row + slab, t * LANES : (t + 1) * LANES] = w_ref[
                k, base + t * slab : base + (t + 1) * slab, :
            ]
    for h in range(GROUP):
        out_ref[h * LANES + HEAD_DIM : (h + 1) * LANES, :] = fill


def weight_grads_kernel(
    slab, near_ref, far_ref, b0, b1, b2, b3, b4, b5, b6, b7,
    group_near_from, group_far_from, spread_from, rest_from, normed_from, all_ref,
    group_near, group_far, spread_ref, rest_ref, normed_ref, sems,
):
    wait = started(
        (group_near_from, group_far_from, spread_from, rest_from, normed_from),
        (group_near, group_far, spread_ref, rest_ref, normed_ref),
        sems,
    )
    pieces = (b0, b1, b2, b3, b4, b5, b6, b7)
    near = jnp.concatenate([ref[...] for ref in pieces[:4]], axis=0)
    wait(0, 2)
    grad = dot_tn(group_near[...], near)
    far = jnp.concatenate([ref[...] for ref in pieces[4:]], axis=0)
    grad = (grad + dot_tn(group_far[...], far)).astype(jnp.bfloat16)
    base = all_ref.shape[1] - grad.shape[1] // LANES * slab
    for k in range(all_ref.shape[0]):
        row = k // 2 * LANES + k % 2 * slab
        for t in range(grad.shape[1] // LANES):
            all_ref[k, base + t * slab : base + (t + 1) * slab, :] = grad[
                row : row + slab, t * LANES : (t + 1) * LANES
            ]
    block = base // 8
    wait(2, 5)
    half = slab // 2
    span = normed_ref.shape[1] // 4
    for s in range(4):
        rows = near_ref.shape[0]
        cols = slice(s * span, (s + 1) * span)
        table = (
            dot_tn(normed_ref[:rows, cols], near_ref[...])
            + dot_tn(normed_ref[rows:, cols], far_ref[...])
        ).astype(jnp.bfloat16)
        main = dot_nt(table, spread_ref[...])
        early = dot_nt(table, rest_ref[0])
        late = dot_nt(table, rest_ref[1])
        for zz in range(4):
            for y in range(2):
                g = 2 * s + y
                row = (zz * 2 + y) * slab
                for t in range(4):
                    at = g * block + t * slab
                    all_ref[zz, at : at + slab, :] = main[
                        row : row + slab, t * LANES : (t + 1) * LANES
                    ].astype(jnp.bfloat16)
                rest = early[row : row + half] + late[row + half : row + slab]
                all_ref[zz, g * block + 4 * slab : (g + 1) * block, :] = jnp.concatenate(
                    [rest, jnp.zeros((8, LANES), jnp.float32)], axis=0
                ).astype(jnp.bfloat16)


def assemble_kernel(sub, w_ref, gu_ref, down_ref):
    deep = w_ref.shape[3]
    units = w_ref.shape[0] * sub
    parts = deep // LANES
    for zz in range(w_ref.shape[0]):
        for s in range(w_ref.shape[1]):
            for m in range(2):
                at = m * units + zz * sub
                gu_ref[s * deep : (s + 1) * deep, at : at + sub] = w_ref[zz, s, m]
            for c in range(parts):
                at = (s * parts + c) * LANES
                down_ref[zz * sub : (zz + 1) * sub, at : at + LANES] = w_ref[
                    zz, s, 2, c * sub : (c + 1) * sub, :
                ]


def hidden_kernel(
    x0, x1, x2, x3, x4, x5, x6, x7, c0, c1, c2, c3, c4, c5, c6, c7, gu_ref, down_ref,
    hidden_near, hidden_far, grad_near, grad_far,
):
    units = down_ref.shape[0]
    xs = (x0, x1, x2, x3, x4, x5, x6, x7)
    cs = (c0, c1, c2, c3, c4, c5, c6, c7)
    for part in (2, 3, 0, 1):
        pair = (2 * part, 2 * part + 1)
        value = jnp.concatenate([xs[i][...] for i in pair], axis=0)
        gate_up = dot_plain(value, gu_ref[...])
        gate, up = gate_up[:, :units], gate_up[:, units:]
        cot = jnp.concatenate([cs[i][...] for i in pair], axis=0)
        grad_hidden = dot_nt(cot, down_ref[...])
        sig = 1.0 / (1.0 + jnp.exp(-gate))
        silu = gate * sig
        hidden_ref, grad_ref = (hidden_near, grad_near) if part < 2 else (hidden_far, grad_far)
        rows = slice(part % 2 * 2 * BLOCK, (part % 2 + 1) * 2 * BLOCK)
        hidden_ref[rows, :] = (silu * up).astype(jnp.bfloat16)
        grad_ref[rows, :units] = (
            grad_hidden * up * sig * (1.0 + gate * (1.0 - sig))
        ).astype(jnp.bfloat16)
        grad_ref[rows, units:] = (grad_hidden * silu).astype(jnp.bfloat16)


def hidden_grad_kernel(
    sub, hidden_near, hidden_far, grad_near, grad_far,
    x0, x1, x2, x3, x4, x5, x6, x7, c0, c1, c2, c3, c4, c5, c6, c7, out_ref, x_ref, c_ref, sems,
):
    deep = out_ref.shape[3]
    depth = out_ref.shape[0]
    units = depth * sub
    rows = [slice(slot * BLOCK, (slot + 1) * BLOCK) for slot in range(8)]
    wait = started(
        (x0, x1, x2, x3, x4, x5, x6, x7, c0, c1, c2, c3, c4, c5, c6, c7),
        [x_ref.at[part, :] for part in rows] + [c_ref.at[part, :] for part in rows],
        sems,
    )
    half = 4 * BLOCK
    wait(0, 8)
    for s in range(out_ref.shape[1]):
        cols = slice(s * deep, (s + 1) * deep)
        table = (
            dot_tn(x_ref[:half, cols], grad_near[...]) + dot_tn(x_ref[half:, cols], grad_far[...])
        ).astype(jnp.bfloat16)
        for zz in range(depth):
            for m in range(2):
                at = m * units + zz * sub
                out_ref[zz, s, m] = table[:, at : at + sub]
    wait(8, 16)
    for s in range(out_ref.shape[1]):
        cols = slice(s * deep, (s + 1) * deep)
        down = (
            dot_tn(hidden_near[...], c_ref[:half, cols])
            + dot_tn(hidden_far[...], c_ref[half:, cols])
        ).astype(jnp.bfloat16)
        for zz in range(depth):
            for c in range(deep // LANES):
                out_ref[zz, s, 2, c * sub : (c + 1) * sub, :] = down[
                    zz * sub : (zz + 1) * sub, c * LANES : (c + 1) * LANES
                ]


def pack_hidden_kernel(sub, gate_ref, up_ref, down_ref, out_ref):
    deep = gate_ref.shape[0]
    for s in range(out_ref.shape[0]):
        for m, ref in enumerate((gate_ref, up_ref)):
            out_ref[s, m] = ref[:, s * sub : (s + 1) * sub].astype(jnp.bfloat16)
        for c in range(deep // LANES):
            out_ref[s, 2, c * sub : (c + 1) * sub, :] = down_ref[
                s * sub : (s + 1) * sub, c * LANES : (c + 1) * LANES
            ].astype(jnp.bfloat16)


def unpack_hidden_kernel(sub, in_ref, gate_ref, up_ref, down_ref):
    deep = gate_ref.shape[0]
    for s in range(in_ref.shape[0]):
        for m, ref in enumerate((gate_ref, up_ref)):
            ref[:, s * sub : (s + 1) * sub] = in_ref[s, m].astype(jnp.float32)
        for c in range(deep // LANES):
            down_ref[s * sub : (s + 1) * sub, c * LANES : (c + 1) * LANES] = in_ref[
                s, 2, c * sub : (c + 1) * sub, :
            ].astype(jnp.float32)


def total_of(refs):
    total = refs[0][...]
    for ref in refs[1:]:
        total = total + ref[...].astype(jnp.float32)
    return total


def middle_kernel(s0, s1, s2, s3, token_ref, gains_ref, middle_ref, in_ref):
    middle = token_ref[...].astype(jnp.float32) + total_of((s0, s1, s2, s3))
    middle_ref[...] = middle
    scale = lax.rsqrt(jnp.mean(middle * middle, axis=-1, keepdims=True) + epsilon)
    in_ref[...] = (middle * scale * gains_ref[2:3, :]).astype(jnp.bfloat16)


def norm_back(row, grad, value, gains_ref, first):
    scale = lax.rsqrt(jnp.mean(value * value, axis=-1, keepdims=True) + epsilon)
    scaled = grad * gains_ref[row : row + 1, :]
    mean = jnp.mean(scaled * value, axis=-1, keepdims=True)
    return first + (scale * scaled - value * (scale * scale * scale) * mean)


def middle_back_kernel(
    s0, s1, s2, s3, middle_ref, cot_ref, gains_ref, grad_ref, branch_ref, gain_ref
):
    value = middle_ref[...]
    total = total_of((s0, s1, s2, s3))
    grad = norm_back(2, total, value, gains_ref, cot_ref[...].astype(jnp.float32))
    grad_ref[...] = grad
    branch_ref[...] = grad.astype(jnp.bfloat16)
    scale = lax.rsqrt(jnp.mean(value * value, axis=-1, keepdims=True) + epsilon)
    gain_ref[...] = fold_rows(total * value * scale)


def input_back_kernel(s0, s1, s2, s3, token_ref, middle_ref, gains_ref, grad_ref):
    token = token_ref[...].astype(jnp.float32)
    grad_ref[...] = norm_back(
        0, total_of((s0, s1, s2, s3)), token, gains_ref, middle_ref[...]
    ).astype(jnp.bfloat16)


def output_kernel(s0, s1, s2, s3, middle_ref, out_ref):
    out_ref[...] = (middle_ref[...] + total_of((s0, s1, s2, s3))).astype(jnp.bfloat16)


def conv_tables(kernel):
    heads = kernel.shape[0]
    u = iota((2 * LANES, CQ * LANES), 0)
    j = iota((2 * LANES, CQ * LANES), 1) % LANES
    table = jnp.zeros((heads, 2 * LANES, CQ * LANES), jnp.float32)
    for b in range(CK):
        taps = jnp.repeat(kernel[:, :, b], LANES, axis=1)
        table = jnp.where((j - u + CK - 1 == b)[None], taps[:, None, :], table)
    return halves(table)


FLAT = ("seq", "wide")


def swapped(value, flip):
    total = lax.axis_size("seq") * lax.axis_size("wide")
    return lax.ppermute(value, FLAT, [(i, i ^ flip) for i in range(total)])


class Place:
    def __init__(self):
        self.wide_count = lax.axis_size("wide")
        self.depth = self.wide_count // 2
        self.seq = lax.axis_index("seq")
        wide = lax.axis_index("wide")
        self.y = wide % 2
        self.z = wide // 2
        self.plane = 2 * self.seq + self.y
        self.x_flip = 2 * self.wide_count
        self.core_flip = self.wide_count
        self.y_flip = 1
        self.chip_flips = (self.x_flip, self.y_flip, self.x_flip | self.y_flip)
        seqs = range(lax.axis_size("seq"))
        self.plane_groups = [
            [s * self.wide_count + z * 2 + y for s in seqs for y in range(2)] for z in range(self.depth)
        ]
        self.line_groups = [[z * 2 + y for z in range(self.depth)] for y in range(2)]


def chip_gather(place, value):
    return [value] + [swapped(value, flip) for flip in place.chip_flips]


def core_gather(place, near):
    return near + [swapped(part, place.core_flip) for part in near]


def plane_gather(place, value):
    return core_gather(place, chip_gather(place, value))


def plane_terms(place, near, far, weight, other, transposed, name, tokens=None, got=None):
    width = weight.shape[0] if transposed else weight.shape[1]
    flat = (BLOCK, width)
    if got is None:
        got = swapped(far, place.core_flip)
    return list(
        kernel_call(
            functools.partial(pair_kernel, transposed) if tokens is None else pair_gain_kernel,
            name,
            [shape_of(flat, jnp.float32)]
            + [shape_of(flat)] * 3
            + ([] if tokens is None else [shape_of((8, width), jnp.float32)]),
            (near, got, weight, other) + (tokens or ()),
            flops=16 * BLOCK * weight.size,
            vmem=24,
            lazy=2 + len(tokens or ()),
        )
    )


def chip_scatter(place, terms):
    return [terms[0]] + [
        swapped(part, flip) for part, flip in zip(terms[1:], place.chip_flips)
    ]


def line_gather(place, value):
    return lax.all_gather(value, "wide", axis=0, axis_index_groups=place.line_groups)


def line_scatter(place, blocks):
    return lax.psum_scatter(
        blocks, "wide", scatter_dimension=0, axis_index_groups=place.line_groups
    )


def plane_exchange(place, blocks):
    return lax.all_to_all(blocks, FLAT, 0, 0, axis_index_groups=place.plane_groups)


def out_pairs(place):
    return [
        (s * place.wide_count + 4 * y + z, s * place.wide_count + 2 * z + y)
        for s in range(lax.axis_size("seq"))
        for z in range(place.depth)
        for y in range(2)
    ]


def spread_tables():
    target = iota((4 * LANES, 3 * GROUP * LANES), 1)
    column = target // LANES * HEAD_DIM + target % LANES
    real = target % LANES < HEAD_DIM
    source = iota(target.shape, 0)
    main = jnp.where(real & (column == source), 1.0, 0.0).astype(jnp.bfloat16)
    source, column, real = source[:LANES], column[:LANES], real[:LANES]
    rest = [
        jnp.where(
            real & (column >= 4 * LANES) & (column - 4 * LANES + side * (LANES // 2) == source), 1.0, 0.0
        ).astype(jnp.bfloat16)
        for side in range(2)
    ]
    return main, jnp.stack(rest)


def after(done, *values):
    return lax.optimization_barrier((done,) + values)[1:]


def plane_shards(
    tokens, segments, w_query, w_key, w_value, w_out, gain_attn, gain_group, gain_ffn,
    conv_kernel, head_mix, w_gate, w_up, w_down, cotangent,
):
    place = Place()
    seq_count = lax.axis_size("seq")
    depth = place.depth
    count = tokens.shape[1]
    length = count * seq_count
    width = tokens.shape[2]
    slab = w_query.shape[0]
    blocks = length // BLOCK
    reach = (length // 2 - 1) // BLOCK + 1
    lanes = GROUP * LANES
    cols = GROUP * HEAD_DIM
    bf16 = jnp.bfloat16
    f32 = jnp.float32
    at = jnp.stack([place.plane, place.z, place.y]).astype(jnp.int32)
    own_tokens = tokens[0]
    own_cot = cotangent[0]

    gains_own = jnp.stack([gain_attn, gain_group, gain_ffn]).astype(bf16)
    gains_own = jnp.pad(gains_own, ((0, 5), (0, LANES - slab)))
    pack_rows = 4 * slab + slab // 2 + 8
    out_rows = width // LANES * slab
    packed, w_out_rows = kernel_call(
        functools.partial(pack_kernel, slab),
        "pack_projections",
        [shape_of((8, pack_rows, LANES)), shape_of((out_rows, LANES))],
        (w_query, w_key, w_value, gains_own, w_out),
        vmem=16,
    )
    sub = w_gate.shape[1] // seq_count
    deep = w_gate.shape[0]
    packed, own_tokens, w_out_rows, segments, conv_kernel, w_gate, w_up, w_down = (
        lax.optimization_barrier(
            (packed, own_tokens, w_out_rows, segments, conv_kernel, w_gate, w_up, w_down)
        )
    )
    w_out_rows = lax.ppermute(w_out_rows, FLAT, out_pairs(place))
    packed = plane_exchange(place, packed)
    (ffn_own,) = kernel_call(
        functools.partial(pack_hidden_kernel, sub),
        "pack_hidden",
        [shape_of((seq_count, 3, deep, sub))],
        (w_gate, w_up, w_down),
        vmem=16,
    )
    token_near = chip_gather(place, own_tokens)
    packed, ffn_own, own_cot = lax.optimization_barrier((packed, ffn_own, own_cot))
    w_all = line_gather(
        place, jnp.concatenate([packed.reshape(8 * pack_rows, LANES), w_out_rows])
    )
    ffn_own = lax.all_to_all(ffn_own, "seq", 0, 0)
    cot_near = chip_gather(place, own_cot)
    token_parts = core_gather(place, token_near)

    other_row = swapped(segments, place.y_flip)
    seg = jnp.where(
        place.y == 0,
        jnp.concatenate([segments, other_row]),
        jnp.concatenate([other_row, segments]),
    )
    starts = jnp.sum(seg[:, None, :] < seg[:, :, None], axis=-1, dtype=jnp.int32)
    stops = jnp.sum(seg[:, None, :] <= seg[:, :, None], axis=-1, dtype=jnp.int32)
    starts = jnp.broadcast_to(starts[:, :, None], (2, length, LANES))
    stops = jnp.broadcast_to(stops[:, :, None], (2, length, LANES))
    taps = lax.dynamic_slice_in_dim(conv_kernel, place.plane * GROUP, GROUP)
    mix = lax.dynamic_slice_in_dim(head_mix, place.plane * GROUP, GROUP)
    table_high, table_low = conv_tables(taps)
    spread_main, spread_rest = spread_tables()

    ffn_w = line_gather(place, ffn_own)
    units = depth * sub
    w_all, starts, stops, *cot_near = lax.optimization_barrier(
        (w_all, starts, stops, *cot_near)
    )
    (w_out_heads,) = kernel_call(
        functools.partial(out_rows_kernel, slab),
        "out_rows",
        [shape_of((lanes, width))],
        (w_all,),
        vmem=16,
    )
    w_out_other = swapped(w_out_heads, place.core_flip)
    cot_parts = core_gather(place, cot_near)

    padded = length + LANES
    half = 4 * count
    (
        normed, w_wide, queries, keys, values, probs, high, attended, grouped_near, grouped_far,
        gains, gain_heads,
    ) = kernel_call(
        functools.partial(forward_kernel, blocks, reach, slab),
        "attention_forward",
        [
            shape_of((8 * count, width)),
            shape_of((width, 3 * lanes)),
            shape_of((2, length, lanes)),
            shape_of((2, padded, lanes)),
            shape_of((2, length, lanes)),
            shape_of((2, GROUP, length, (reach + 1) * LANES), f32),
            shape_of((2, GROUP, RIM + length, padded)),
            shape_of((2, length, lanes), f32),
            shape_of((half, lanes)),
            shape_of((half, lanes)),
            shape_of((8, width), f32),
            shape_of((1, lanes), f32),
        ],
        (
            at, mix, w_all, *token_parts, starts, table_high, table_low, spread_main, spread_rest,
        ),
        [
            pltpu.VMEM((2, length, lanes), bf16),
            pltpu.VMEM((2, length, lanes), f32),
            pltpu.VMEM((GROUP, RIM + length, padded), bf16),
            pltpu.VMEM((CQ, RIM + BLOCK, LANES), f32),
        ],
        flops=25 * 10**9,
        smem=2,
    )
    w_wide_other = swapped(w_wide, place.core_flip)
    grouped_near, *cot_parts[4:] = lax.optimization_barrier((grouped_near, *cot_parts[4:]))
    terms = chip_scatter(
        place,
        plane_terms(place, grouped_near, grouped_far, w_out_heads, w_out_other, False, "branch"),
    )
    flat = (count, width)
    middle, ffn_in = kernel_call(
        middle_kernel,
        "middle",
        [shape_of(flat, f32), shape_of(flat)],
        (*terms, own_tokens, gains),
        vmem=16,
    )

    ffn_parts = plane_gather(place, ffn_in)
    ffn_w, *ffn_parts[1:4] = lax.optimization_barrier((ffn_w, *ffn_parts[1:4]))
    w_gate_up, w_down_all = kernel_call(
        functools.partial(assemble_kernel, sub),
        "assemble_feed_forward",
        [shape_of((width, 2 * units)), shape_of((units, width))],
        (ffn_w,),
        vmem=24,
    )
    *ffn_parts[4:], w_gate_up, w_down_all = lax.optimization_barrier(
        (*ffn_parts[4:], w_gate_up, w_down_all)
    )
    gate_up_other = swapped(w_gate_up, place.core_flip)
    down_other = swapped(w_down_all, place.core_flip)
    hidden_near, hidden_far, grad_near, grad_far = kernel_call(
        hidden_kernel,
        "feed_forward",
        [
            shape_of((half, units)),
            shape_of((half, units)),
            shape_of((half, 2 * units)),
            shape_of((half, 2 * units)),
        ],
        (*ffn_parts, *cot_parts, w_gate_up, w_down_all),
        flops=10 * 10**9,
        vmem=26,
    )
    grad_got = swapped(grad_far, place.core_flip)
    grad_got, gate_up_other, hidden_near, hidden_far, grad_near, grad_far = (
        lax.optimization_barrier(
            (grad_got, gate_up_other, hidden_near, hidden_far, grad_near, grad_far)
        )
    )
    (ffn_g,) = kernel_call(
        functools.partial(hidden_grad_kernel, sub),
        "feed_forward_weights",
        [shape_of((depth, seq_count, 3, deep, sub))],
        (hidden_near, hidden_far, grad_near, grad_far, *ffn_parts, *cot_parts),
        [
            pltpu.VMEM((8 * count, width), bf16),
            pltpu.VMEM((8 * count, width), bf16),
            pltpu.SemaphoreType.DMA((16,)),
        ],
        hbm=16,
        flops=5 * 10**9,
        vmem=26,
    )
    ffn_g, grad_near = lax.optimization_barrier((ffn_g, grad_near))
    ffn_g = line_scatter(place, ffn_g)
    terms = plane_terms(
        place, grad_near, grad_far, w_gate_up, gate_up_other, True, "feed_forward_back",
        got=grad_got,
    )
    terms[0], hidden_near = lax.optimization_barrier((terms[0], hidden_near))
    terms = chip_scatter(place, terms)
    grad_middle, grad_branch, gain_ffn_sum = kernel_call(
        middle_back_kernel,
        "middle_back",
        [shape_of(flat, f32), shape_of(flat), shape_of((8, width), f32)],
        (*terms, middle, own_cot, gains),
        vmem=16,
    )
    ffn_g = lax.all_to_all(ffn_g, "seq", 0, 0)

    out_terms = plane_terms(
        place, hidden_near, hidden_far, w_down_all, down_other, False, "feed_forward_out"
    )
    out_terms[0], grad_branch = lax.optimization_barrier((out_terms[0], grad_branch))
    branch_parts = plane_gather(place, grad_branch)
    branch_parts[3], *out_terms = lax.optimization_barrier((branch_parts[3], *out_terms))
    out_terms = chip_scatter(place, out_terms)
    dqkv_near, dqkv_far, grad_taps, grad_mix, grad_gain_group = kernel_call(
        functools.partial(backward_kernel, blocks, reach),
        "attention_backward",
        [
            shape_of((half, 3 * lanes)),
            shape_of((half, 3 * lanes)),
            shape_of((GROUP, 16, CQ * LANES), f32),
            shape_of((GROUP * GROUP, 8, LANES), f32),
            shape_of((8, lanes), f32),
        ],
        (
            at, mix, *branch_parts, w_out_heads, gain_heads,
            attended, values, probs, starts, stops, table_high, high, keys, queries,
        ),
        [
            pltpu.VMEM((2, length, lanes), f32),
            pltpu.VMEM((2, length, 3 * lanes), bf16),
            pltpu.VMEM((GROUP, blocks, length + 8, LANES), f32),
            pltpu.VMEM((GROUP, 2 * LANES, CQ * LANES), f32),
            pltpu.VMEM((GROUP, padded, LANES), f32),
            pltpu.VMEM((length, lanes), f32),
        ],
        flops=30 * 10**9,
        smem=2,
        vmem=34,
        lazy=9,
    )
    dqkv_near, dqkv_far, *out_terms = lax.optimization_barrier(
        (dqkv_near, dqkv_far, *out_terms)
    )
    (table,) = kernel_call(
        functools.partial(weight_grads_kernel, slab),
        "attention_weights",
        [shape_of((depth, 8 * pack_rows + out_rows, LANES))],
        (
            dqkv_near, dqkv_far, *branch_parts,
            grouped_near, grouped_far, spread_main, spread_rest, normed,
        ),
        flops=5 * 10**9,
        vmem=36,
        lazy=5,
    )
    table, dqkv_near = lax.optimization_barrier((table, dqkv_near))
    table = line_scatter(place, table)
    *terms, gain_attn_sum = plane_terms(
        place, dqkv_near, dqkv_far, w_wide, w_wide_other, True, "project_back",
        tuple(token_parts[:4]),
    )
    (small,) = kernel_call(
        small_kernel,
        "small_sums",
        [shape_of((2 * (width // LANES) + 2 * HEADS, LANES), f32)],
        (at, gain_attn_sum, gain_ffn_sum, grad_taps, grad_mix, grad_gain_group),
        smem=1,
        vmem=16,
    )
    terms = chip_scatter(place, terms)
    for flip in (place.core_flip, 2, 4, place.y_flip, place.x_flip):
        small = small + swapped(small, flip)
    (grad_tokens,) = kernel_call(
        input_back_kernel,
        "input_back",
        [shape_of(flat)],
        (*terms, own_tokens, grad_middle, gains),
        vmem=16,
    )
    (output,) = kernel_call(
        output_kernel, "output", [shape_of(flat)], (*out_terms, middle), vmem=16
    )
    grad_w_gate, grad_w_up, grad_w_down = kernel_call(
        functools.partial(unpack_hidden_kernel, sub),
        "unpack_hidden",
        [
            shape_of((deep, seq_count * sub), f32),
            shape_of((deep, seq_count * sub), f32),
            shape_of((seq_count * sub, deep), f32),
        ],
        (ffn_g,),
        vmem=16,
    )
    output, grad_w_gate, grad_tokens, small, table = lax.optimization_barrier(
        (output, grad_w_gate, grad_tokens, small, table)
    )
    back = [(target, source) for source, target in out_pairs(place)]
    out_table = lax.ppermute(table[8 * pack_rows :], FLAT, back)
    table = plane_exchange(place, table[: 8 * pack_rows].reshape(8, pack_rows, LANES))
    grad_rows = kernel_call(
        functools.partial(unpack_kernel, slab),
        "unpack_projections",
        [shape_of((slab, width), f32)] * 4,
        (table, out_table),
        vmem=16,
    )
    small_flat = small.reshape(-1)
    row = (place.seq * place.wide_count + lax.axis_index("wide")) * slab
    tiles = width // LANES
    gain_grads = [lax.dynamic_slice_in_dim(small_flat, i * width + row, slab) for i in range(2)]
    head, side = row // HEAD_DIM, row % HEAD_DIM
    gain_grads.append(
        lax.dynamic_slice_in_dim(small_flat, (2 * tiles + head) * LANES + side, slab)
    )
    heads = small[2 * tiles + HEADS :]
    grad_conv = heads[:, : 16 * CQ].reshape(HEADS, CQ, 16)[:, :, :CK]
    grad_head_mix = heads[:, 16 * CQ : 16 * CQ + GROUP]
    return (
        output[None],
        grad_tokens[None],
        grad_rows[0],
        grad_rows[1],
        grad_rows[2],
        grad_rows[3],
        gain_grads[0],
        gain_grads[2],
        gain_grads[1],
        grad_conv,
        grad_head_mix,
        grad_w_gate,
        grad_w_up,
        grad_w_down,
    )


def solution(mesh):
    planes = mesh.shape["seq"] == 4 and mesh.shape["wide"] == 8
    return jax.shard_map(
        plane_shards if planes else shards,
        mesh=mesh,
        in_specs=(
            P("wide", "seq", None),
            P("wide", None),
            P(("seq", "wide"), None),
            P(("seq", "wide"), None),
            P(("seq", "wide"), None),
            P(("seq", "wide"), None),
            P(("seq", "wide")),
            P(("seq", "wide")),
            P(("seq", "wide")),
            P(),
            P(),
            P("seq", "wide"),
            P("seq", "wide"),
            P("wide", "seq"),
            P("wide", "seq", None),
        ),
        out_specs=(
            P("wide", "seq", None),
            P("wide", "seq", None),
            P(("seq", "wide"), None),
            P(("seq", "wide"), None),
            P(("seq", "wide"), None),
            P(("seq", "wide"), None),
            P(("seq", "wide")),
            P(("seq", "wide")),
            P(("seq", "wide")),
            P(),
            P(),
            P("seq", "wide"),
            P("seq", "wide"),
            P("wide", "seq"),
        ),
        check_vma=False,
    )
```

```python
import functools

import jax
import jax.numpy as jnp
from jax import lax
from jax.experimental import pallas as pl
from jax.experimental.pallas import tpu as pltpu
from jax.sharding import PartitionSpec as P

HEADS = 16
HEAD_DIM = 96
CQ = 6
CK = 11
GROUP = 2
LANES = 128
BLOCK = 128
RIM = 16


precise = lax.Precision.HIGHEST
epsilon = 1e-05


def passed_along(value, axis, by):
    devices = lax.axis_size(axis)
    pairs = [(i, i + by) for i in range(devices) if 0 <= i + by < devices]
    return lax.ppermute(value, axis, pairs)


def extended(block, sides, width):
    for axis, dim in sides:
        count = lax.axis_size(axis)
        forward = [(i, i + 1) for i in range(count - 1)]
        backward = [(target, source) for source, target in forward]
        low = lax.ppermute(
            lax.slice_in_dim(block, block.shape[dim] - width, None, axis=dim), axis, forward
        )
        high = lax.ppermute(lax.slice_in_dim(block, 0, width, axis=dim), axis, backward)
        block = jnp.concatenate([low, block, high], axis=dim)
    return block


def rms_scaled(values, gain_vec):
    return (
        values * lax.rsqrt(jnp.mean(values * values, axis=-1, keepdims=True) + epsilon) * gain_vec
    )


def group_scaled(values, gain_vec):
    center = values - jnp.mean(values, axis=-1, keepdims=True)
    spread = jnp.mean(center * center, axis=-1, keepdims=True)
    return center * lax.rsqrt(spread + epsilon) * gain_vec


def tile_masks(seg_query, pos_query, seg_key, pos_key, valid_flag):
    query_rim = CQ - 1
    key_rim = CK // 2
    allowed = (
        (seg_query[:, None] == seg_key[None, :])
        & (pos_key[None, :] <= pos_query[:, None])
        & valid_flag
    )
    row_count = seg_query.shape[0] - query_rim
    row_masks = jnp.stack(
        [
            (
                seg_query[query_rim - shift_q : query_rim - shift_q + row_count]
                == seg_query[query_rim:]
            ).astype(jnp.float32)
            for shift_q in range(CQ)
        ]
    )
    final_mask = allowed[query_rim:, key_rim : key_rim + row_count]
    return (allowed, row_masks, final_mask)


def convolve(scores, allowed, row_masks, kernel):
    query_rim = CQ - 1
    key_rim = CK // 2
    row_count = scores.shape[1] - query_rim
    col_count = scores.shape[2] - 2 * key_rim
    masked = jnp.where(allowed[None], scores, 0.0)
    summed = jnp.zeros((scores.shape[0], row_count, col_count), jnp.float32)
    for shift_q in range(CQ):
        inner_sum = jnp.zeros((scores.shape[0], row_count, col_count), jnp.float32)
        for shift_k in range(CK):
            piece_view = masked[
                :,
                query_rim - shift_q : query_rim - shift_q + row_count,
                2 * key_rim - shift_k : 2 * key_rim - shift_k + col_count,
            ]
            inner_sum = inner_sum + kernel[:, shift_q, shift_k][:, None, None] * piece_view
        summed = summed + row_masks[shift_q][None, :, None] * inner_sum
    return summed


def mix_heads(probs, head_mix):
    lead_dims = probs.shape[:-3]
    tail_dims = probs.shape[-2:]
    grouped = probs.reshape(lead_dims + (HEADS // GROUP, GROUP) + tail_dims)
    mixing = head_mix.reshape(HEADS // GROUP, GROUP, GROUP)
    summed = jnp.zeros(lead_dims + (HEADS // GROUP, GROUP) + tail_dims, jnp.float32)
    for source in range(GROUP):
        summed = summed + mixing[:, :, source][:, :, None, None] * jnp.expand_dims(
            grouped[..., :, source, :, :], -3
        )
    return summed.reshape(probs.shape)


def unmix_heads(grads, head_mix):
    lead_dims = grads.shape[:-3]
    tail_dims = grads.shape[-2:]
    grouped = grads.reshape(lead_dims + (HEADS // GROUP, GROUP) + tail_dims)
    mixing = head_mix.reshape(HEADS // GROUP, GROUP, GROUP)
    summed = jnp.zeros(lead_dims + (HEADS // GROUP, GROUP) + tail_dims, jnp.float32)
    for target in range(GROUP):
        summed = summed + mixing[:, target, :][:, :, None, None] * jnp.expand_dims(
            grouped[..., :, target, :, :], -3
        )
    return summed.reshape(grads.shape)


def contract(left_op, right_op, left_dim, right_dim):
    return lax.dot_general(
        left_op,
        right_op,
        (((left_dim,), (right_dim,)), ((), ())),
        preferred_element_type=jnp.float32,
    )


def gather_attention(w_query, w_key, w_value, w_out, gain_attn, gain_group, gain_ffn):
    return (
        lax.all_gather(w_query.astype(jnp.bfloat16), ("seq", "wide"), axis=0, tiled=True),
        lax.all_gather(w_key.astype(jnp.bfloat16), ("seq", "wide"), axis=0, tiled=True),
        lax.all_gather(w_value.astype(jnp.bfloat16), ("seq", "wide"), axis=0, tiled=True),
        lax.all_gather(w_out.astype(jnp.bfloat16), ("seq", "wide"), axis=0, tiled=True),
        lax.all_gather(gain_attn.astype(jnp.bfloat16), ("seq", "wide"), axis=0, tiled=True),
        lax.all_gather(gain_group.astype(jnp.bfloat16), ("seq", "wide"), axis=0, tiled=True),
        lax.all_gather(gain_ffn.astype(jnp.bfloat16), ("seq", "wide"), axis=0, tiled=True),
    )


def collect_packets(own, reach_len):
    stored = jnp.zeros((reach_len,) + own.shape, own.dtype).at[0].set(own)

    def advance(turn_index, state_pair):
        packet, stored_now = state_pair
        packet = passed_along(packet, "seq", 1)
        return (packet, lax.dynamic_update_index_in_dim(stored_now, packet, turn_index, 0))

    return lax.fori_loop(1, reach_len, advance, (own, stored))[1]


def tile_logits(query_ext, packet, seg_query, pos_query, seg_key_pad, other_shard, token_count):
    key_rim = CK // 2
    key_ext = packet[: token_count + 2 * key_rim].reshape(
        token_count + 2 * key_rim, HEADS, HEAD_DIM
    )
    scores = jnp.einsum(
        "qhe,khe->hqk", query_ext, key_ext, preferred_element_type=jnp.float32
    ) * HEAD_DIM ** (-0.5)
    key_start = other_shard * token_count
    seg_key = lax.dynamic_slice_in_dim(
        seg_key_pad, jnp.maximum(key_start, 0), token_count + 2 * key_rim
    )
    pos_key = key_start - key_rim + jnp.arange(token_count + 2 * key_rim, dtype=jnp.int32)
    allowed, row_masks, final_mask = tile_masks(
        seg_query, pos_query, seg_key, pos_key, other_shard >= 0
    )
    return (scores, allowed, row_masks, final_mask, key_ext)


def shards(
    tokens,
    segments,
    w_query,
    w_key,
    w_value,
    w_out,
    gain_attn,
    gain_group,
    gain_ffn,
    conv_kernel,
    head_mix,
    w_gate,
    w_up,
    w_down,
    cotangent,
):
    token_count = tokens.shape[1]
    query_rim = CQ - 1
    key_rim = CK // 2
    width_all = HEADS * HEAD_DIM
    scaling = HEAD_DIM ** (-0.5)
    seq_count = lax.axis_size("seq")
    longest_doc = min(1024, token_count * seq_count // 2)
    reach_len = min(seq_count - 1, (longest_doc - 1) // token_count + 1) + 1
    seq_index = lax.axis_index("seq")
    row_start = seq_index * token_count
    seg_row = segments[0]
    seg_query_pad = jnp.concatenate([jnp.full((query_rim,), -1, jnp.int32), seg_row])
    seg_key_pad = jnp.concatenate(
        [jnp.full((key_rim,), -2, jnp.int32), seg_row, jnp.full((key_rim,), -2, jnp.int32)]
    )
    seg_query = lax.dynamic_slice_in_dim(seg_query_pad, row_start, token_count + query_rim)
    pos_query = row_start - query_rim + jnp.arange(token_count + query_rim, dtype=jnp.int32)
    weights = gather_attention(w_query, w_key, w_value, w_out, gain_attn, gain_group, gain_ffn)
    query_mat, key_mat, value_mat, out_mat, gain_one, gain_mid, gain_two = weights
    inputs = tokens[0].astype(jnp.float32)
    gain_first = gain_one.astype(jnp.float32)
    normed = rms_scaled(inputs, gain_first).astype(jnp.bfloat16)
    queries = jnp.dot(normed, query_mat, preferred_element_type=jnp.float32).astype(jnp.bfloat16)
    keys_loc = jnp.dot(normed, key_mat, preferred_element_type=jnp.float32).astype(jnp.bfloat16)
    values_loc = jnp.dot(normed, value_mat, preferred_element_type=jnp.float32).astype(jnp.bfloat16)
    rimmed = extended(jnp.stack([queries, keys_loc]), (("seq", 1),), key_rim)
    query_ext = rimmed[0, : token_count + query_rim].reshape(
        token_count + query_rim, HEADS, HEAD_DIM
    )
    own = jnp.concatenate([rimmed[1], values_loc], axis=0)
    packets = collect_packets(own, reach_len)

    def all_logits(packet_stack):

        def logits_of(turn_index):
            packet = lax.dynamic_index_in_dim(packet_stack, turn_index, 0, keepdims=False)
            scores, allowed, row_masks, final_mask, key_ext = tile_logits(
                query_ext,
                packet,
                seg_query,
                pos_query,
                seg_key_pad,
                seq_index - turn_index,
                token_count,
            )
            return jnp.where(
                final_mask[None], convolve(scores, allowed, row_masks, conv_kernel), -jnp.inf
            )

        return lax.map(logits_of, jnp.arange(reach_len, dtype=jnp.int32))

    logits = all_logits(packets)
    peak_val = jnp.max(logits, axis=(0, 3))
    log_total = peak_val + jnp.log(
        jnp.sum(jnp.exp(logits - peak_val[None, :, :, None]), axis=(0, 3))
    )
    probs_all = jnp.exp(logits - log_total[None, :, :, None])
    mixed_b = mix_heads(probs_all, head_mix).astype(jnp.bfloat16)
    values_all = packets[:, token_count + 2 * key_rim :].reshape(
        reach_len, token_count, HEADS, HEAD_DIM
    )
    attended = jnp.einsum("rhtk,rkhe->the", mixed_b, values_all, preferred_element_type=jnp.float32)
    gain_middle = gain_mid.astype(jnp.float32).reshape(HEADS, HEAD_DIM)
    grouped = (
        group_scaled(attended, gain_middle).reshape(token_count, width_all).astype(jnp.bfloat16)
    )
    middle = inputs + jnp.dot(grouped, out_mat, preferred_element_type=jnp.float32)
    gain_second = gain_two.astype(jnp.float32)
    ffn_in = rms_scaled(middle, gain_second).astype(jnp.bfloat16)
    ffn_all = lax.all_gather(ffn_in, "wide", axis=0, tiled=True)
    gate_mat, up_mat, down_mat = (
        lax.all_gather(w_gate.astype(jnp.bfloat16), "seq", axis=0, tiled=True),
        lax.all_gather(w_up.astype(jnp.bfloat16), "seq", axis=0, tiled=True),
        lax.all_gather(w_down.astype(jnp.bfloat16), "seq", axis=1, tiled=True),
    )
    gate_val = jnp.dot(ffn_all, gate_mat, preferred_element_type=jnp.float32)
    up_val = jnp.dot(ffn_all, up_mat, preferred_element_type=jnp.float32)
    hidden = (jax.nn.silu(gate_val) * up_val).astype(jnp.bfloat16)
    ffn_out = lax.psum_scatter(
        jnp.dot(hidden, down_mat, preferred_element_type=jnp.float32).astype(jnp.bfloat16),
        "wide",
        scatter_dimension=0,
        tiled=True,
    ).astype(jnp.float32)
    output = (middle + ffn_out).astype(jnp.bfloat16)
    grad_out = cotangent[0]
    grad_all = lax.all_gather(grad_out, "wide", axis=0, tiled=True)
    grad_hidden = contract(grad_all, down_mat, 1, 1)
    grad_down = contract(hidden, grad_all, 0, 0)
    sig_gate = jax.nn.sigmoid(gate_val)
    grad_gate = (grad_hidden * up_val * sig_gate * (1.0 + gate_val * (1.0 - sig_gate))).astype(
        jnp.bfloat16
    )
    grad_up = (grad_hidden * gate_val * sig_gate).astype(jnp.bfloat16)
    grad_gate_w = contract(ffn_all, grad_gate, 0, 0)
    grad_up_w = contract(ffn_all, grad_up, 0, 0)
    grad_ffn_in = lax.psum_scatter(
        (contract(grad_gate, gate_mat, 1, 1) + contract(grad_up, up_mat, 1, 1)).astype(
            jnp.bfloat16
        ),
        "wide",
        scatter_dimension=0,
        tiled=True,
    ).astype(jnp.float32)
    ffn_grads = (
        lax.psum_scatter(
            grad_gate_w.astype(jnp.bfloat16), "seq", scatter_dimension=0, tiled=True
        ).astype(jnp.float32),
        lax.psum_scatter(
            grad_up_w.astype(jnp.bfloat16), "seq", scatter_dimension=0, tiled=True
        ).astype(jnp.float32),
        lax.psum_scatter(
            grad_down.astype(jnp.bfloat16), "seq", scatter_dimension=1, tiled=True
        ).astype(jnp.float32),
    )
    norm_two_back = jax.vjp(rms_scaled, middle, gain_second)[1]
    grad_mid_part, grad_gain_two = norm_two_back(grad_ffn_in)
    grad_middle = grad_out.astype(jnp.float32) + grad_mid_part
    grad_branch = grad_middle.astype(jnp.bfloat16)
    back_weights = gather_attention(w_query, w_key, w_value, w_out, gain_attn, gain_group, gain_ffn)
    query_back, key_back, value_back, out_back = (
        back_weights[0],
        back_weights[1],
        back_weights[2],
        back_weights[3],
    )
    grad_grouped = contract(grad_branch, out_back, 1, 1)
    grad_out_w = contract(grouped, grad_branch, 0, 0)
    group_back = jax.vjp(group_scaled, attended, gain_middle)[1]
    grad_attended, grad_gain_mid = group_back(grad_grouped.reshape(token_count, HEADS, HEAD_DIM))
    grad_att_b = grad_attended.astype(jnp.bfloat16)
    back_packets = collect_packets(own, reach_len)
    logits_again = all_logits(back_packets)
    probs_again = jnp.exp(logits_again - log_total[None, :, :, None])
    mixed_again = mix_heads(probs_again, head_mix).astype(jnp.bfloat16)
    values_back = back_packets[:, token_count + 2 * key_rim :].reshape(
        reach_len, token_count, HEADS, HEAD_DIM
    )
    grad_mixed = jnp.einsum(
        "the,rkhe->rhtk", grad_att_b, values_back, preferred_element_type=jnp.float32
    )
    grad_values = jnp.einsum(
        "rhtk,the->rkhe", mixed_again, grad_att_b, preferred_element_type=jnp.float32
    ).reshape(reach_len, token_count, width_all)
    probs_grouped = probs_again.reshape(reach_len, HEADS // GROUP, GROUP, token_count, token_count)
    mixed_grouped = grad_mixed.reshape(reach_len, HEADS // GROUP, GROUP, token_count, token_count)
    grad_mix = jnp.einsum(
        "rgdtk,rgctk->gcd", probs_grouped, mixed_grouped, precision=precise
    ).reshape(HEADS, GROUP)
    grad_probs = unmix_heads(grad_mixed, head_mix)
    delta_row = jnp.sum(probs_again * grad_probs, axis=(0, 3))
    grad_logits = probs_again * (grad_probs - delta_row[None, :, :, None])

    def tile_grads(turn_index):
        packet = lax.dynamic_index_in_dim(back_packets, turn_index, 0, keepdims=False)
        scores, allowed, row_masks, final_mask, key_ext = tile_logits(
            query_ext,
            packet,
            seg_query,
            pos_query,
            seg_key_pad,
            seq_index - turn_index,
            token_count,
        )
        conv_back = jax.vjp(
            lambda field, weights_k: convolve(field, allowed, row_masks, weights_k),
            scores,
            conv_kernel,
        )[1]
        grad_scores, grad_kernel = conv_back(
            lax.dynamic_index_in_dim(grad_logits, turn_index, 0, keepdims=False)
        )
        grad_scores_b = grad_scores.astype(jnp.bfloat16)
        grad_query_ext = (
            jnp.einsum("hqk,khe->qhe", grad_scores_b, key_ext, preferred_element_type=jnp.float32)
            * scaling
        )
        grad_key_ext = (
            jnp.einsum("hqk,qhe->khe", grad_scores_b, query_ext, preferred_element_type=jnp.float32)
            * scaling
        )
        cycle_term = jnp.concatenate(
            [
                grad_key_ext.reshape(token_count + 2 * key_rim, width_all),
                lax.dynamic_index_in_dim(grad_values, turn_index, 0, keepdims=False),
            ],
            axis=0,
        )
        return (cycle_term, grad_query_ext, grad_kernel)

    start_term, start_query, start_kernel = tile_grads(reach_len - 1)

    def descend(turn_index, state_all):
        cycle_acc, query_acc, kernel_acc = state_all
        cycle_term, query_part, kernel_part = tile_grads(reach_len - 1 - turn_index)
        moved_acc = passed_along(cycle_acc.astype(jnp.bfloat16), "seq", -1).astype(cycle_acc.dtype)
        return (moved_acc + cycle_term, query_acc + query_part, kernel_acc + kernel_part)

    cycle_acc, query_acc, kernel_acc = lax.fori_loop(
        1, reach_len, descend, (start_term, start_query, start_kernel)
    )
    query_flat = query_acc.reshape(token_count + query_rim, width_all)
    key_ext_grad = cycle_acc[: token_count + 2 * key_rim]
    grad_values_own = cycle_acc[token_count + 2 * key_rim :]
    edge_grads = jnp.stack(
        [
            jnp.concatenate([query_flat[:query_rim], jnp.zeros((key_rim, width_all), jnp.float32)]),
            jnp.concatenate([key_ext_grad[:key_rim], key_ext_grad[token_count + key_rim :]]),
        ]
    )
    rim_back = extended(edge_grads.astype(jnp.bfloat16), (("seq", 1),), key_rim).astype(
        edge_grads.dtype
    )
    grad_queries = (
        query_flat[query_rim:].at[token_count - key_rim :].add(rim_back[0, 3 * key_rim :])
    )
    grad_keys = (
        key_ext_grad[key_rim : key_rim + token_count]
        .at[:key_rim]
        .add(rim_back[1, :key_rim])
        .at[token_count - key_rim :]
        .add(rim_back[1, 3 * key_rim :])
    )
    grad_query_b = grad_queries.astype(jnp.bfloat16)
    grad_key_b = grad_keys.astype(jnp.bfloat16)
    grad_value_b = grad_values_own.astype(jnp.bfloat16)
    grad_query_w = contract(normed, grad_query_b, 0, 0)
    grad_key_w = contract(normed, grad_key_b, 0, 0)
    grad_value_w = contract(normed, grad_value_b, 0, 0)
    grad_normed = (
        contract(grad_query_b, query_back, 1, 1)
        + contract(grad_key_b, key_back, 1, 1)
        + contract(grad_value_b, value_back, 1, 1)
    )
    norm_one_back = jax.vjp(rms_scaled, inputs, gain_first)[1]
    grad_in_part, grad_gain_one = norm_one_back(grad_normed)
    grad_input = (grad_middle + grad_in_part).astype(jnp.bfloat16)
    attn_grads = (
        lax.psum_scatter(grad_query_w, ("seq", "wide"), scatter_dimension=0, tiled=True),
        lax.psum_scatter(grad_key_w, ("seq", "wide"), scatter_dimension=0, tiled=True),
        lax.psum_scatter(grad_value_w, ("seq", "wide"), scatter_dimension=0, tiled=True),
        lax.psum_scatter(grad_out_w, ("seq", "wide"), scatter_dimension=0, tiled=True),
        lax.psum_scatter(grad_gain_one, ("seq", "wide"), scatter_dimension=0, tiled=True),
        lax.psum_scatter(
            grad_gain_mid.reshape(width_all), ("seq", "wide"), scatter_dimension=0, tiled=True
        ),
        lax.psum_scatter(grad_gain_two, ("seq", "wide"), scatter_dimension=0, tiled=True),
    )
    small_sums = lax.psum((kernel_acc, grad_mix), ("seq", "wide"))
    return (
        output[None],
        grad_input[None],
        attn_grads[0],
        attn_grads[1],
        attn_grads[2],
        attn_grads[3],
        attn_grads[4],
        attn_grads[5],
        attn_grads[6],
        small_sums[0],
        small_sums[1],
        ffn_grads[0],
        ffn_grads[1],
        ffn_grads[2],
    )


def dot_plain(left, right):
    return contract(left, right, 1, 0)


def dot_nt(left, right):
    return contract(left, right, 1, 1)


def dot_tn(left, right):
    return contract(left, right, 0, 0)


def halves(value):
    high = value.astype(jnp.bfloat16)
    return high, (value - high.astype(jnp.float32)).astype(jnp.bfloat16)


def iota(shape, dim):
    return lax.broadcasted_iota(jnp.int32, shape, dim)


def spread_lanes(tile, count):
    return tile if count == 1 else jnp.concatenate([tile] * count, axis=1)


def allowed_mask(starts, block, first_col, count):
    cols = iota((BLOCK, count * LANES), 1) + first_col
    rows = iota((BLOCK, count * LANES), 0) + block * BLOCK
    return (cols >= spread_lanes(starts, count)) & (cols <= rows)


def head_stats(values):
    lane = iota(values.shape, 1)
    mean = jnp.sum(values, axis=-1, keepdims=True) * (1.0 / HEAD_DIM)
    center = jnp.where(lane < HEAD_DIM, values - mean, 0.0)
    spread = jnp.sum(center * center, axis=-1, keepdims=True) * (1.0 / HEAD_DIM)
    inverse = lax.rsqrt(spread + epsilon)
    return center * inverse, inverse


def fold_rows(value):
    return jnp.sum(value.reshape(value.shape[0] // 8, 8, value.shape[1]), axis=0)


def full_spec():
    return pl.BlockSpec(memory_space=pltpu.VMEM)


def smem_spec():
    return pl.BlockSpec(memory_space=pltpu.SMEM)


def shape_of(shape, dtype=jnp.bfloat16):
    return jax.ShapeDtypeStruct(shape, dtype)


def in_hbm(value):
    return pltpu.with_memory_space_constraint(value, pltpu.HBM)


def kernel_call(body, name, outs, ins, scratch=(), flops=0, smem=0, vmem=40, lazy=0, hbm=0):
    still = lazy + hbm
    moved = sum(v.size * v.dtype.itemsize for v in ins) + sum(
        o.size * o.dtype.itemsize for o in outs
    )
    return pl.pallas_call(
        body,
        in_specs=[smem_spec()] * smem
        + [full_spec()] * (len(ins) - smem - still)
        + [pl.BlockSpec(memory_space=pltpu.HBM)] * still,
        out_specs=[full_spec()] * len(outs),
        out_shape=list(outs),
        scratch_shapes=[pltpu.VMEM(v.shape, v.dtype) for v in ins[len(ins) - lazy :]]
        + [pltpu.SemaphoreType.DMA((lazy,))] * min(lazy, 1)
        + list(scratch),
        compiler_params=pltpu.CompilerParams(vmem_limit_bytes=vmem << 20),
        cost_estimate=pl.CostEstimate(flops=flops, bytes_accessed=moved, transcendentals=0),
        name=name,
    )(*ins[: len(ins) - still], *(in_hbm(v) for v in ins[len(ins) - still :]))


def started(sources, targets, sems):
    copies = [
        pltpu.make_async_copy(source, target, sems.at[i])
        for i, (source, target) in enumerate(zip(sources, targets))
    ]
    for copy in copies:
        copy.start()

    def wait(first, last):
        for copy in copies[first:last]:
            copy.wait()

    return wait


ORDER = (0, 4, 1, 5, 2, 6, 3, 7)


def slot_place(plane, slot):
    other = plane ^ ORDER[slot]
    return other & 1, pl.multiple_of((other >> 1) * BLOCK, BLOCK)


def half_tile(tiles, index):
    tile = tiles[index // 2]
    return tile, pltpu.roll(tile, LANES // 2, 1), index % 2


def joined(first, second):
    low = first[1] if first[2] else first[0]
    high = second[0] if second[2] else second[1]
    lane = iota(low.shape, 1)
    return jnp.where(lane < LANES // 2, low, high)


def pack_kernel(
    slab, gains_ref, q_from, k_from, v_from, rows_from, out_ref, rows_out_ref,
    q_ref, k_ref, v_ref, rows_ref, sems,
):
    wait = started(
        (q_from, k_from, v_from, rows_from), (q_ref, k_ref, v_ref, rows_ref), sems
    )
    wait(0, 4)
    tiles = [
        [ref[:, t * LANES : (t + 1) * LANES] for t in range(ref.shape[1] // LANES)]
        for ref in (q_ref, k_ref, v_ref)
    ]
    per = GROUP * HEAD_DIM // (LANES // 2)
    for g in range(8):
        parts = [half_tile(tiles[w], per * g + i) for w in range(3) for i in range(per)]
        for t in range(4):
            out_ref[g, t * slab : (t + 1) * slab, :] = joined(
                parts[2 * t], parts[2 * t + 1]
            ).astype(jnp.bfloat16)
        tile, turned, side = parts[8]
        first, second = (turned, tile) if side else (tile, turned)
        half = slab // 2
        lane = iota((half, LANES), 1)
        out_ref[g, 4 * slab : 4 * slab + half, :] = jnp.where(
            lane < LANES // 2, first[:half], second[half:]
        ).astype(jnp.bfloat16)
        out_ref[g, 4 * slab + half :, :] = gains_ref[...]
    for t in range(rows_ref.shape[1] // LANES):
        rows_out_ref[t * slab : (t + 1) * slab, :] = rows_ref[
            :, t * LANES : (t + 1) * LANES
        ].astype(jnp.bfloat16)


def unpack_kernel(slab, in_ref, rows_ref, q_ref, k_ref, v_ref, out_ref):
    per = GROUP * HEAD_DIM // (LANES // 2)
    pieces = [[], [], []]
    half = slab // 2
    lane = iota((half, LANES), 1)
    for g in range(8):
        tiles = [
            in_ref[g, t * slab : (t + 1) * slab, :].astype(jnp.float32) for t in range(4)
        ]
        rest = in_ref[g, 4 * slab : 4 * slab + half, :].astype(jnp.float32)
        turned = pltpu.roll(rest, LANES // 2, 1)
        tiles.append(jnp.concatenate([rest, turned], axis=0))
        for i in range(3 * per):
            pieces[i // per].append(half_tile(tiles, i))
    for ref, parts in zip((q_ref, k_ref, v_ref), pieces):
        for t in range(len(parts) // 2):
            ref[:, t * LANES : (t + 1) * LANES] = joined(parts[2 * t], parts[2 * t + 1])
    for t in range(out_ref.shape[1] // LANES):
        out_ref[:, t * LANES : (t + 1) * LANES] = rows_ref[t * slab : (t + 1) * slab, :].astype(
            jnp.float32
        )


def attend_pack(p, blocks, reach, mix_ref, q_ref, k_ref, v_ref, start_ref, th_ref, tl_ref, gain,
                probs_ref, high_ref, att_ref, grouped_ref, low_ref, part_ref):
    key_rim = CK // 2
    scaling = HEAD_DIM ** (-0.5)
    for h in range(GROUP):
        lanes = slice(h * LANES, (h + 1) * LANES)
        high_ref[p, h, :RIM, :] = jnp.zeros((RIM, high_ref.shape[3]), jnp.bfloat16)
        low_ref[h, :RIM, :] = jnp.zeros((RIM, high_ref.shape[3]), jnp.bfloat16)
        for n in range(blocks):
            first, last = max(0, n - reach), min(n + 3, blocks + 1)
            rows = slice(n * BLOCK, (n + 1) * BLOCK)
            scores = (
                dot_nt(q_ref[p, rows, lanes], k_ref[p, first * BLOCK : last * BLOCK, lanes]) * scaling
            )
            keep = allowed_mask(start_ref[p, rows, :], n, first * BLOCK - key_rim, last - first)
            high, low = halves(jnp.where(keep, scores, 0.0))
            into = slice(RIM + n * BLOCK, RIM + (n + 1) * BLOCK)
            cols = slice(first * LANES, last * LANES)
            high_ref[p, h, into, cols] = high
            low_ref[h, into, cols] = low
    for n in range(blocks):
        first = max(0, n - reach)
        count = n - first + 1
        rows = slice(n * BLOCK, (n + 1) * BLOCK)
        starts = start_ref[p, rows, :]
        offset = iota((BLOCK, LANES), 0) + n * BLOCK - starts
        keep = allowed_mask(starts, n, first * BLOCK, count)
        window = slice((reach + 1 - count) * LANES, (reach + 1) * LANES)
        probs = []
        for h in range(GROUP):
            pieces = []
            for m in range(first, n + 1):
                rim_rows = slice(n * BLOCK, (n + 1) * BLOCK + RIM)
                cols = slice(m * LANES, (m + 2) * LANES)
                high = high_ref[p, h, rim_rows, cols]
                low = low_ref[h, rim_rows, cols]
                part = (
                    dot_plain(high, th_ref[h])
                    + dot_plain(low, th_ref[h])
                    + dot_plain(high, tl_ref[h])
                )
                for a in range(CQ):
                    part_ref[a] = part[:, a * LANES : (a + 1) * LANES]
                total = part_ref[0, RIM:, :]
                for a in range(1, CQ):
                    total = total + jnp.where(
                        offset >= a, part_ref[a, RIM - a : RIM - a + BLOCK, :], 0.0
                    )
                pieces.append(total)
            logits = pieces[0] if count == 1 else jnp.concatenate(pieces, axis=1)
            logits = jnp.where(keep, logits, -jnp.inf)
            peak = jnp.max(logits, axis=-1, keepdims=True)
            raised = jnp.exp(logits - peak)
            prob = raised / jnp.sum(raised, axis=-1, keepdims=True)
            probs_ref[p, h, rows, window] = prob
            probs.append(prob)
        keys = slice(first * BLOCK, (n + 1) * BLOCK)
        for h in range(GROUP):
            lanes = slice(h * LANES, (h + 1) * LANES)
            mixed = (mix_ref[h, 0] * probs[0] + mix_ref[h, 1] * probs[1]).astype(jnp.bfloat16)
            attended = dot_plain(mixed, v_ref[p, keys, lanes])
            att_ref[p, rows, lanes] = attended
            normal, _ = head_stats(attended)
            grouped_ref[p, rows, lanes] = (normal * gain[:, lanes]).astype(jnp.bfloat16)


def forward_kernel(
    blocks, reach, slab, at_ref, mix_ref, w_ref, t0, t1, t2, t3, t4, t5, t6, t7,
    start_ref, th_ref, tl_ref, spread_ref, rest_ref,
    normed_ref, wide_ref, q_ref, k_ref, v_ref, probs_ref, high_ref, att_ref, near_ref,
    far_ref, gains_ref, gain_ref,
    grp_ref, shift_ref, low_ref, part_ref,
):
    plane = at_ref[0]
    half = slab // 2
    block = 4 * slab + half + 8
    gains_ref[...] = jnp.zeros_like(gains_ref)
    span = gains_ref.shape[1] // 4
    for zz in range(w_ref.shape[0]):
        ref = w_ref.at[zz]
        main = jnp.concatenate(
            [
                jnp.concatenate(
                    [ref[g * block + t * slab : g * block + (t + 1) * slab, :] for t in range(4)],
                    axis=1,
                )
                for g in range(8)
            ],
            axis=0,
        )
        rest = jnp.concatenate(
            [ref[g * block + 4 * slab : g * block + 4 * slab + half, :] for g in range(8)], axis=0
        )
        table = dot_plain(main, spread_ref[...])
        early = dot_plain(rest, rest_ref[0])
        late = dot_plain(rest, rest_ref[1])
        for g in range(8):
            row = (g // 2 * 8 + g % 2 + 2 * zz) * slab
            tail = jnp.concatenate(
                [early[g * half : (g + 1) * half], late[g * half : (g + 1) * half]], axis=0
            )
            wide_ref[row : row + slab, :] = (table[g * slab : (g + 1) * slab] + tail).astype(
                jnp.bfloat16
            )
        lane = iota((LANES, span), 0)
        for y in range(2):
            place = (iota((LANES, span), 1) == lane + (zz * 2 + y) * slab) & (lane < slab)
            place = jnp.where(place, 1.0, 0.0).astype(jnp.bfloat16)
            for s in range(4):
                gains_ref[:, s * span : (s + 1) * span] += dot_plain(
                    ref[(2 * s + y + 1) * block - 8 : (2 * s + y + 1) * block, :], place
                )
    cols = GROUP * HEAD_DIM
    width = gains_ref.shape[1]
    lane = iota((width, GROUP * LANES), 1)
    from_row = iota((width, GROUP * LANES), 0) - plane * cols
    select = (from_row == lane // LANES * HEAD_DIM + lane % LANES) & (lane % LANES < HEAD_DIM)
    gain_ref[...] = dot_plain(
        gains_ref[...].astype(jnp.bfloat16), jnp.where(select, 1.0, 0.0).astype(jnp.bfloat16)
    )[1:2]
    gain = gain_ref[...]
    for slot, ref in enumerate((t0, t1, t2, t3, t4, t5, t6, t7)):
        value = ref[...].astype(jnp.float32)
        scale = lax.rsqrt(jnp.mean(value * value, axis=-1, keepdims=True) + epsilon)
        normed_ref[slot * BLOCK : (slot + 1) * BLOCK, :] = (
            value * scale * gains_ref[0:1, :]
        ).astype(jnp.bfloat16)
    lanes = GROUP * LANES
    shift_ref[...] = jnp.zeros_like(shift_ref)
    for slots in (range(4), range(4, 8)):
        rows = slice(slots[0] * BLOCK, (slots[-1] + 1) * BLOCK)
        qkv = dot_plain(normed_ref[rows, :], wide_ref[...])
        for i, slot in enumerate(slots):
            pack, row = slot_place(plane, slot)
            part = qkv[i * BLOCK : (i + 1) * BLOCK]
            q_ref[pack, pl.ds(row, BLOCK), :] = part[:, :lanes].astype(jnp.bfloat16)
            shift_ref[pack, pl.ds(row, BLOCK), :] = part[:, lanes : 2 * lanes]
            v_ref[pack, pl.ds(row, BLOCK), :] = part[:, 2 * lanes :].astype(jnp.bfloat16)
    key_rim = CK // 2
    length = q_ref.shape[1]
    @pl.loop(0, 2)
    def _(p):
        moved = jnp.concatenate(
            [
                jnp.zeros((8, lanes), jnp.float32),
                shift_ref[p],
                jnp.zeros((LANES - 8, lanes), jnp.float32),
            ],
            axis=0,
        )
        moved = pltpu.roll(moved, length + LANES - (8 - key_rim), 0)
        k_ref[p] = moved.astype(jnp.bfloat16)
        attend_pack(
            p, blocks, reach, mix_ref, q_ref, k_ref, v_ref, start_ref, th_ref, tl_ref, gain,
            probs_ref, high_ref, att_ref, grp_ref, low_ref, part_ref,
        )

    for slot in range(8):
        pack, row = slot_place(plane, slot)
        into = near_ref if slot < 4 else far_ref
        into[slot % 4 * BLOCK : (slot % 4 + 1) * BLOCK, :] = grp_ref[pack, pl.ds(row, BLOCK), :]


def store_blocks(value, refs):
    for i, ref in enumerate(refs):
        ref[...] = value[i * BLOCK : (i + 1) * BLOCK].astype(ref.dtype)


def pair_kernel(
    transposed, own_ref, got_ref, w_from, other_from, total_ref, r1, r2, r3, w_ref, other_ref, sems
):
    wait = started((w_from, other_from), (w_ref, other_ref), sems)
    dot = dot_nt if transposed else dot_plain
    wait(0, 1)
    value = dot(own_ref[...], w_ref[...])
    wait(1, 2)
    value = value + dot(got_ref[...], other_ref[...])
    store_blocks(value, (total_ref, r1, r2, r3))


def pair_gain_kernel(
    own_ref, got_ref, w_from, other_from, t0_from, t1_from, t2_from, t3_from,
    total_ref, r1, r2, r3, gain_ref,
    w_ref, other_ref, t0, t1, t2, t3, sems,
):
    wait = started(
        (w_from, other_from, t0_from, t1_from, t2_from, t3_from),
        (w_ref, other_ref, t0, t1, t2, t3),
        sems,
    )
    wait(0, 1)
    value = dot_nt(own_ref[...], w_ref[...])
    wait(1, 6)
    value = value + dot_nt(got_ref[...], other_ref[...])
    store_blocks(value, (total_ref, r1, r2, r3))
    total = jnp.zeros(gain_ref.shape, jnp.float32)
    for i, ref in enumerate((t0, t1, t2, t3)):
        token = ref[...].astype(jnp.float32)
        scale = lax.rsqrt(jnp.mean(token * token, axis=-1, keepdims=True) + epsilon)
        total = total + fold_rows(value[i * BLOCK : (i + 1) * BLOCK] * (token * scale))
    gain_ref[...] = total


def small_kernel(at_ref, attn_ref, ffn_ref, taps_ref, mix_ref, group_ref, out_ref):
    plane = at_ref[0]
    out_ref[...] = jnp.zeros_like(out_ref)
    tiles = attn_ref.shape[1] // LANES
    for i, ref in enumerate((attn_ref, ffn_ref)):
        row = jnp.sum(ref[...], axis=0, keepdims=True)
        for t in range(tiles):
            out_ref[i * tiles + t : i * tiles + t + 1, :] = row[:, t * LANES : (t + 1) * LANES]
    group = jnp.sum(group_ref[...], axis=0, keepdims=True)
    lane = iota((16, LANES), 1)
    place = iota((16, LANES), 0)
    first = iota((1, LANES), 1)
    for h in range(GROUP):
        head = GROUP * plane + h
        out_ref[pl.ds(2 * tiles + head, 1), :] = group[:, h * LANES : (h + 1) * LANES]
        total = jnp.zeros((16, LANES), jnp.float32)
        for a in range(CQ):
            sums = jnp.sum(taps_ref[h, :, a * LANES : (a + 1) * LANES], axis=-1, keepdims=True)
            total = total + jnp.where(lane == 16 * a + place, sums, 0.0)
        row = jnp.sum(total, axis=0, keepdims=True)
        for d in range(GROUP):
            value = jnp.sum(mix_ref[h * GROUP + d], axis=0, keepdims=True)
            value = jnp.sum(value, axis=1, keepdims=True)
            row = row + jnp.where(first == 16 * CQ + d, value, 0.0)
        out_ref[pl.ds(2 * tiles + HEADS + head, 1), :] = row


def backward_pack(p, blocks, reach, mix_ref, gg_ref, att_ref, gain_ref, q_ref, k_ref, v_ref,
                  start_ref, stop_ref, probs_ref, high_ref, th_ref,
                  dqkv_ref, mixg_ref, gaing_ref, grad_ref, cross_ref, keyg_ref, valueg_ref, ready):
    key_rim = CK // 2
    scaling = HEAD_DIM ** (-0.5)
    all_lanes = GROUP * LANES
    grad_ref[...] = jnp.zeros_like(grad_ref)
    keyg_ref[...] = jnp.zeros_like(keyg_ref)
    valueg_ref[...] = jnp.zeros_like(valueg_ref)
    lane = iota((BLOCK, LANES), 1)
    for n in range(blocks):
        first = max(0, n - reach)
        count = n - first + 1
        rows = slice(n * BLOCK, (n + 1) * BLOCK)
        keys = slice(first * BLOCK, (n + 1) * BLOCK)
        window = slice((reach + 1 - count) * LANES, (reach + 1) * LANES)
        probs = [probs_ref[p, h, rows, window] for h in range(GROUP)]
        mixed_grads = []
        for h in range(GROUP):
            lanes = slice(h * LANES, (h + 1) * LANES)
            normal, inverse = head_stats(att_ref[p, rows, lanes])
            grad_grouped = gg_ref[p, rows, lanes]
            gaing_ref[:, lanes] += fold_rows(grad_grouped * normal)
            scaled = jnp.where(lane < HEAD_DIM, grad_grouped * gain_ref[:, lanes], 0.0)
            mean_one = jnp.sum(scaled, axis=-1, keepdims=True) * (1.0 / HEAD_DIM)
            mean_two = jnp.sum(scaled * normal, axis=-1, keepdims=True) * (1.0 / HEAD_DIM)
            grad_att = inverse * (scaled - mean_one - normal * mean_two)
            grad_att = jnp.where(lane < HEAD_DIM, grad_att, 0.0).astype(jnp.bfloat16)
            mixed_grads.append(dot_nt(grad_att, v_ref[p, keys, lanes]))
            mixed = (mix_ref[h, 0] * probs[0] + mix_ref[h, 1] * probs[1]).astype(jnp.bfloat16)
            valueg_ref[keys, lanes] += dot_tn(mixed, grad_att)
        for h in range(GROUP):
            for d in range(GROUP):
                product = fold_rows(probs[d] * mixed_grads[h])
                total = product[:, :LANES]
                for m in range(1, count):
                    total = total + product[:, m * LANES : (m + 1) * LANES]
                mixg_ref[h * GROUP + d] += total
        for d in range(GROUP):
            grad_probs = mix_ref[0, d] * mixed_grads[0] + mix_ref[1, d] * mixed_grads[1]
            delta = jnp.sum(probs[d] * grad_probs, axis=-1, keepdims=True)
            grad_logits = probs[d] * (grad_probs - delta)
            for m in range(count):
                grad_ref[d, first + m, rows, :] = grad_logits[:, m * LANES : (m + 1) * LANES]
    ready()
    for h in range(GROUP):
        lanes = slice(h * LANES, (h + 1) * LANES)
        for n in range(blocks):
            first, last = max(0, n - reach), min(n + 1, blocks - 1)
            rows = slice(n * BLOCK, (n + 1) * BLOCK)
            room = stop_ref[p, rows, :] - (iota((BLOCK, LANES), 0) + n * BLOCK)
            count = n + 2 - first
            sums = [None] * (count + 1)
            for m in range(first, last + 1):
                pieces = []
                for a in range(CQ):
                    piece = grad_ref[h, m, n * BLOCK + a : (n + 1) * BLOCK + a, :]
                    if a:
                        piece = jnp.where(room > a, piece, 0.0)
                    pieces.append(piece.astype(jnp.bfloat16))
                high = jnp.concatenate(pieces, axis=1)
                part = dot_nt(high, th_ref[h])
                for side in range(2):
                    place = m - first + side
                    value = part[:, side * LANES : (side + 1) * LANES]
                    sums[place] = value if sums[place] is None else sums[place] + value
                scores = high_ref[
                    p, h, RIM + n * BLOCK : RIM + (n + 1) * BLOCK, m * LANES : (m + 2) * LANES
                ]
                if m <= n:
                    cross_ref[h] += dot_tn(scores, high)
                else:
                    cross_ref[h, :LANES, :] += dot_tn(scores[:, :LANES], high)
            total = jnp.concatenate(sums[:count], axis=1)
            keep = allowed_mask(start_ref[p, rows, :], n, first * BLOCK - key_rim, count)
            grad_scores = jnp.where(keep, total, 0.0).astype(jnp.bfloat16)
            cols = slice(first * BLOCK, (first + count) * BLOCK)
            dqkv_ref[p, rows, lanes] = (
                dot_plain(grad_scores, k_ref[p, cols, lanes]) * scaling
            ).astype(jnp.bfloat16)
            keyg_ref[h, cols, :] += dot_tn(grad_scores, q_ref[p, rows, lanes])
        key_lanes = slice(all_lanes + h * LANES, all_lanes + (h + 1) * LANES)
        dqkv_ref[p, :, key_lanes] = (
            keyg_ref[h, key_rim : key_rim + blocks * BLOCK, :] * scaling
        ).astype(jnp.bfloat16)
    dqkv_ref[p, :, 2 * all_lanes :] = valueg_ref[...].astype(jnp.bfloat16)


def backward_kernel(
    blocks, reach, at_ref, mix_ref, b0, b1, b2, b3, b4, b5, b6, b7, out_w_ref, gain_ref,
    att_from, v_from, probs_from, start_from, stop_from, th_from, high_from, k_from, q_from,
    near_ref, far_ref, taps_ref, mixg_ref, gaing_ref,
    att_ref, v_ref, probs_ref, start_ref, stop_ref, th_ref, high_ref, k_ref, q_ref, sems,
    gg_ref, abs_ref, grad_ref, cross_ref, keyg_ref, valueg_ref,
):
    plane = at_ref[0]
    sources = (
        att_from, v_from, probs_from, start_from, stop_from, th_from, high_from, k_from, q_from
    )
    targets = (
        att_ref, v_ref, probs_ref, start_ref, stop_ref, th_ref, high_ref, k_ref, q_ref
    )
    wait = started(sources, targets, sems)
    pieces = (b0, b1, b2, b3, b4, b5, b6, b7)
    for slots in (range(4), range(4, 8)):
        branch = jnp.concatenate([pieces[slot][...] for slot in slots], axis=0)
        part = dot_nt(branch, out_w_ref[...])
        for i, slot in enumerate(slots):
            pack, row = slot_place(plane, slot)
            gg_ref[pack, pl.ds(row, BLOCK), :] = part[i * BLOCK : (i + 1) * BLOCK]
    cross_ref[...] = jnp.zeros_like(cross_ref)
    mixg_ref[...] = jnp.zeros_like(mixg_ref)
    gaing_ref[...] = jnp.zeros_like(gaing_ref)
    wait(0, 3)

    for p in range(2):
        backward_pack(
            p, blocks, reach, mix_ref, gg_ref, att_ref, gain_ref, q_ref, k_ref, v_ref,
            start_ref, stop_ref, probs_ref, high_ref, th_ref,
            abs_ref, mixg_ref, gaing_ref, grad_ref, cross_ref, keyg_ref, valueg_ref,
            (lambda: wait(3, 9)) if p == 0 else lambda: None,
        )
    for slot in range(8):
        pack, row = slot_place(plane, slot)
        into = near_ref if slot < 4 else far_ref
        into[slot % 4 * BLOCK : (slot % 4 + 1) * BLOCK, :] = abs_ref[pack, pl.ds(row, BLOCK), :]
    height = LANES + 2 * 8
    shift = iota((height, CQ * LANES), 1) % LANES - iota((height, CQ * LANES), 0) + (CK - 1)
    for h in range(GROUP):
        cross = cross_ref[h, :height, :]
        taps_ref[h] = jnp.zeros(taps_ref.shape[1:], jnp.float32)
        for b in range(CK):
            taps_ref[h, b : b + 1, :] = jnp.sum(
                jnp.where(shift == b, cross, 0.0), axis=0, keepdims=True
            )


def out_rows_kernel(slab, w_ref, out_ref):
    width = out_ref.shape[1]
    base = w_ref.shape[1] - width // LANES * slab
    fill = jnp.zeros((LANES - HEAD_DIM, width), jnp.bfloat16)
    for k in range(w_ref.shape[0]):
        row = k // 2 * LANES + k % 2 * slab
        for t in range(width // LANES):
            out_ref[row : row + slab, t * LANES : (t + 1) * LANES] = w_ref[
                k, base + t * slab : base + (t + 1) * slab, :
            ]
    for h in range(GROUP):
        out_ref[h * LANES + HEAD_DIM : (h + 1) * LANES, :] = fill


def weight_grads_kernel(
    slab, near_ref, far_ref, b0, b1, b2, b3, b4, b5, b6, b7,
    group_near_from, group_far_from, spread_from, rest_from, normed_from, all_ref,
    group_near, group_far, spread_ref, rest_ref, normed_ref, sems,
):
    wait = started(
        (group_near_from, group_far_from, spread_from, rest_from, normed_from),
        (group_near, group_far, spread_ref, rest_ref, normed_ref),
        sems,
    )
    pieces = (b0, b1, b2, b3, b4, b5, b6, b7)
    near = jnp.concatenate([ref[...] for ref in pieces[:4]], axis=0)
    wait(0, 2)
    grad = dot_tn(group_near[...], near)
    far = jnp.concatenate([ref[...] for ref in pieces[4:]], axis=0)
    grad = (grad + dot_tn(group_far[...], far)).astype(jnp.bfloat16)
    base = all_ref.shape[1] - grad.shape[1] // LANES * slab
    for k in range(all_ref.shape[0]):
        row = k // 2 * LANES + k % 2 * slab
        for t in range(grad.shape[1] // LANES):
            all_ref[k, base + t * slab : base + (t + 1) * slab, :] = grad[
                row : row + slab, t * LANES : (t + 1) * LANES
            ]
    block = base // 8
    wait(2, 5)
    half = slab // 2
    span = normed_ref.shape[1] // 4
    for s in range(4):
        rows = near_ref.shape[0]
        cols = slice(s * span, (s + 1) * span)
        table = (
            dot_tn(normed_ref[:rows, cols], near_ref[...])
            + dot_tn(normed_ref[rows:, cols], far_ref[...])
        ).astype(jnp.bfloat16)
        main = dot_nt(table, spread_ref[...])
        early = dot_nt(table, rest_ref[0])
        late = dot_nt(table, rest_ref[1])
        for zz in range(4):
            for y in range(2):
                g = 2 * s + y
                row = (zz * 2 + y) * slab
                for t in range(4):
                    at = g * block + t * slab
                    all_ref[zz, at : at + slab, :] = main[
                        row : row + slab, t * LANES : (t + 1) * LANES
                    ].astype(jnp.bfloat16)
                rest = early[row : row + half] + late[row + half : row + slab]
                all_ref[zz, g * block + 4 * slab : (g + 1) * block, :] = jnp.concatenate(
                    [rest, jnp.zeros((8, LANES), jnp.float32)], axis=0
                ).astype(jnp.bfloat16)


def assemble_kernel(sub, w_ref, gu_ref, down_ref):
    deep = w_ref.shape[3]
    units = w_ref.shape[0] * sub
    parts = deep // LANES
    for zz in range(w_ref.shape[0]):
        for s in range(w_ref.shape[1]):
            for m in range(2):
                at = m * units + zz * sub
                gu_ref[s * deep : (s + 1) * deep, at : at + sub] = w_ref[zz, s, m]
            for c in range(parts):
                at = (s * parts + c) * LANES
                down_ref[zz * sub : (zz + 1) * sub, at : at + LANES] = w_ref[
                    zz, s, 2, c * sub : (c + 1) * sub, :
                ]


def hidden_kernel(
    x0, x1, x2, x3, x4, x5, x6, x7, c0, c1, c2, c3, c4, c5, c6, c7, gu_ref, down_ref,
    hidden_near, hidden_far, grad_near, grad_far,
):
    units = down_ref.shape[0]
    xs = (x0, x1, x2, x3, x4, x5, x6, x7)
    cs = (c0, c1, c2, c3, c4, c5, c6, c7)
    for part in (2, 3, 0, 1):
        pair = (2 * part, 2 * part + 1)
        value = jnp.concatenate([xs[i][...] for i in pair], axis=0)
        gate_up = dot_plain(value, gu_ref[...])
        gate, up = gate_up[:, :units], gate_up[:, units:]
        cot = jnp.concatenate([cs[i][...] for i in pair], axis=0)
        grad_hidden = dot_nt(cot, down_ref[...])
        sig = 1.0 / (1.0 + jnp.exp(-gate))
        silu = gate * sig
        hidden_ref, grad_ref = (hidden_near, grad_near) if part < 2 else (hidden_far, grad_far)
        rows = slice(part % 2 * 2 * BLOCK, (part % 2 + 1) * 2 * BLOCK)
        hidden_ref[rows, :] = (silu * up).astype(jnp.bfloat16)
        grad_ref[rows, :units] = (
            grad_hidden * up * sig * (1.0 + gate * (1.0 - sig))
        ).astype(jnp.bfloat16)
        grad_ref[rows, units:] = (grad_hidden * silu).astype(jnp.bfloat16)


def hidden_grad_kernel(
    sub, hidden_near, hidden_far, grad_near, grad_far,
    x0, x1, x2, x3, x4, x5, x6, x7, c0, c1, c2, c3, c4, c5, c6, c7, out_ref, x_ref, c_ref, sems,
):
    deep = out_ref.shape[3]
    depth = out_ref.shape[0]
    units = depth * sub
    rows = [slice(slot * BLOCK, (slot + 1) * BLOCK) for slot in range(8)]
    wait = started(
        (x0, x1, x2, x3, x4, x5, x6, x7, c0, c1, c2, c3, c4, c5, c6, c7),
        [x_ref.at[part, :] for part in rows] + [c_ref.at[part, :] for part in rows],
        sems,
    )
    half = 4 * BLOCK
    wait(0, 8)
    for s in range(out_ref.shape[1]):
        cols = slice(s * deep, (s + 1) * deep)
        table = (
            dot_tn(x_ref[:half, cols], grad_near[...]) + dot_tn(x_ref[half:, cols], grad_far[...])
        ).astype(jnp.bfloat16)
        for zz in range(depth):
            for m in range(2):
                at = m * units + zz * sub
                out_ref[zz, s, m] = table[:, at : at + sub]
    wait(8, 16)
    for s in range(out_ref.shape[1]):
        cols = slice(s * deep, (s + 1) * deep)
        down = (
            dot_tn(hidden_near[...], c_ref[:half, cols])
            + dot_tn(hidden_far[...], c_ref[half:, cols])
        ).astype(jnp.bfloat16)
        for zz in range(depth):
            for c in range(deep // LANES):
                out_ref[zz, s, 2, c * sub : (c + 1) * sub, :] = down[
                    zz * sub : (zz + 1) * sub, c * LANES : (c + 1) * LANES
                ]


def pack_hidden_kernel(sub, gate_ref, up_ref, down_ref, out_ref):
    deep = gate_ref.shape[0]
    for s in range(out_ref.shape[0]):
        for m, ref in enumerate((gate_ref, up_ref)):
            out_ref[s, m] = ref[:, s * sub : (s + 1) * sub].astype(jnp.bfloat16)
        for c in range(deep // LANES):
            out_ref[s, 2, c * sub : (c + 1) * sub, :] = down_ref[
                s * sub : (s + 1) * sub, c * LANES : (c + 1) * LANES
            ].astype(jnp.bfloat16)


def unpack_hidden_kernel(sub, in_ref, gate_ref, up_ref, down_ref):
    deep = gate_ref.shape[0]
    for s in range(in_ref.shape[0]):
        for m, ref in enumerate((gate_ref, up_ref)):
            ref[:, s * sub : (s + 1) * sub] = in_ref[s, m].astype(jnp.float32)
        for c in range(deep // LANES):
            down_ref[s * sub : (s + 1) * sub, c * LANES : (c + 1) * LANES] = in_ref[
                s, 2, c * sub : (c + 1) * sub, :
            ].astype(jnp.float32)


def total_of(refs):
    total = refs[0][...]
    for ref in refs[1:]:
        total = total + ref[...].astype(jnp.float32)
    return total


def middle_kernel(s0, s1, s2, s3, token_ref, gains_ref, middle_ref, in_ref):
    middle = token_ref[...].astype(jnp.float32) + total_of((s0, s1, s2, s3))
    middle_ref[...] = middle
    scale = lax.rsqrt(jnp.mean(middle * middle, axis=-1, keepdims=True) + epsilon)
    in_ref[...] = (middle * scale * gains_ref[2:3, :]).astype(jnp.bfloat16)


def norm_back(row, grad, value, gains_ref, first):
    scale = lax.rsqrt(jnp.mean(value * value, axis=-1, keepdims=True) + epsilon)
    scaled = grad * gains_ref[row : row + 1, :]
    mean = jnp.mean(scaled * value, axis=-1, keepdims=True)
    return first + (scale * scaled - value * (scale * scale * scale) * mean)


def middle_back_kernel(
    s0, s1, s2, s3, middle_ref, cot_ref, gains_ref, grad_ref, branch_ref, gain_ref
):
    value = middle_ref[...]
    total = total_of((s0, s1, s2, s3))
    grad = norm_back(2, total, value, gains_ref, cot_ref[...].astype(jnp.float32))
    grad_ref[...] = grad
    branch_ref[...] = grad.astype(jnp.bfloat16)
    scale = lax.rsqrt(jnp.mean(value * value, axis=-1, keepdims=True) + epsilon)
    gain_ref[...] = fold_rows(total * value * scale)


def input_back_kernel(s0, s1, s2, s3, token_ref, middle_ref, gains_ref, grad_ref):
    token = token_ref[...].astype(jnp.float32)
    grad_ref[...] = norm_back(
        0, total_of((s0, s1, s2, s3)), token, gains_ref, middle_ref[...]
    ).astype(jnp.bfloat16)


def output_kernel(s0, s1, s2, s3, middle_ref, out_ref):
    out_ref[...] = (middle_ref[...] + total_of((s0, s1, s2, s3))).astype(jnp.bfloat16)


def conv_tables(kernel):
    heads = kernel.shape[0]
    u = iota((2 * LANES, CQ * LANES), 0)
    j = iota((2 * LANES, CQ * LANES), 1) % LANES
    table = jnp.zeros((heads, 2 * LANES, CQ * LANES), jnp.float32)
    for b in range(CK):
        taps = jnp.repeat(kernel[:, :, b], LANES, axis=1)
        table = jnp.where((j - u + CK - 1 == b)[None], taps[:, None, :], table)
    return halves(table)


FLAT = ("seq", "wide")


def swapped(value, flip):
    total = lax.axis_size("seq") * lax.axis_size("wide")
    return lax.ppermute(value, FLAT, [(i, i ^ flip) for i in range(total)])


class Place:
    def __init__(self):
        self.wide_count = lax.axis_size("wide")
        self.depth = self.wide_count // 2
        self.seq = lax.axis_index("seq")
        wide = lax.axis_index("wide")
        self.y = wide % 2
        self.z = wide // 2
        self.plane = 2 * self.seq + self.y
        self.x_flip = 2 * self.wide_count
        self.core_flip = self.wide_count
        self.y_flip = 1
        self.chip_flips = (self.x_flip, self.y_flip, self.x_flip | self.y_flip)
        seqs = range(lax.axis_size("seq"))
        self.plane_groups = [
            [s * self.wide_count + z * 2 + y for s in seqs for y in range(2)] for z in range(self.depth)
        ]
        self.line_groups = [[z * 2 + y for z in range(self.depth)] for y in range(2)]


def chip_gather(place, value):
    return [value] + [swapped(value, flip) for flip in place.chip_flips]


def core_gather(place, near):
    return near + [swapped(part, place.core_flip) for part in near]


def plane_gather(place, value):
    return core_gather(place, chip_gather(place, value))


def plane_terms(place, near, far, weight, other, transposed, name, tokens=None, got=None):
    width = weight.shape[0] if transposed else weight.shape[1]
    flat = (BLOCK, width)
    if got is None:
        got = swapped(far, place.core_flip)
    return list(
        kernel_call(
            functools.partial(pair_kernel, transposed) if tokens is None else pair_gain_kernel,
            name,
            [shape_of(flat, jnp.float32)]
            + [shape_of(flat)] * 3
            + ([] if tokens is None else [shape_of((8, width), jnp.float32)]),
            (near, got, weight, other) + (tokens or ()),
            flops=16 * BLOCK * weight.size,
            vmem=24,
            lazy=2 + len(tokens or ()),
        )
    )


def chip_scatter(place, terms):
    return [terms[0]] + [
        swapped(part, flip) for part, flip in zip(terms[1:], place.chip_flips)
    ]


def line_gather(place, value):
    return lax.all_gather(value, "wide", axis=0, axis_index_groups=place.line_groups)


def line_scatter(place, blocks):
    return lax.psum_scatter(
        blocks, "wide", scatter_dimension=0, axis_index_groups=place.line_groups
    )


def plane_exchange(place, blocks):
    return lax.all_to_all(blocks, FLAT, 0, 0, axis_index_groups=place.plane_groups)


def out_pairs(place):
    return [
        (s * place.wide_count + 4 * y + z, s * place.wide_count + 2 * z + y)
        for s in range(lax.axis_size("seq"))
        for z in range(place.depth)
        for y in range(2)
    ]


def spread_tables():
    target = iota((4 * LANES, 3 * GROUP * LANES), 1)
    column = target // LANES * HEAD_DIM + target % LANES
    real = target % LANES < HEAD_DIM
    source = iota(target.shape, 0)
    main = jnp.where(real & (column == source), 1.0, 0.0).astype(jnp.bfloat16)
    source, column, real = source[:LANES], column[:LANES], real[:LANES]
    rest = [
        jnp.where(
            real & (column >= 4 * LANES) & (column - 4 * LANES + side * (LANES // 2) == source), 1.0, 0.0
        ).astype(jnp.bfloat16)
        for side in range(2)
    ]
    return main, jnp.stack(rest)


def after(done, *values):
    return lax.optimization_barrier((done,) + values)[1:]


def plane_shards(
    tokens, segments, w_query, w_key, w_value, w_out, gain_attn, gain_group, gain_ffn,
    conv_kernel, head_mix, w_gate, w_up, w_down, cotangent,
):
    place = Place()
    seq_count = lax.axis_size("seq")
    depth = place.depth
    count = tokens.shape[1]
    length = count * seq_count
    width = tokens.shape[2]
    slab = w_query.shape[0]
    blocks = length // BLOCK
    reach = (length // 2 - 1) // BLOCK + 1
    lanes = GROUP * LANES
    cols = GROUP * HEAD_DIM
    bf16 = jnp.bfloat16
    f32 = jnp.float32
    at = jnp.stack([place.plane, place.z, place.y]).astype(jnp.int32)
    own_tokens = tokens[0]
    own_cot = cotangent[0]

    gains_own = jnp.stack([gain_attn, gain_group, gain_ffn]).astype(bf16)
    gains_own = jnp.pad(gains_own, ((0, 5), (0, LANES - slab)))
    pack_rows = 4 * slab + slab // 2 + 8
    out_rows = width // LANES * slab
    packed, w_out_rows = kernel_call(
        functools.partial(pack_kernel, slab),
        "pack_projections",
        [shape_of((8, pack_rows, LANES)), shape_of((out_rows, LANES))],
        (gains_own, w_query, w_key, w_value, w_out),
        vmem=16,
        lazy=4,
    )
    sub = w_gate.shape[1] // seq_count
    deep = w_gate.shape[0]
    packed, own_tokens, w_out_rows, segments, conv_kernel, w_gate, w_up, w_down = (
        lax.optimization_barrier(
            (packed, own_tokens, w_out_rows, segments, conv_kernel, w_gate, w_up, w_down)
        )
    )
    w_out_rows = lax.ppermute(w_out_rows, FLAT, out_pairs(place))
    packed = plane_exchange(place, packed)
    (ffn_own,) = kernel_call(
        functools.partial(pack_hidden_kernel, sub),
        "pack_hidden",
        [shape_of((seq_count, 3, deep, sub))],
        (w_gate, w_up, w_down),
        vmem=16,
    )
    token_near = chip_gather(place, own_tokens)
    packed, ffn_own, own_cot = lax.optimization_barrier((packed, ffn_own, own_cot))
    w_all = line_gather(
        place, jnp.concatenate([packed.reshape(8 * pack_rows, LANES), w_out_rows])
    )
    ffn_own = lax.all_to_all(ffn_own, "seq", 0, 0)
    cot_near = chip_gather(place, own_cot)
    token_parts = core_gather(place, token_near)

    other_row = swapped(segments, place.y_flip)
    seg = jnp.where(
        place.y == 0,
        jnp.concatenate([segments, other_row]),
        jnp.concatenate([other_row, segments]),
    )
    starts = jnp.sum(seg[:, None, :] < seg[:, :, None], axis=-1, dtype=jnp.int32)
    stops = jnp.sum(seg[:, None, :] <= seg[:, :, None], axis=-1, dtype=jnp.int32)
    starts = jnp.broadcast_to(starts[:, :, None], (2, length, LANES))
    stops = jnp.broadcast_to(stops[:, :, None], (2, length, LANES))
    taps = lax.dynamic_slice_in_dim(conv_kernel, place.plane * GROUP, GROUP)
    mix = lax.dynamic_slice_in_dim(head_mix, place.plane * GROUP, GROUP)
    table_high, table_low = conv_tables(taps)
    spread_main, spread_rest = spread_tables()

    ffn_w = line_gather(place, ffn_own)
    units = depth * sub
    w_all, starts, stops, *cot_near = lax.optimization_barrier(
        (w_all, starts, stops, *cot_near)
    )
    (w_out_heads,) = kernel_call(
        functools.partial(out_rows_kernel, slab),
        "out_rows",
        [shape_of((lanes, width))],
        (w_all,),
        vmem=16,
    )
    w_out_other = swapped(w_out_heads, place.core_flip)
    cot_parts = core_gather(place, cot_near)

    padded = length + LANES
    half = 4 * count
    (
        normed, w_wide, queries, keys, values, probs, high, attended, grouped_near, grouped_far,
        gains, gain_heads,
    ) = kernel_call(
        functools.partial(forward_kernel, blocks, reach, slab),
        "attention_forward",
        [
            shape_of((8 * count, width)),
            shape_of((width, 3 * lanes)),
            shape_of((2, length, lanes)),
            shape_of((2, padded, lanes)),
            shape_of((2, length, lanes)),
            shape_of((2, GROUP, length, (reach + 1) * LANES), f32),
            shape_of((2, GROUP, RIM + length, padded)),
            shape_of((2, length, lanes), f32),
            shape_of((half, lanes)),
            shape_of((half, lanes)),
            shape_of((8, width), f32),
            shape_of((1, lanes), f32),
        ],
        (
            at, mix, w_all, *token_parts, starts, table_high, table_low, spread_main, spread_rest,
        ),
        [
            pltpu.VMEM((2, length, lanes), bf16),
            pltpu.VMEM((2, length, lanes), f32),
            pltpu.VMEM((GROUP, RIM + length, padded), bf16),
            pltpu.VMEM((CQ, RIM + BLOCK, LANES), f32),
        ],
        flops=25 * 10**9,
        smem=2,
    )
    w_wide_other = swapped(w_wide, place.core_flip)
    grouped_near, *cot_parts[4:] = lax.optimization_barrier((grouped_near, *cot_parts[4:]))
    terms = chip_scatter(
        place,
        plane_terms(place, grouped_near, grouped_far, w_out_heads, w_out_other, False, "branch"),
    )
    flat = (count, width)
    middle, ffn_in = kernel_call(
        middle_kernel,
        "middle",
        [shape_of(flat, f32), shape_of(flat)],
        (*terms, own_tokens, gains),
        vmem=16,
    )

    ffn_parts = plane_gather(place, ffn_in)
    ffn_w, *ffn_parts[1:4] = lax.optimization_barrier((ffn_w, *ffn_parts[1:4]))
    w_gate_up, w_down_all = kernel_call(
        functools.partial(assemble_kernel, sub),
        "assemble_feed_forward",
        [shape_of((width, 2 * units)), shape_of((units, width))],
        (ffn_w,),
        vmem=24,
    )
    *ffn_parts[4:], w_gate_up, w_down_all = lax.optimization_barrier(
        (*ffn_parts[4:], w_gate_up, w_down_all)
    )
    gate_up_other = swapped(w_gate_up, place.core_flip)
    down_other = swapped(w_down_all, place.core_flip)
    hidden_near, hidden_far, grad_near, grad_far = kernel_call(
        hidden_kernel,
        "feed_forward",
        [
            shape_of((half, units)),
            shape_of((half, units)),
            shape_of((half, 2 * units)),
            shape_of((half, 2 * units)),
        ],
        (*ffn_parts, *cot_parts, w_gate_up, w_down_all),
        flops=10 * 10**9,
        vmem=26,
    )
    grad_got = swapped(grad_far, place.core_flip)
    grad_got, gate_up_other, hidden_near, hidden_far, grad_near, grad_far = (
        lax.optimization_barrier(
            (grad_got, gate_up_other, hidden_near, hidden_far, grad_near, grad_far)
        )
    )
    (ffn_g,) = kernel_call(
        functools.partial(hidden_grad_kernel, sub),
        "feed_forward_weights",
        [shape_of((depth, seq_count, 3, deep, sub))],
        (hidden_near, hidden_far, grad_near, grad_far, *ffn_parts, *cot_parts),
        [
            pltpu.VMEM((8 * count, width), bf16),
            pltpu.VMEM((8 * count, width), bf16),
            pltpu.SemaphoreType.DMA((16,)),
        ],
        hbm=16,
        flops=5 * 10**9,
        vmem=26,
    )
    ffn_g, grad_near = lax.optimization_barrier((ffn_g, grad_near))
    ffn_g = line_scatter(place, ffn_g)
    terms = plane_terms(
        place, grad_near, grad_far, w_gate_up, gate_up_other, True, "feed_forward_back",
        got=grad_got,
    )
    terms = chip_scatter(place, terms)
    grad_middle, grad_branch, gain_ffn_sum = kernel_call(
        middle_back_kernel,
        "middle_back",
        [shape_of(flat, f32), shape_of(flat), shape_of((8, width), f32)],
        (*terms, middle, own_cot, gains),
        vmem=16,
    )
    ffn_g = lax.all_to_all(ffn_g, "seq", 0, 0)

    branch_near = chip_gather(place, grad_branch)
    hidden_near, hidden_far = after(grad_branch, hidden_near, hidden_far)
    out_terms = plane_terms(
        place, hidden_near, hidden_far, w_down_all, down_other, False, "feed_forward_out"
    )
    held = lax.optimization_barrier((*branch_near, *out_terms))
    branch_near, out_terms = list(held[:4]), list(held[4:])
    branch_parts = core_gather(place, branch_near)
    out_terms = chip_scatter(place, out_terms)
    dqkv_near, dqkv_far, grad_taps, grad_mix, grad_gain_group = kernel_call(
        functools.partial(backward_kernel, blocks, reach),
        "attention_backward",
        [
            shape_of((half, 3 * lanes)),
            shape_of((half, 3 * lanes)),
            shape_of((GROUP, 16, CQ * LANES), f32),
            shape_of((GROUP * GROUP, 8, LANES), f32),
            shape_of((8, lanes), f32),
        ],
        (
            at, mix, *branch_parts, w_out_heads, gain_heads,
            attended, values, probs, starts, stops, table_high, high, keys, queries,
        ),
        [
            pltpu.VMEM((2, length, lanes), f32),
            pltpu.VMEM((2, length, 3 * lanes), bf16),
            pltpu.VMEM((GROUP, blocks, length + 8, LANES), f32),
            pltpu.VMEM((GROUP, 2 * LANES, CQ * LANES), f32),
            pltpu.VMEM((GROUP, padded, LANES), f32),
            pltpu.VMEM((length, lanes), f32),
        ],
        flops=30 * 10**9,
        smem=2,
        vmem=34,
        lazy=9,
    )
    dqkv_near, dqkv_far, *out_terms = lax.optimization_barrier(
        (dqkv_near, dqkv_far, *out_terms)
    )
    (table,) = kernel_call(
        functools.partial(weight_grads_kernel, slab),
        "attention_weights",
        [shape_of((depth, 8 * pack_rows + out_rows, LANES))],
        (
            dqkv_near, dqkv_far, *branch_parts,
            grouped_near, grouped_far, spread_main, spread_rest, normed,
        ),
        flops=5 * 10**9,
        vmem=36,
        lazy=5,
    )
    table, dqkv_near = lax.optimization_barrier((table, dqkv_near))
    table = line_scatter(place, table)
    *terms, gain_attn_sum = plane_terms(
        place, dqkv_near, dqkv_far, w_wide, w_wide_other, True, "project_back",
        tuple(token_parts[:4]),
    )
    (small,) = kernel_call(
        small_kernel,
        "small_sums",
        [shape_of((2 * (width // LANES) + 2 * HEADS, LANES), f32)],
        (at, gain_attn_sum, gain_ffn_sum, grad_taps, grad_mix, grad_gain_group),
        smem=1,
        vmem=16,
    )
    terms = chip_scatter(place, terms)
    for flip in (place.core_flip, 2, 4, place.y_flip, place.x_flip):
        small = small + swapped(small, flip)
    (grad_tokens,) = kernel_call(
        input_back_kernel,
        "input_back",
        [shape_of(flat)],
        (*terms, own_tokens, grad_middle, gains),
        vmem=16,
    )
    (output,) = kernel_call(
        output_kernel, "output", [shape_of(flat)], (*out_terms, middle), vmem=16
    )
    grad_w_gate, grad_w_up, grad_w_down = kernel_call(
        functools.partial(unpack_hidden_kernel, sub),
        "unpack_hidden",
        [
            shape_of((deep, seq_count * sub), f32),
            shape_of((deep, seq_count * sub), f32),
            shape_of((seq_count * sub, deep), f32),
        ],
        (ffn_g,),
        vmem=16,
    )
    output, grad_w_gate, grad_tokens, small, table = lax.optimization_barrier(
        (output, grad_w_gate, grad_tokens, small, table)
    )
    back = [(target, source) for source, target in out_pairs(place)]
    out_table = lax.ppermute(table[8 * pack_rows :], FLAT, back)
    table = plane_exchange(place, table[: 8 * pack_rows].reshape(8, pack_rows, LANES))
    grad_rows = kernel_call(
        functools.partial(unpack_kernel, slab),
        "unpack_projections",
        [shape_of((slab, width), f32)] * 4,
        (table, out_table),
        vmem=16,
    )
    small_flat = small.reshape(-1)
    row = (place.seq * place.wide_count + lax.axis_index("wide")) * slab
    tiles = width // LANES
    gain_grads = [lax.dynamic_slice_in_dim(small_flat, i * width + row, slab) for i in range(2)]
    head, side = row // HEAD_DIM, row % HEAD_DIM
    gain_grads.append(
        lax.dynamic_slice_in_dim(small_flat, (2 * tiles + head) * LANES + side, slab)
    )
    heads = small[2 * tiles + HEADS :]
    grad_conv = heads[:, : 16 * CQ].reshape(HEADS, CQ, 16)[:, :, :CK]
    grad_head_mix = heads[:, 16 * CQ : 16 * CQ + GROUP]
    return (
        output[None],
        grad_tokens[None],
        grad_rows[0],
        grad_rows[1],
        grad_rows[2],
        grad_rows[3],
        gain_grads[0],
        gain_grads[2],
        gain_grads[1],
        grad_conv,
        grad_head_mix,
        grad_w_gate,
        grad_w_up,
        grad_w_down,
    )


def solution(mesh):
    planes = mesh.shape["seq"] == 4 and mesh.shape["wide"] == 8
    return jax.shard_map(
        plane_shards if planes else shards,
        mesh=mesh,
        in_specs=(
            P("wide", "seq", None),
            P("wide", None),
            P(("seq", "wide"), None),
            P(("seq", "wide"), None),
            P(("seq", "wide"), None),
            P(("seq", "wide"), None),
            P(("seq", "wide")),
            P(("seq", "wide")),
            P(("seq", "wide")),
            P(),
            P(),
            P("seq", "wide"),
            P("seq", "wide"),
            P("wide", "seq"),
            P("wide", "seq", None),
        ),
        out_specs=(
            P("wide", "seq", None),
            P("wide", "seq", None),
            P(("seq", "wide"), None),
            P(("seq", "wide"), None),
            P(("seq", "wide"), None),
            P(("seq", "wide"), None),
            P(("seq", "wide")),
            P(("seq", "wide")),
            P(("seq", "wide")),
            P(),
            P(),
            P("seq", "wide"),
            P("seq", "wide"),
            P("wide", "seq"),
        ),
        check_vma=False,
    )
```

```python
import functools

import jax
import jax.numpy as jnp
from jax import lax
from jax.experimental import pallas as pl
from jax.experimental.pallas import tpu as pltpu
from jax.sharding import PartitionSpec as P

HEADS = 16
HEAD_DIM = 96
CQ = 6
CK = 11
GROUP = 2
LANES = 128
BLOCK = 128
RIM = 16


precise = lax.Precision.HIGHEST
epsilon = 1e-05


def passed_along(value, axis, by):
    devices = lax.axis_size(axis)
    pairs = [(i, i + by) for i in range(devices) if 0 <= i + by < devices]
    return lax.ppermute(value, axis, pairs)


def extended(block, sides, width):
    for axis, dim in sides:
        count = lax.axis_size(axis)
        forward = [(i, i + 1) for i in range(count - 1)]
        backward = [(target, source) for source, target in forward]
        low = lax.ppermute(
            lax.slice_in_dim(block, block.shape[dim] - width, None, axis=dim), axis, forward
        )
        high = lax.ppermute(lax.slice_in_dim(block, 0, width, axis=dim), axis, backward)
        block = jnp.concatenate([low, block, high], axis=dim)
    return block


def rms_scaled(values, gain_vec):
    return (
        values * lax.rsqrt(jnp.mean(values * values, axis=-1, keepdims=True) + epsilon) * gain_vec
    )


def group_scaled(values, gain_vec):
    center = values - jnp.mean(values, axis=-1, keepdims=True)
    spread = jnp.mean(center * center, axis=-1, keepdims=True)
    return center * lax.rsqrt(spread + epsilon) * gain_vec


def tile_masks(seg_query, pos_query, seg_key, pos_key, valid_flag):
    query_rim = CQ - 1
    key_rim = CK // 2
    allowed = (
        (seg_query[:, None] == seg_key[None, :])
        & (pos_key[None, :] <= pos_query[:, None])
        & valid_flag
    )
    row_count = seg_query.shape[0] - query_rim
    row_masks = jnp.stack(
        [
            (
                seg_query[query_rim - shift_q : query_rim - shift_q + row_count]
                == seg_query[query_rim:]
            ).astype(jnp.float32)
            for shift_q in range(CQ)
        ]
    )
    final_mask = allowed[query_rim:, key_rim : key_rim + row_count]
    return (allowed, row_masks, final_mask)


def convolve(scores, allowed, row_masks, kernel):
    query_rim = CQ - 1
    key_rim = CK // 2
    row_count = scores.shape[1] - query_rim
    col_count = scores.shape[2] - 2 * key_rim
    masked = jnp.where(allowed[None], scores, 0.0)
    summed = jnp.zeros((scores.shape[0], row_count, col_count), jnp.float32)
    for shift_q in range(CQ):
        inner_sum = jnp.zeros((scores.shape[0], row_count, col_count), jnp.float32)
        for shift_k in range(CK):
            piece_view = masked[
                :,
                query_rim - shift_q : query_rim - shift_q + row_count,
                2 * key_rim - shift_k : 2 * key_rim - shift_k + col_count,
            ]
            inner_sum = inner_sum + kernel[:, shift_q, shift_k][:, None, None] * piece_view
        summed = summed + row_masks[shift_q][None, :, None] * inner_sum
    return summed


def mix_heads(probs, head_mix):
    lead_dims = probs.shape[:-3]
    tail_dims = probs.shape[-2:]
    grouped = probs.reshape(lead_dims + (HEADS // GROUP, GROUP) + tail_dims)
    mixing = head_mix.reshape(HEADS // GROUP, GROUP, GROUP)
    summed = jnp.zeros(lead_dims + (HEADS // GROUP, GROUP) + tail_dims, jnp.float32)
    for source in range(GROUP):
        summed = summed + mixing[:, :, source][:, :, None, None] * jnp.expand_dims(
            grouped[..., :, source, :, :], -3
        )
    return summed.reshape(probs.shape)


def unmix_heads(grads, head_mix):
    lead_dims = grads.shape[:-3]
    tail_dims = grads.shape[-2:]
    grouped = grads.reshape(lead_dims + (HEADS // GROUP, GROUP) + tail_dims)
    mixing = head_mix.reshape(HEADS // GROUP, GROUP, GROUP)
    summed = jnp.zeros(lead_dims + (HEADS // GROUP, GROUP) + tail_dims, jnp.float32)
    for target in range(GROUP):
        summed = summed + mixing[:, target, :][:, :, None, None] * jnp.expand_dims(
            grouped[..., :, target, :, :], -3
        )
    return summed.reshape(grads.shape)


def contract(left_op, right_op, left_dim, right_dim):
    return lax.dot_general(
        left_op,
        right_op,
        (((left_dim,), (right_dim,)), ((), ())),
        preferred_element_type=jnp.float32,
    )


def gather_attention(w_query, w_key, w_value, w_out, gain_attn, gain_group, gain_ffn):
    return (
        lax.all_gather(w_query.astype(jnp.bfloat16), ("seq", "wide"), axis=0, tiled=True),
        lax.all_gather(w_key.astype(jnp.bfloat16), ("seq", "wide"), axis=0, tiled=True),
        lax.all_gather(w_value.astype(jnp.bfloat16), ("seq", "wide"), axis=0, tiled=True),
        lax.all_gather(w_out.astype(jnp.bfloat16), ("seq", "wide"), axis=0, tiled=True),
        lax.all_gather(gain_attn.astype(jnp.bfloat16), ("seq", "wide"), axis=0, tiled=True),
        lax.all_gather(gain_group.astype(jnp.bfloat16), ("seq", "wide"), axis=0, tiled=True),
        lax.all_gather(gain_ffn.astype(jnp.bfloat16), ("seq", "wide"), axis=0, tiled=True),
    )


def collect_packets(own, reach_len):
    stored = jnp.zeros((reach_len,) + own.shape, own.dtype).at[0].set(own)

    def advance(turn_index, state_pair):
        packet, stored_now = state_pair
        packet = passed_along(packet, "seq", 1)
        return (packet, lax.dynamic_update_index_in_dim(stored_now, packet, turn_index, 0))

    return lax.fori_loop(1, reach_len, advance, (own, stored))[1]


def tile_logits(query_ext, packet, seg_query, pos_query, seg_key_pad, other_shard, token_count):
    key_rim = CK // 2
    key_ext = packet[: token_count + 2 * key_rim].reshape(
        token_count + 2 * key_rim, HEADS, HEAD_DIM
    )
    scores = jnp.einsum(
        "qhe,khe->hqk", query_ext, key_ext, preferred_element_type=jnp.float32
    ) * HEAD_DIM ** (-0.5)
    key_start = other_shard * token_count
    seg_key = lax.dynamic_slice_in_dim(
        seg_key_pad, jnp.maximum(key_start, 0), token_count + 2 * key_rim
    )
    pos_key = key_start - key_rim + jnp.arange(token_count + 2 * key_rim, dtype=jnp.int32)
    allowed, row_masks, final_mask = tile_masks(
        seg_query, pos_query, seg_key, pos_key, other_shard >= 0
    )
    return (scores, allowed, row_masks, final_mask, key_ext)


def shards(
    tokens,
    segments,
    w_query,
    w_key,
    w_value,
    w_out,
    gain_attn,
    gain_group,
    gain_ffn,
    conv_kernel,
    head_mix,
    w_gate,
    w_up,
    w_down,
    cotangent,
):
    token_count = tokens.shape[1]
    query_rim = CQ - 1
    key_rim = CK // 2
    width_all = HEADS * HEAD_DIM
    scaling = HEAD_DIM ** (-0.5)
    seq_count = lax.axis_size("seq")
    longest_doc = min(1024, token_count * seq_count // 2)
    reach_len = min(seq_count - 1, (longest_doc - 1) // token_count + 1) + 1
    seq_index = lax.axis_index("seq")
    row_start = seq_index * token_count
    seg_row = segments[0]
    seg_query_pad = jnp.concatenate([jnp.full((query_rim,), -1, jnp.int32), seg_row])
    seg_key_pad = jnp.concatenate(
        [jnp.full((key_rim,), -2, jnp.int32), seg_row, jnp.full((key_rim,), -2, jnp.int32)]
    )
    seg_query = lax.dynamic_slice_in_dim(seg_query_pad, row_start, token_count + query_rim)
    pos_query = row_start - query_rim + jnp.arange(token_count + query_rim, dtype=jnp.int32)
    weights = gather_attention(w_query, w_key, w_value, w_out, gain_attn, gain_group, gain_ffn)
    query_mat, key_mat, value_mat, out_mat, gain_one, gain_mid, gain_two = weights
    inputs = tokens[0].astype(jnp.float32)
    gain_first = gain_one.astype(jnp.float32)
    normed = rms_scaled(inputs, gain_first).astype(jnp.bfloat16)
    queries = jnp.dot(normed, query_mat, preferred_element_type=jnp.float32).astype(jnp.bfloat16)
    keys_loc = jnp.dot(normed, key_mat, preferred_element_type=jnp.float32).astype(jnp.bfloat16)
    values_loc = jnp.dot(normed, value_mat, preferred_element_type=jnp.float32).astype(jnp.bfloat16)
    rimmed = extended(jnp.stack([queries, keys_loc]), (("seq", 1),), key_rim)
    query_ext = rimmed[0, : token_count + query_rim].reshape(
        token_count + query_rim, HEADS, HEAD_DIM
    )
    own = jnp.concatenate([rimmed[1], values_loc], axis=0)
    packets = collect_packets(own, reach_len)

    def all_logits(packet_stack):

        def logits_of(turn_index):
            packet = lax.dynamic_index_in_dim(packet_stack, turn_index, 0, keepdims=False)
            scores, allowed, row_masks, final_mask, key_ext = tile_logits(
                query_ext,
                packet,
                seg_query,
                pos_query,
                seg_key_pad,
                seq_index - turn_index,
                token_count,
            )
            return jnp.where(
                final_mask[None], convolve(scores, allowed, row_masks, conv_kernel), -jnp.inf
            )

        return lax.map(logits_of, jnp.arange(reach_len, dtype=jnp.int32))

    logits = all_logits(packets)
    peak_val = jnp.max(logits, axis=(0, 3))
    log_total = peak_val + jnp.log(
        jnp.sum(jnp.exp(logits - peak_val[None, :, :, None]), axis=(0, 3))
    )
    probs_all = jnp.exp(logits - log_total[None, :, :, None])
    mixed_b = mix_heads(probs_all, head_mix).astype(jnp.bfloat16)
    values_all = packets[:, token_count + 2 * key_rim :].reshape(
        reach_len, token_count, HEADS, HEAD_DIM
    )
    attended = jnp.einsum("rhtk,rkhe->the", mixed_b, values_all, preferred_element_type=jnp.float32)
    gain_middle = gain_mid.astype(jnp.float32).reshape(HEADS, HEAD_DIM)
    grouped = (
        group_scaled(attended, gain_middle).reshape(token_count, width_all).astype(jnp.bfloat16)
    )
    middle = inputs + jnp.dot(grouped, out_mat, preferred_element_type=jnp.float32)
    gain_second = gain_two.astype(jnp.float32)
    ffn_in = rms_scaled(middle, gain_second).astype(jnp.bfloat16)
    ffn_all = lax.all_gather(ffn_in, "wide", axis=0, tiled=True)
    gate_mat, up_mat, down_mat = (
        lax.all_gather(w_gate.astype(jnp.bfloat16), "seq", axis=0, tiled=True),
        lax.all_gather(w_up.astype(jnp.bfloat16), "seq", axis=0, tiled=True),
        lax.all_gather(w_down.astype(jnp.bfloat16), "seq", axis=1, tiled=True),
    )
    gate_val = jnp.dot(ffn_all, gate_mat, preferred_element_type=jnp.float32)
    up_val = jnp.dot(ffn_all, up_mat, preferred_element_type=jnp.float32)
    hidden = (jax.nn.silu(gate_val) * up_val).astype(jnp.bfloat16)
    ffn_out = lax.psum_scatter(
        jnp.dot(hidden, down_mat, preferred_element_type=jnp.float32).astype(jnp.bfloat16),
        "wide",
        scatter_dimension=0,
        tiled=True,
    ).astype(jnp.float32)
    output = (middle + ffn_out).astype(jnp.bfloat16)
    grad_out = cotangent[0]
    grad_all = lax.all_gather(grad_out, "wide", axis=0, tiled=True)
    grad_hidden = contract(grad_all, down_mat, 1, 1)
    grad_down = contract(hidden, grad_all, 0, 0)
    sig_gate = jax.nn.sigmoid(gate_val)
    grad_gate = (grad_hidden * up_val * sig_gate * (1.0 + gate_val * (1.0 - sig_gate))).astype(
        jnp.bfloat16
    )
    grad_up = (grad_hidden * gate_val * sig_gate).astype(jnp.bfloat16)
    grad_gate_w = contract(ffn_all, grad_gate, 0, 0)
    grad_up_w = contract(ffn_all, grad_up, 0, 0)
    grad_ffn_in = lax.psum_scatter(
        (contract(grad_gate, gate_mat, 1, 1) + contract(grad_up, up_mat, 1, 1)).astype(
            jnp.bfloat16
        ),
        "wide",
        scatter_dimension=0,
        tiled=True,
    ).astype(jnp.float32)
    ffn_grads = (
        lax.psum_scatter(
            grad_gate_w.astype(jnp.bfloat16), "seq", scatter_dimension=0, tiled=True
        ).astype(jnp.float32),
        lax.psum_scatter(
            grad_up_w.astype(jnp.bfloat16), "seq", scatter_dimension=0, tiled=True
        ).astype(jnp.float32),
        lax.psum_scatter(
            grad_down.astype(jnp.bfloat16), "seq", scatter_dimension=1, tiled=True
        ).astype(jnp.float32),
    )
    norm_two_back = jax.vjp(rms_scaled, middle, gain_second)[1]
    grad_mid_part, grad_gain_two = norm_two_back(grad_ffn_in)
    grad_middle = grad_out.astype(jnp.float32) + grad_mid_part
    grad_branch = grad_middle.astype(jnp.bfloat16)
    back_weights = gather_attention(w_query, w_key, w_value, w_out, gain_attn, gain_group, gain_ffn)
    query_back, key_back, value_back, out_back = (
        back_weights[0],
        back_weights[1],
        back_weights[2],
        back_weights[3],
    )
    grad_grouped = contract(grad_branch, out_back, 1, 1)
    grad_out_w = contract(grouped, grad_branch, 0, 0)
    group_back = jax.vjp(group_scaled, attended, gain_middle)[1]
    grad_attended, grad_gain_mid = group_back(grad_grouped.reshape(token_count, HEADS, HEAD_DIM))
    grad_att_b = grad_attended.astype(jnp.bfloat16)
    back_packets = collect_packets(own, reach_len)
    logits_again = all_logits(back_packets)
    probs_again = jnp.exp(logits_again - log_total[None, :, :, None])
    mixed_again = mix_heads(probs_again, head_mix).astype(jnp.bfloat16)
    values_back = back_packets[:, token_count + 2 * key_rim :].reshape(
        reach_len, token_count, HEADS, HEAD_DIM
    )
    grad_mixed = jnp.einsum(
        "the,rkhe->rhtk", grad_att_b, values_back, preferred_element_type=jnp.float32
    )
    grad_values = jnp.einsum(
        "rhtk,the->rkhe", mixed_again, grad_att_b, preferred_element_type=jnp.float32
    ).reshape(reach_len, token_count, width_all)
    probs_grouped = probs_again.reshape(reach_len, HEADS // GROUP, GROUP, token_count, token_count)
    mixed_grouped = grad_mixed.reshape(reach_len, HEADS // GROUP, GROUP, token_count, token_count)
    grad_mix = jnp.einsum(
        "rgdtk,rgctk->gcd", probs_grouped, mixed_grouped, precision=precise
    ).reshape(HEADS, GROUP)
    grad_probs = unmix_heads(grad_mixed, head_mix)
    delta_row = jnp.sum(probs_again * grad_probs, axis=(0, 3))
    grad_logits = probs_again * (grad_probs - delta_row[None, :, :, None])

    def tile_grads(turn_index):
        packet = lax.dynamic_index_in_dim(back_packets, turn_index, 0, keepdims=False)
        scores, allowed, row_masks, final_mask, key_ext = tile_logits(
            query_ext,
            packet,
            seg_query,
            pos_query,
            seg_key_pad,
            seq_index - turn_index,
            token_count,
        )
        conv_back = jax.vjp(
            lambda field, weights_k: convolve(field, allowed, row_masks, weights_k),
            scores,
            conv_kernel,
        )[1]
        grad_scores, grad_kernel = conv_back(
            lax.dynamic_index_in_dim(grad_logits, turn_index, 0, keepdims=False)
        )
        grad_scores_b = grad_scores.astype(jnp.bfloat16)
        grad_query_ext = (
            jnp.einsum("hqk,khe->qhe", grad_scores_b, key_ext, preferred_element_type=jnp.float32)
            * scaling
        )
        grad_key_ext = (
            jnp.einsum("hqk,qhe->khe", grad_scores_b, query_ext, preferred_element_type=jnp.float32)
            * scaling
        )
        cycle_term = jnp.concatenate(
            [
                grad_key_ext.reshape(token_count + 2 * key_rim, width_all),
                lax.dynamic_index_in_dim(grad_values, turn_index, 0, keepdims=False),
            ],
            axis=0,
        )
        return (cycle_term, grad_query_ext, grad_kernel)

    start_term, start_query, start_kernel = tile_grads(reach_len - 1)

    def descend(turn_index, state_all):
        cycle_acc, query_acc, kernel_acc = state_all
        cycle_term, query_part, kernel_part = tile_grads(reach_len - 1 - turn_index)
        moved_acc = passed_along(cycle_acc.astype(jnp.bfloat16), "seq", -1).astype(cycle_acc.dtype)
        return (moved_acc + cycle_term, query_acc + query_part, kernel_acc + kernel_part)

    cycle_acc, query_acc, kernel_acc = lax.fori_loop(
        1, reach_len, descend, (start_term, start_query, start_kernel)
    )
    query_flat = query_acc.reshape(token_count + query_rim, width_all)
    key_ext_grad = cycle_acc[: token_count + 2 * key_rim]
    grad_values_own = cycle_acc[token_count + 2 * key_rim :]
    edge_grads = jnp.stack(
        [
            jnp.concatenate([query_flat[:query_rim], jnp.zeros((key_rim, width_all), jnp.float32)]),
            jnp.concatenate([key_ext_grad[:key_rim], key_ext_grad[token_count + key_rim :]]),
        ]
    )
    rim_back = extended(edge_grads.astype(jnp.bfloat16), (("seq", 1),), key_rim).astype(
        edge_grads.dtype
    )
    grad_queries = (
        query_flat[query_rim:].at[token_count - key_rim :].add(rim_back[0, 3 * key_rim :])
    )
    grad_keys = (
        key_ext_grad[key_rim : key_rim + token_count]
        .at[:key_rim]
        .add(rim_back[1, :key_rim])
        .at[token_count - key_rim :]
        .add(rim_back[1, 3 * key_rim :])
    )
    grad_query_b = grad_queries.astype(jnp.bfloat16)
    grad_key_b = grad_keys.astype(jnp.bfloat16)
    grad_value_b = grad_values_own.astype(jnp.bfloat16)
    grad_query_w = contract(normed, grad_query_b, 0, 0)
    grad_key_w = contract(normed, grad_key_b, 0, 0)
    grad_value_w = contract(normed, grad_value_b, 0, 0)
    grad_normed = (
        contract(grad_query_b, query_back, 1, 1)
        + contract(grad_key_b, key_back, 1, 1)
        + contract(grad_value_b, value_back, 1, 1)
    )
    norm_one_back = jax.vjp(rms_scaled, inputs, gain_first)[1]
    grad_in_part, grad_gain_one = norm_one_back(grad_normed)
    grad_input = (grad_middle + grad_in_part).astype(jnp.bfloat16)
    attn_grads = (
        lax.psum_scatter(grad_query_w, ("seq", "wide"), scatter_dimension=0, tiled=True),
        lax.psum_scatter(grad_key_w, ("seq", "wide"), scatter_dimension=0, tiled=True),
        lax.psum_scatter(grad_value_w, ("seq", "wide"), scatter_dimension=0, tiled=True),
        lax.psum_scatter(grad_out_w, ("seq", "wide"), scatter_dimension=0, tiled=True),
        lax.psum_scatter(grad_gain_one, ("seq", "wide"), scatter_dimension=0, tiled=True),
        lax.psum_scatter(
            grad_gain_mid.reshape(width_all), ("seq", "wide"), scatter_dimension=0, tiled=True
        ),
        lax.psum_scatter(grad_gain_two, ("seq", "wide"), scatter_dimension=0, tiled=True),
    )
    small_sums = lax.psum((kernel_acc, grad_mix), ("seq", "wide"))
    return (
        output[None],
        grad_input[None],
        attn_grads[0],
        attn_grads[1],
        attn_grads[2],
        attn_grads[3],
        attn_grads[4],
        attn_grads[5],
        attn_grads[6],
        small_sums[0],
        small_sums[1],
        ffn_grads[0],
        ffn_grads[1],
        ffn_grads[2],
    )


def dot_plain(left, right):
    return contract(left, right, 1, 0)


def dot_nt(left, right):
    return contract(left, right, 1, 1)


def dot_tn(left, right):
    return contract(left, right, 0, 0)


def halves(value):
    high = value.astype(jnp.bfloat16)
    return high, (value - high.astype(jnp.float32)).astype(jnp.bfloat16)


def iota(shape, dim):
    return lax.broadcasted_iota(jnp.int32, shape, dim)


def spread_lanes(tile, count):
    return tile if count == 1 else jnp.concatenate([tile] * count, axis=1)


def allowed_mask(starts, block, first_col, count):
    cols = iota((BLOCK, count * LANES), 1) + first_col
    rows = iota((BLOCK, count * LANES), 0) + block * BLOCK
    return (cols >= spread_lanes(starts, count)) & (cols <= rows)


def head_stats(values):
    lane = iota(values.shape, 1)
    mean = jnp.sum(values, axis=-1, keepdims=True) * (1.0 / HEAD_DIM)
    center = jnp.where(lane < HEAD_DIM, values - mean, 0.0)
    spread = jnp.sum(center * center, axis=-1, keepdims=True) * (1.0 / HEAD_DIM)
    inverse = lax.rsqrt(spread + epsilon)
    return center * inverse, inverse


def fold_rows(value):
    return jnp.sum(value.reshape(value.shape[0] // 8, 8, value.shape[1]), axis=0)


def full_spec():
    return pl.BlockSpec(memory_space=pltpu.VMEM)


def smem_spec():
    return pl.BlockSpec(memory_space=pltpu.SMEM)


def shape_of(shape, dtype=jnp.bfloat16):
    return jax.ShapeDtypeStruct(shape, dtype)


def in_hbm(value):
    return pltpu.with_memory_space_constraint(value, pltpu.HBM)


def kernel_call(body, name, outs, ins, scratch=(), flops=0, smem=0, vmem=40, lazy=0, hbm=0):
    still = lazy + hbm
    moved = sum(v.size * v.dtype.itemsize for v in ins) + sum(
        o.size * o.dtype.itemsize for o in outs
    )
    return pl.pallas_call(
        body,
        in_specs=[smem_spec()] * smem
        + [full_spec()] * (len(ins) - smem - still)
        + [pl.BlockSpec(memory_space=pltpu.HBM)] * still,
        out_specs=[full_spec()] * len(outs),
        out_shape=list(outs),
        scratch_shapes=[pltpu.VMEM(v.shape, v.dtype) for v in ins[len(ins) - lazy :]]
        + [pltpu.SemaphoreType.DMA((lazy,))] * min(lazy, 1)
        + list(scratch),
        compiler_params=pltpu.CompilerParams(vmem_limit_bytes=vmem << 20),
        cost_estimate=pl.CostEstimate(flops=flops, bytes_accessed=moved, transcendentals=0),
        name=name,
    )(*ins[: len(ins) - still], *(in_hbm(v) for v in ins[len(ins) - still :]))


def started(sources, targets, sems):
    copies = [
        pltpu.make_async_copy(source, target, sems.at[i])
        for i, (source, target) in enumerate(zip(sources, targets))
    ]
    for copy in copies:
        copy.start()

    def wait(first, last):
        for copy in copies[first:last]:
            copy.wait()

    return wait


ORDER = (0, 4, 1, 5, 2, 6, 3, 7)


def slot_place(plane, slot):
    other = plane ^ ORDER[slot]
    return other & 1, pl.multiple_of((other >> 1) * BLOCK, BLOCK)


def half_tile(tiles, index):
    tile = tiles[index // 2]
    return tile, pltpu.roll(tile, LANES // 2, 1), index % 2


def joined(first, second):
    low = first[1] if first[2] else first[0]
    high = second[0] if second[2] else second[1]
    lane = iota(low.shape, 1)
    return jnp.where(lane < LANES // 2, low, high)


def pack_kernel(
    slab, gains_ref, q_from, k_from, v_from, rows_from, out_ref, rows_out_ref,
    q_ref, k_ref, v_ref, rows_ref, sems,
):
    wait = started(
        (q_from, k_from, v_from, rows_from), (q_ref, k_ref, v_ref, rows_ref), sems
    )
    wait(0, 4)
    tiles = [
        [ref[:, t * LANES : (t + 1) * LANES] for t in range(ref.shape[1] // LANES)]
        for ref in (q_ref, k_ref, v_ref)
    ]
    per = GROUP * HEAD_DIM // (LANES // 2)
    for g in range(8):
        parts = [half_tile(tiles[w], per * g + i) for w in range(3) for i in range(per)]
        for t in range(4):
            out_ref[g, t * slab : (t + 1) * slab, :] = joined(
                parts[2 * t], parts[2 * t + 1]
            ).astype(jnp.bfloat16)
        tile, turned, side = parts[8]
        first, second = (turned, tile) if side else (tile, turned)
        half = slab // 2
        lane = iota((half, LANES), 1)
        out_ref[g, 4 * slab : 4 * slab + half, :] = jnp.where(
            lane < LANES // 2, first[:half], second[half:]
        ).astype(jnp.bfloat16)
        out_ref[g, 4 * slab + half :, :] = gains_ref[...]
    for t in range(rows_ref.shape[1] // LANES):
        rows_out_ref[t * slab : (t + 1) * slab, :] = rows_ref[
            :, t * LANES : (t + 1) * LANES
        ].astype(jnp.bfloat16)


def unpack_kernel(slab, in_ref, rows_ref, q_ref, k_ref, v_ref, out_ref):
    per = GROUP * HEAD_DIM // (LANES // 2)
    pieces = [[], [], []]
    half = slab // 2
    lane = iota((half, LANES), 1)
    for g in range(8):
        tiles = [
            in_ref[g, t * slab : (t + 1) * slab, :].astype(jnp.float32) for t in range(4)
        ]
        rest = in_ref[g, 4 * slab : 4 * slab + half, :].astype(jnp.float32)
        turned = pltpu.roll(rest, LANES // 2, 1)
        tiles.append(jnp.concatenate([rest, turned], axis=0))
        for i in range(3 * per):
            pieces[i // per].append(half_tile(tiles, i))
    for ref, parts in zip((q_ref, k_ref, v_ref), pieces):
        for t in range(len(parts) // 2):
            ref[:, t * LANES : (t + 1) * LANES] = joined(parts[2 * t], parts[2 * t + 1])
    for t in range(out_ref.shape[1] // LANES):
        out_ref[:, t * LANES : (t + 1) * LANES] = rows_ref[t * slab : (t + 1) * slab, :].astype(
            jnp.float32
        )


def attend_pack(p, blocks, reach, mix_ref, q_ref, k_ref, v_ref, start_ref, th_ref, tl_ref, gain,
                probs_ref, high_ref, att_ref, grouped_ref, low_ref, part_ref):
    key_rim = CK // 2
    scaling = HEAD_DIM ** (-0.5)
    for h in range(GROUP):
        lanes = slice(h * LANES, (h + 1) * LANES)
        high_ref[p, h, :RIM, :] = jnp.zeros((RIM, high_ref.shape[3]), jnp.bfloat16)
        low_ref[h, :RIM, :] = jnp.zeros((RIM, high_ref.shape[3]), jnp.bfloat16)
        for n in range(blocks):
            first, last = max(0, n - reach), min(n + 3, blocks + 1)
            rows = slice(n * BLOCK, (n + 1) * BLOCK)
            scores = (
                dot_nt(q_ref[p, rows, lanes], k_ref[p, first * BLOCK : last * BLOCK, lanes]) * scaling
            )
            keep = allowed_mask(start_ref[p, rows, :], n, first * BLOCK - key_rim, last - first)
            high, low = halves(jnp.where(keep, scores, 0.0))
            into = slice(RIM + n * BLOCK, RIM + (n + 1) * BLOCK)
            cols = slice(first * LANES, last * LANES)
            high_ref[p, h, into, cols] = high
            low_ref[h, into, cols] = low
    for n in range(blocks):
        first = max(0, n - reach)
        count = n - first + 1
        rows = slice(n * BLOCK, (n + 1) * BLOCK)
        starts = start_ref[p, rows, :]
        offset = iota((BLOCK, LANES), 0) + n * BLOCK - starts
        keep = allowed_mask(starts, n, first * BLOCK, count)
        window = slice((reach + 1 - count) * LANES, (reach + 1) * LANES)
        probs = []
        for h in range(GROUP):
            pieces = []
            for m in range(first, n + 1):
                rim_rows = slice(n * BLOCK, (n + 1) * BLOCK + RIM)
                cols = slice(m * LANES, (m + 2) * LANES)
                high = high_ref[p, h, rim_rows, cols]
                low = low_ref[h, rim_rows, cols]
                part = (
                    dot_plain(high, th_ref[h])
                    + dot_plain(low, th_ref[h])
                    + dot_plain(high, tl_ref[h])
                )
                for a in range(CQ):
                    part_ref[a] = part[:, a * LANES : (a + 1) * LANES]
                total = part_ref[0, RIM:, :]
                for a in range(1, CQ):
                    total = total + jnp.where(
                        offset >= a, part_ref[a, RIM - a : RIM - a + BLOCK, :], 0.0
                    )
                pieces.append(total)
            logits = pieces[0] if count == 1 else jnp.concatenate(pieces, axis=1)
            logits = jnp.where(keep, logits, -jnp.inf)
            peak = jnp.max(logits, axis=-1, keepdims=True)
            raised = jnp.exp(logits - peak)
            prob = raised / jnp.sum(raised, axis=-1, keepdims=True)
            probs_ref[p, h, rows, window] = prob
            probs.append(prob)
        keys = slice(first * BLOCK, (n + 1) * BLOCK)
        for h in range(GROUP):
            lanes = slice(h * LANES, (h + 1) * LANES)
            mixed = (mix_ref[h, 0] * probs[0] + mix_ref[h, 1] * probs[1]).astype(jnp.bfloat16)
            attended = dot_plain(mixed, v_ref[p, keys, lanes])
            att_ref[p, rows, lanes] = attended
            normal, _ = head_stats(attended)
            grouped_ref[p, rows, lanes] = (normal * gain[:, lanes]).astype(jnp.bfloat16)


def forward_kernel(
    blocks, reach, slab, at_ref, mix_ref, w_ref, t0, t1, t2, t3, t4, t5, t6, t7,
    start_ref, th_ref, tl_ref, spread_ref, rest_ref,
    normed_ref, wide_ref, q_ref, k_ref, v_ref, probs_ref, high_ref, att_ref, near_ref,
    far_ref, gains_ref, gain_ref,
    grp_ref, shift_ref, low_ref, part_ref,
):
    plane = at_ref[0]
    half = slab // 2
    block = 4 * slab + half + 8
    gains_ref[...] = jnp.zeros_like(gains_ref)
    span = gains_ref.shape[1] // 4
    for zz in range(w_ref.shape[0]):
        ref = w_ref.at[zz]
        main = jnp.concatenate(
            [
                jnp.concatenate(
                    [ref[g * block + t * slab : g * block + (t + 1) * slab, :] for t in range(4)],
                    axis=1,
                )
                for g in range(8)
            ],
            axis=0,
        )
        rest = jnp.concatenate(
            [ref[g * block + 4 * slab : g * block + 4 * slab + half, :] for g in range(8)], axis=0
        )
        table = dot_plain(main, spread_ref[...])
        early = dot_plain(rest, rest_ref[0])
        late = dot_plain(rest, rest_ref[1])
        for g in range(8):
            row = (g // 2 * 8 + g % 2 + 2 * zz) * slab
            tail = jnp.concatenate(
                [early[g * half : (g + 1) * half], late[g * half : (g + 1) * half]], axis=0
            )
            wide_ref[row : row + slab, :] = (table[g * slab : (g + 1) * slab] + tail).astype(
                jnp.bfloat16
            )
        lane = iota((LANES, span), 0)
        for y in range(2):
            place = (iota((LANES, span), 1) == lane + (zz * 2 + y) * slab) & (lane < slab)
            place = jnp.where(place, 1.0, 0.0).astype(jnp.bfloat16)
            for s in range(4):
                gains_ref[:, s * span : (s + 1) * span] += dot_plain(
                    ref[(2 * s + y + 1) * block - 8 : (2 * s + y + 1) * block, :], place
                )
    cols = GROUP * HEAD_DIM
    width = gains_ref.shape[1]
    lane = iota((width, GROUP * LANES), 1)
    from_row = iota((width, GROUP * LANES), 0) - plane * cols
    select = (from_row == lane // LANES * HEAD_DIM + lane % LANES) & (lane % LANES < HEAD_DIM)
    gain_ref[...] = dot_plain(
        gains_ref[...].astype(jnp.bfloat16), jnp.where(select, 1.0, 0.0).astype(jnp.bfloat16)
    )[1:2]
    gain = gain_ref[...]
    for slot, ref in enumerate((t0, t1, t2, t3, t4, t5, t6, t7)):
        value = ref[...].astype(jnp.float32)
        scale = lax.rsqrt(jnp.mean(value * value, axis=-1, keepdims=True) + epsilon)
        normed_ref[slot * BLOCK : (slot + 1) * BLOCK, :] = (
            value * scale * gains_ref[0:1, :]
        ).astype(jnp.bfloat16)
    lanes = GROUP * LANES
    shift_ref[...] = jnp.zeros_like(shift_ref)
    for slots in (range(4), range(4, 8)):
        rows = slice(slots[0] * BLOCK, (slots[-1] + 1) * BLOCK)
        qkv = dot_plain(normed_ref[rows, :], wide_ref[...])
        for i, slot in enumerate(slots):
            pack, row = slot_place(plane, slot)
            part = qkv[i * BLOCK : (i + 1) * BLOCK]
            q_ref[pack, pl.ds(row, BLOCK), :] = part[:, :lanes].astype(jnp.bfloat16)
            shift_ref[pack, pl.ds(row, BLOCK), :] = part[:, lanes : 2 * lanes]
            v_ref[pack, pl.ds(row, BLOCK), :] = part[:, 2 * lanes :].astype(jnp.bfloat16)
    key_rim = CK // 2
    length = q_ref.shape[1]
    @pl.loop(0, 2)
    def _(p):
        moved = jnp.concatenate(
            [
                jnp.zeros((8, lanes), jnp.float32),
                shift_ref[p],
                jnp.zeros((LANES - 8, lanes), jnp.float32),
            ],
            axis=0,
        )
        moved = pltpu.roll(moved, length + LANES - (8 - key_rim), 0)
        k_ref[p] = moved.astype(jnp.bfloat16)
        attend_pack(
            p, blocks, reach, mix_ref, q_ref, k_ref, v_ref, start_ref, th_ref, tl_ref, gain,
            probs_ref, high_ref, att_ref, grp_ref, low_ref, part_ref,
        )

    for slot in range(8):
        pack, row = slot_place(plane, slot)
        into = near_ref if slot < 4 else far_ref
        into[slot % 4 * BLOCK : (slot % 4 + 1) * BLOCK, :] = grp_ref[pack, pl.ds(row, BLOCK), :]


def store_blocks(value, refs):
    for i, ref in enumerate(refs):
        ref[...] = value[i * BLOCK : (i + 1) * BLOCK].astype(ref.dtype)


def pair_kernel(
    transposed, own_ref, got_ref, w_from, other_from, total_ref, r1, r2, r3, w_ref, other_ref, sems
):
    wait = started((w_from, other_from), (w_ref, other_ref), sems)
    dot = dot_nt if transposed else dot_plain
    wait(0, 1)
    value = dot(own_ref[...], w_ref[...])
    wait(1, 2)
    value = value + dot(got_ref[...], other_ref[...])
    store_blocks(value, (total_ref, r1, r2, r3))


def pair_gain_kernel(
    own_ref, got_ref, w_from, other_from, t0_from, t1_from, t2_from, t3_from,
    total_ref, r1, r2, r3, gain_ref,
    w_ref, other_ref, t0, t1, t2, t3, sems,
):
    wait = started(
        (w_from, other_from, t0_from, t1_from, t2_from, t3_from),
        (w_ref, other_ref, t0, t1, t2, t3),
        sems,
    )
    wait(0, 1)
    value = dot_nt(own_ref[...], w_ref[...])
    wait(1, 6)
    value = value + dot_nt(got_ref[...], other_ref[...])
    store_blocks(value, (total_ref, r1, r2, r3))
    total = jnp.zeros(gain_ref.shape, jnp.float32)
    for i, ref in enumerate((t0, t1, t2, t3)):
        token = ref[...].astype(jnp.float32)
        scale = lax.rsqrt(jnp.mean(token * token, axis=-1, keepdims=True) + epsilon)
        total = total + fold_rows(value[i * BLOCK : (i + 1) * BLOCK] * (token * scale))
    gain_ref[...] = total


def small_kernel(at_ref, attn_ref, ffn_ref, taps_ref, mix_ref, group_ref, out_ref):
    plane = at_ref[0]
    out_ref[...] = jnp.zeros_like(out_ref)
    tiles = attn_ref.shape[1] // LANES
    for i, ref in enumerate((attn_ref, ffn_ref)):
        row = jnp.sum(ref[...], axis=0, keepdims=True)
        for t in range(tiles):
            out_ref[i * tiles + t : i * tiles + t + 1, :] = row[:, t * LANES : (t + 1) * LANES]
    group = jnp.sum(group_ref[...], axis=0, keepdims=True)
    lane = iota((16, LANES), 1)
    place = iota((16, LANES), 0)
    first = iota((1, LANES), 1)
    for h in range(GROUP):
        head = GROUP * plane + h
        out_ref[pl.ds(2 * tiles + head, 1), :] = group[:, h * LANES : (h + 1) * LANES]
        total = jnp.zeros((16, LANES), jnp.float32)
        for a in range(CQ):
            sums = jnp.sum(taps_ref[h, :, a * LANES : (a + 1) * LANES], axis=-1, keepdims=True)
            total = total + jnp.where(lane == 16 * a + place, sums, 0.0)
        row = jnp.sum(total, axis=0, keepdims=True)
        for d in range(GROUP):
            value = jnp.sum(mix_ref[h * GROUP + d], axis=0, keepdims=True)
            value = jnp.sum(value, axis=1, keepdims=True)
            row = row + jnp.where(first == 16 * CQ + d, value, 0.0)
        out_ref[pl.ds(2 * tiles + HEADS + head, 1), :] = row


def backward_pack(p, blocks, reach, mix_ref, gg_ref, att_ref, gain_ref, q_ref, k_ref, v_ref,
                  start_ref, stop_ref, probs_ref, high_ref, th_ref,
                  dqkv_ref, mixg_ref, gaing_ref, grad_ref, cross_ref, keyg_ref, valueg_ref, ready):
    key_rim = CK // 2
    scaling = HEAD_DIM ** (-0.5)
    all_lanes = GROUP * LANES
    grad_ref[...] = jnp.zeros_like(grad_ref)
    keyg_ref[...] = jnp.zeros_like(keyg_ref)
    valueg_ref[...] = jnp.zeros_like(valueg_ref)
    lane = iota((BLOCK, LANES), 1)
    for n in range(blocks):
        first = max(0, n - reach)
        count = n - first + 1
        rows = slice(n * BLOCK, (n + 1) * BLOCK)
        keys = slice(first * BLOCK, (n + 1) * BLOCK)
        window = slice((reach + 1 - count) * LANES, (reach + 1) * LANES)
        probs = [probs_ref[p, h, rows, window] for h in range(GROUP)]
        mixed_grads = []
        for h in range(GROUP):
            lanes = slice(h * LANES, (h + 1) * LANES)
            normal, inverse = head_stats(att_ref[p, rows, lanes])
            grad_grouped = gg_ref[p, rows, lanes]
            gaing_ref[:, lanes] += fold_rows(grad_grouped * normal)
            scaled = jnp.where(lane < HEAD_DIM, grad_grouped * gain_ref[:, lanes], 0.0)
            mean_one = jnp.sum(scaled, axis=-1, keepdims=True) * (1.0 / HEAD_DIM)
            mean_two = jnp.sum(scaled * normal, axis=-1, keepdims=True) * (1.0 / HEAD_DIM)
            grad_att = inverse * (scaled - mean_one - normal * mean_two)
            grad_att = jnp.where(lane < HEAD_DIM, grad_att, 0.0).astype(jnp.bfloat16)
            mixed_grads.append(dot_nt(grad_att, v_ref[p, keys, lanes]))
            mixed = (mix_ref[h, 0] * probs[0] + mix_ref[h, 1] * probs[1]).astype(jnp.bfloat16)
            valueg_ref[keys, lanes] += dot_tn(mixed, grad_att)
        for h in range(GROUP):
            for d in range(GROUP):
                product = fold_rows(probs[d] * mixed_grads[h])
                total = product[:, :LANES]
                for m in range(1, count):
                    total = total + product[:, m * LANES : (m + 1) * LANES]
                mixg_ref[h * GROUP + d] += total
        for d in range(GROUP):
            grad_probs = mix_ref[0, d] * mixed_grads[0] + mix_ref[1, d] * mixed_grads[1]
            delta = jnp.sum(probs[d] * grad_probs, axis=-1, keepdims=True)
            grad_logits = probs[d] * (grad_probs - delta)
            for m in range(count):
                grad_ref[d, first + m, rows, :] = grad_logits[:, m * LANES : (m + 1) * LANES]
    ready()
    for h in range(GROUP):
        lanes = slice(h * LANES, (h + 1) * LANES)
        for n in range(blocks):
            first, last = max(0, n - reach), min(n + 1, blocks - 1)
            rows = slice(n * BLOCK, (n + 1) * BLOCK)
            room = stop_ref[p, rows, :] - (iota((BLOCK, LANES), 0) + n * BLOCK)
            count = n + 2 - first
            sums = [None] * (count + 1)
            for m in range(first, last + 1):
                pieces = []
                for a in range(CQ):
                    piece = grad_ref[h, m, n * BLOCK + a : (n + 1) * BLOCK + a, :]
                    if a:
                        piece = jnp.where(room > a, piece, 0.0)
                    pieces.append(piece.astype(jnp.bfloat16))
                high = jnp.concatenate(pieces, axis=1)
                part = dot_nt(high, th_ref[h])
                for side in range(2):
                    place = m - first + side
                    value = part[:, side * LANES : (side + 1) * LANES]
                    sums[place] = value if sums[place] is None else sums[place] + value
                scores = high_ref[
                    p, h, RIM + n * BLOCK : RIM + (n + 1) * BLOCK, m * LANES : (m + 2) * LANES
                ]
                if m <= n:
                    cross_ref[h] += dot_tn(scores, high)
                else:
                    cross_ref[h, :LANES, :] += dot_tn(scores[:, :LANES], high)
            total = jnp.concatenate(sums[:count], axis=1)
            keep = allowed_mask(start_ref[p, rows, :], n, first * BLOCK - key_rim, count)
            grad_scores = jnp.where(keep, total, 0.0).astype(jnp.bfloat16)
            cols = slice(first * BLOCK, (first + count) * BLOCK)
            dqkv_ref[p, rows, lanes] = (
                dot_plain(grad_scores, k_ref[p, cols, lanes]) * scaling
            ).astype(jnp.bfloat16)
            keyg_ref[h, cols, :] += dot_tn(grad_scores, q_ref[p, rows, lanes])
        key_lanes = slice(all_lanes + h * LANES, all_lanes + (h + 1) * LANES)
        dqkv_ref[p, :, key_lanes] = (
            keyg_ref[h, key_rim : key_rim + blocks * BLOCK, :] * scaling
        ).astype(jnp.bfloat16)
    dqkv_ref[p, :, 2 * all_lanes :] = valueg_ref[...].astype(jnp.bfloat16)


def backward_kernel(
    blocks, reach, at_ref, mix_ref, b0, b1, b2, b3, b4, b5, b6, b7, out_w_ref, gain_ref,
    att_from, v_from, probs_from, start_from, stop_from, th_from, high_from, k_from, q_from,
    near_ref, far_ref, taps_ref, mixg_ref, gaing_ref,
    att_ref, v_ref, probs_ref, start_ref, stop_ref, th_ref, high_ref, k_ref, q_ref, sems,
    gg_ref, abs_ref, grad_ref, cross_ref, keyg_ref, valueg_ref,
):
    plane = at_ref[0]
    sources = (
        att_from, v_from, probs_from, start_from, stop_from, th_from, high_from, k_from, q_from
    )
    targets = (
        att_ref, v_ref, probs_ref, start_ref, stop_ref, th_ref, high_ref, k_ref, q_ref
    )
    wait = started(sources, targets, sems)
    pieces = (b0, b1, b2, b3, b4, b5, b6, b7)
    for slots in (range(4), range(4, 8)):
        branch = jnp.concatenate([pieces[slot][...] for slot in slots], axis=0)
        part = dot_nt(branch, out_w_ref[...])
        for i, slot in enumerate(slots):
            pack, row = slot_place(plane, slot)
            gg_ref[pack, pl.ds(row, BLOCK), :] = part[i * BLOCK : (i + 1) * BLOCK]
    cross_ref[...] = jnp.zeros_like(cross_ref)
    mixg_ref[...] = jnp.zeros_like(mixg_ref)
    gaing_ref[...] = jnp.zeros_like(gaing_ref)
    wait(0, 3)

    for p in range(2):
        backward_pack(
            p, blocks, reach, mix_ref, gg_ref, att_ref, gain_ref, q_ref, k_ref, v_ref,
            start_ref, stop_ref, probs_ref, high_ref, th_ref,
            abs_ref, mixg_ref, gaing_ref, grad_ref, cross_ref, keyg_ref, valueg_ref,
            (lambda: wait(3, 9)) if p == 0 else lambda: None,
        )
    for slot in range(8):
        pack, row = slot_place(plane, slot)
        into = near_ref if slot < 4 else far_ref
        into[slot % 4 * BLOCK : (slot % 4 + 1) * BLOCK, :] = abs_ref[pack, pl.ds(row, BLOCK), :]
    height = LANES + 2 * 8
    shift = iota((height, CQ * LANES), 1) % LANES - iota((height, CQ * LANES), 0) + (CK - 1)
    for h in range(GROUP):
        cross = cross_ref[h, :height, :]
        taps_ref[h] = jnp.zeros(taps_ref.shape[1:], jnp.float32)
        for b in range(CK):
            taps_ref[h, b : b + 1, :] = jnp.sum(
                jnp.where(shift == b, cross, 0.0), axis=0, keepdims=True
            )


def out_rows_kernel(slab, w_ref, out_ref):
    width = out_ref.shape[1]
    base = w_ref.shape[1] - width // LANES * slab
    fill = jnp.zeros((LANES - HEAD_DIM, width), jnp.bfloat16)
    for k in range(w_ref.shape[0]):
        row = k // 2 * LANES + k % 2 * slab
        for t in range(width // LANES):
            out_ref[row : row + slab, t * LANES : (t + 1) * LANES] = w_ref[
                k, base + t * slab : base + (t + 1) * slab, :
            ]
    for h in range(GROUP):
        out_ref[h * LANES + HEAD_DIM : (h + 1) * LANES, :] = fill


def weight_grads_kernel(
    slab, near_ref, far_ref, b0, b1, b2, b3, b4, b5, b6, b7,
    group_near_from, group_far_from, spread_from, rest_from, normed_from, all_ref,
    group_near, group_far, spread_ref, rest_ref, normed_ref, sems,
):
    wait = started(
        (group_near_from, group_far_from, spread_from, rest_from, normed_from),
        (group_near, group_far, spread_ref, rest_ref, normed_ref),
        sems,
    )
    pieces = (b0, b1, b2, b3, b4, b5, b6, b7)
    near = jnp.concatenate([ref[...] for ref in pieces[:4]], axis=0)
    wait(0, 2)
    grad = dot_tn(group_near[...], near)
    far = jnp.concatenate([ref[...] for ref in pieces[4:]], axis=0)
    grad = (grad + dot_tn(group_far[...], far)).astype(jnp.bfloat16)
    base = all_ref.shape[1] - grad.shape[1] // LANES * slab
    for k in range(all_ref.shape[0]):
        row = k // 2 * LANES + k % 2 * slab
        for t in range(grad.shape[1] // LANES):
            all_ref[k, base + t * slab : base + (t + 1) * slab, :] = grad[
                row : row + slab, t * LANES : (t + 1) * LANES
            ]
    block = base // 8
    half = slab // 2
    span = normed_ref.shape[1] // 4
    rows = near_ref.shape[0]
    wait(2, 4)
    packed = []
    for ref in (near_ref, far_ref):
        value = jnp.concatenate(
            [dot_nt(ref[...], spread_ref[...]), dot_nt(ref[...], rest_ref[0])], axis=1
        )
        packed.append(value.astype(jnp.bfloat16))
    wait(4, 5)
    for s in range(4):
        cols = slice(s * span, (s + 1) * span)
        table = dot_tn(normed_ref[:rows, cols], packed[0]) + dot_tn(
            normed_ref[rows:, cols], packed[1]
        )
        rest = table[:, 4 * LANES :]
        for zz in range(4):
            for y in range(2):
                g = 2 * s + y
                row = (zz * 2 + y) * slab
                for t in range(4):
                    at = g * block + t * slab
                    all_ref[zz, at : at + slab, :] = table[
                        row : row + slab, t * LANES : (t + 1) * LANES
                    ].astype(jnp.bfloat16)
                pair = rest[row : row + half] + pltpu.roll(
                    rest[row + half : row + slab], LANES // 2, 1
                )
                all_ref[zz, g * block + 4 * slab : (g + 1) * block, :] = jnp.concatenate(
                    [pair, jnp.zeros((8, LANES), jnp.float32)], axis=0
                ).astype(jnp.bfloat16)


def assemble_kernel(sub, w_ref, gu_ref, down_ref):
    deep = w_ref.shape[3]
    units = w_ref.shape[0] * sub
    parts = deep // LANES
    for zz in range(w_ref.shape[0]):
        for s in range(w_ref.shape[1]):
            for m in range(2):
                at = m * units + zz * sub
                gu_ref[s * deep : (s + 1) * deep, at : at + sub] = w_ref[zz, s, m]
            for c in range(parts):
                at = (s * parts + c) * LANES
                down_ref[zz * sub : (zz + 1) * sub, at : at + LANES] = w_ref[
                    zz, s, 2, c * sub : (c + 1) * sub, :
                ]


def hidden_kernel(
    x0, x1, x2, x3, x4, x5, x6, x7, c0, c1, c2, c3, c4, c5, c6, c7, gu_ref, down_ref,
    hidden_near, hidden_far, grad_near, grad_far,
):
    units = down_ref.shape[0]
    xs = (x0, x1, x2, x3, x4, x5, x6, x7)
    cs = (c0, c1, c2, c3, c4, c5, c6, c7)
    for part in (2, 3, 0, 1):
        pair = (2 * part, 2 * part + 1)
        value = jnp.concatenate([xs[i][...] for i in pair], axis=0)
        gate_up = dot_plain(value, gu_ref[...])
        gate, up = gate_up[:, :units], gate_up[:, units:]
        cot = jnp.concatenate([cs[i][...] for i in pair], axis=0)
        grad_hidden = dot_nt(cot, down_ref[...])
        sig = 1.0 / (1.0 + jnp.exp(-gate))
        silu = gate * sig
        hidden_ref, grad_ref = (hidden_near, grad_near) if part < 2 else (hidden_far, grad_far)
        rows = slice(part % 2 * 2 * BLOCK, (part % 2 + 1) * 2 * BLOCK)
        hidden_ref[rows, :] = (silu * up).astype(jnp.bfloat16)
        grad_ref[rows, :units] = (
            grad_hidden * up * sig * (1.0 + gate * (1.0 - sig))
        ).astype(jnp.bfloat16)
        grad_ref[rows, units:] = (grad_hidden * silu).astype(jnp.bfloat16)


def hidden_grad_kernel(
    sub, hidden_near, hidden_far, grad_near, grad_far,
    x0, x1, x2, x3, x4, x5, x6, x7, c0, c1, c2, c3, c4, c5, c6, c7, out_ref, x_ref, c_ref, sems,
):
    deep = out_ref.shape[3]
    depth = out_ref.shape[0]
    units = depth * sub
    rows = [slice(slot * BLOCK, (slot + 1) * BLOCK) for slot in range(8)]
    wait = started(
        (x0, x1, x2, x3, x4, x5, x6, x7, c0, c1, c2, c3, c4, c5, c6, c7),
        [x_ref.at[part, :] for part in rows] + [c_ref.at[part, :] for part in rows],
        sems,
    )
    half = 4 * BLOCK
    wait(0, 8)
    for s in range(out_ref.shape[1]):
        cols = slice(s * deep, (s + 1) * deep)
        table = (
            dot_tn(x_ref[:half, cols], grad_near[...]) + dot_tn(x_ref[half:, cols], grad_far[...])
        ).astype(jnp.bfloat16)
        for zz in range(depth):
            for m in range(2):
                at = m * units + zz * sub
                out_ref[zz, s, m] = table[:, at : at + sub]
    wait(8, 16)
    for s in range(out_ref.shape[1]):
        cols = slice(s * deep, (s + 1) * deep)
        down = (
            dot_tn(hidden_near[...], c_ref[:half, cols])
            + dot_tn(hidden_far[...], c_ref[half:, cols])
        ).astype(jnp.bfloat16)
        for zz in range(depth):
            for c in range(deep // LANES):
                out_ref[zz, s, 2, c * sub : (c + 1) * sub, :] = down[
                    zz * sub : (zz + 1) * sub, c * LANES : (c + 1) * LANES
                ]


def pack_hidden_kernel(sub, gate_ref, up_ref, down_ref, out_ref):
    deep = gate_ref.shape[0]
    for s in range(out_ref.shape[0]):
        for m, ref in enumerate((gate_ref, up_ref)):
            out_ref[s, m] = ref[:, s * sub : (s + 1) * sub].astype(jnp.bfloat16)
        for c in range(deep // LANES):
            out_ref[s, 2, c * sub : (c + 1) * sub, :] = down_ref[
                s * sub : (s + 1) * sub, c * LANES : (c + 1) * LANES
            ].astype(jnp.bfloat16)


def unpack_hidden_kernel(sub, in_ref, gate_ref, up_ref, down_ref):
    deep = gate_ref.shape[0]
    for s in range(in_ref.shape[0]):
        for m, ref in enumerate((gate_ref, up_ref)):
            ref[:, s * sub : (s + 1) * sub] = in_ref[s, m].astype(jnp.float32)
        for c in range(deep // LANES):
            down_ref[s * sub : (s + 1) * sub, c * LANES : (c + 1) * LANES] = in_ref[
                s, 2, c * sub : (c + 1) * sub, :
            ].astype(jnp.float32)


def total_of(refs):
    total = refs[0][...]
    for ref in refs[1:]:
        total = total + ref[...].astype(jnp.float32)
    return total


def middle_kernel(s0, s1, s2, s3, token_ref, gains_ref, middle_ref, in_ref):
    middle = token_ref[...].astype(jnp.float32) + total_of((s0, s1, s2, s3))
    middle_ref[...] = middle
    scale = lax.rsqrt(jnp.mean(middle * middle, axis=-1, keepdims=True) + epsilon)
    in_ref[...] = (middle * scale * gains_ref[2:3, :]).astype(jnp.bfloat16)


def norm_back(row, grad, value, gains_ref, first):
    scale = lax.rsqrt(jnp.mean(value * value, axis=-1, keepdims=True) + epsilon)
    scaled = grad * gains_ref[row : row + 1, :]
    mean = jnp.mean(scaled * value, axis=-1, keepdims=True)
    return first + (scale * scaled - value * (scale * scale * scale) * mean)


def middle_back_kernel(
    s0, s1, s2, s3, middle_ref, cot_ref, gains_ref, grad_ref, branch_ref, gain_ref
):
    value = middle_ref[...]
    total = total_of((s0, s1, s2, s3))
    grad = norm_back(2, total, value, gains_ref, cot_ref[...].astype(jnp.float32))
    grad_ref[...] = grad
    branch_ref[...] = grad.astype(jnp.bfloat16)
    scale = lax.rsqrt(jnp.mean(value * value, axis=-1, keepdims=True) + epsilon)
    gain_ref[...] = fold_rows(total * value * scale)


def input_back_kernel(s0, s1, s2, s3, token_ref, middle_ref, gains_ref, grad_ref):
    token = token_ref[...].astype(jnp.float32)
    grad_ref[...] = norm_back(
        0, total_of((s0, s1, s2, s3)), token, gains_ref, middle_ref[...]
    ).astype(jnp.bfloat16)


def output_kernel(s0, s1, s2, s3, middle_ref, out_ref):
    out_ref[...] = (middle_ref[...] + total_of((s0, s1, s2, s3))).astype(jnp.bfloat16)


def conv_tables(kernel):
    heads = kernel.shape[0]
    u = iota((2 * LANES, CQ * LANES), 0)
    j = iota((2 * LANES, CQ * LANES), 1) % LANES
    table = jnp.zeros((heads, 2 * LANES, CQ * LANES), jnp.float32)
    for b in range(CK):
        taps = jnp.repeat(kernel[:, :, b], LANES, axis=1)
        table = jnp.where((j - u + CK - 1 == b)[None], taps[:, None, :], table)
    return halves(table)


FLAT = ("seq", "wide")


def swapped(value, flip):
    total = lax.axis_size("seq") * lax.axis_size("wide")
    return lax.ppermute(value, FLAT, [(i, i ^ flip) for i in range(total)])


class Place:
    def __init__(self):
        self.wide_count = lax.axis_size("wide")
        self.depth = self.wide_count // 2
        self.seq = lax.axis_index("seq")
        wide = lax.axis_index("wide")
        self.y = wide % 2
        self.z = wide // 2
        self.plane = 2 * self.seq + self.y
        self.x_flip = 2 * self.wide_count
        self.core_flip = self.wide_count
        self.y_flip = 1
        self.chip_flips = (self.x_flip, self.y_flip, self.x_flip | self.y_flip)
        seqs = range(lax.axis_size("seq"))
        self.plane_groups = [
            [s * self.wide_count + z * 2 + y for s in seqs for y in range(2)] for z in range(self.depth)
        ]
        self.line_groups = [[z * 2 + y for z in range(self.depth)] for y in range(2)]


def chip_gather(place, value):
    return [value] + [swapped(value, flip) for flip in place.chip_flips]


def core_gather(place, near):
    return near + [swapped(part, place.core_flip) for part in near]


def plane_gather(place, value):
    return core_gather(place, chip_gather(place, value))


def plane_terms(place, near, far, weight, other, transposed, name, tokens=None, got=None):
    width = weight.shape[0] if transposed else weight.shape[1]
    flat = (BLOCK, width)
    if got is None:
        got = swapped(far, place.core_flip)
    return list(
        kernel_call(
            functools.partial(pair_kernel, transposed) if tokens is None else pair_gain_kernel,
            name,
            [shape_of(flat, jnp.float32)]
            + [shape_of(flat)] * 3
            + ([] if tokens is None else [shape_of((8, width), jnp.float32)]),
            (near, got, weight, other) + (tokens or ()),
            flops=16 * BLOCK * weight.size,
            vmem=24,
            lazy=2 + len(tokens or ()),
        )
    )


def chip_scatter(place, terms):
    return [terms[0]] + [
        swapped(part, flip) for part, flip in zip(terms[1:], place.chip_flips)
    ]


def line_gather(place, value):
    return lax.all_gather(value, "wide", axis=0, axis_index_groups=place.line_groups)


def line_scatter(place, blocks):
    return lax.psum_scatter(
        blocks, "wide", scatter_dimension=0, axis_index_groups=place.line_groups
    )


def plane_exchange(place, blocks):
    return lax.all_to_all(blocks, FLAT, 0, 0, axis_index_groups=place.plane_groups)


def out_pairs(place):
    return [
        (s * place.wide_count + 4 * y + z, s * place.wide_count + 2 * z + y)
        for s in range(lax.axis_size("seq"))
        for z in range(place.depth)
        for y in range(2)
    ]


def spread_tables():
    target = iota((4 * LANES, 3 * GROUP * LANES), 1)
    column = target // LANES * HEAD_DIM + target % LANES
    real = target % LANES < HEAD_DIM
    source = iota(target.shape, 0)
    main = jnp.where(real & (column == source), 1.0, 0.0).astype(jnp.bfloat16)
    source, column, real = source[:LANES], column[:LANES], real[:LANES]
    rest = [
        jnp.where(
            real & (column >= 4 * LANES) & (column - 4 * LANES + side * (LANES // 2) == source), 1.0, 0.0
        ).astype(jnp.bfloat16)
        for side in range(2)
    ]
    return main, jnp.stack(rest)


def after(done, *values):
    return lax.optimization_barrier((done,) + values)[1:]


def plane_shards(
    tokens, segments, w_query, w_key, w_value, w_out, gain_attn, gain_group, gain_ffn,
    conv_kernel, head_mix, w_gate, w_up, w_down, cotangent,
):
    place = Place()
    seq_count = lax.axis_size("seq")
    depth = place.depth
    count = tokens.shape[1]
    length = count * seq_count
    width = tokens.shape[2]
    slab = w_query.shape[0]
    blocks = length // BLOCK
    reach = (length // 2 - 1) // BLOCK + 1
    lanes = GROUP * LANES
    cols = GROUP * HEAD_DIM
    bf16 = jnp.bfloat16
    f32 = jnp.float32
    at = jnp.stack([place.plane, place.z, place.y]).astype(jnp.int32)
    own_tokens = tokens[0]
    own_cot = cotangent[0]

    gains_own = jnp.stack([gain_attn, gain_group, gain_ffn]).astype(bf16)
    gains_own = jnp.pad(gains_own, ((0, 5), (0, LANES - slab)))
    pack_rows = 4 * slab + slab // 2 + 8
    out_rows = width // LANES * slab
    packed, w_out_rows = kernel_call(
        functools.partial(pack_kernel, slab),
        "pack_projections",
        [shape_of((8, pack_rows, LANES)), shape_of((out_rows, LANES))],
        (gains_own, w_query, w_key, w_value, w_out),
        vmem=16,
        lazy=4,
    )
    sub = w_gate.shape[1] // seq_count
    deep = w_gate.shape[0]
    packed, own_tokens, w_out_rows, segments, conv_kernel, w_gate, w_up, w_down = (
        lax.optimization_barrier(
            (packed, own_tokens, w_out_rows, segments, conv_kernel, w_gate, w_up, w_down)
        )
    )
    w_out_rows = lax.ppermute(w_out_rows, FLAT, out_pairs(place))
    packed = plane_exchange(place, packed)
    (ffn_own,) = kernel_call(
        functools.partial(pack_hidden_kernel, sub),
        "pack_hidden",
        [shape_of((seq_count, 3, deep, sub))],
        (w_gate, w_up, w_down),
        vmem=16,
    )
    token_near = chip_gather(place, own_tokens)
    packed, ffn_own, own_cot = lax.optimization_barrier((packed, ffn_own, own_cot))
    w_all = line_gather(
        place, jnp.concatenate([packed.reshape(8 * pack_rows, LANES), w_out_rows])
    )
    ffn_own = lax.all_to_all(ffn_own, "seq", 0, 0)
    cot_near = chip_gather(place, own_cot)
    token_parts = core_gather(place, token_near)

    other_row = swapped(segments, place.y_flip)
    seg = jnp.where(
        place.y == 0,
        jnp.concatenate([segments, other_row]),
        jnp.concatenate([other_row, segments]),
    )
    starts = jnp.sum(seg[:, None, :] < seg[:, :, None], axis=-1, dtype=jnp.int32)
    stops = jnp.sum(seg[:, None, :] <= seg[:, :, None], axis=-1, dtype=jnp.int32)
    starts = jnp.broadcast_to(starts[:, :, None], (2, length, LANES))
    stops = jnp.broadcast_to(stops[:, :, None], (2, length, LANES))
    taps = lax.dynamic_slice_in_dim(conv_kernel, place.plane * GROUP, GROUP)
    mix = lax.dynamic_slice_in_dim(head_mix, place.plane * GROUP, GROUP)
    table_high, table_low = conv_tables(taps)
    spread_main, spread_rest = spread_tables()

    ffn_w = line_gather(place, ffn_own)
    units = depth * sub
    w_all, starts, stops, *cot_near = lax.optimization_barrier(
        (w_all, starts, stops, *cot_near)
    )
    (w_out_heads,) = kernel_call(
        functools.partial(out_rows_kernel, slab),
        "out_rows",
        [shape_of((lanes, width))],
        (w_all,),
        vmem=16,
    )
    w_out_other = swapped(w_out_heads, place.core_flip)
    cot_parts = core_gather(place, cot_near)

    padded = length + LANES
    half = 4 * count
    (
        normed, w_wide, queries, keys, values, probs, high, attended, grouped_near, grouped_far,
        gains, gain_heads,
    ) = kernel_call(
        functools.partial(forward_kernel, blocks, reach, slab),
        "attention_forward",
        [
            shape_of((8 * count, width)),
            shape_of((width, 3 * lanes)),
            shape_of((2, length, lanes)),
            shape_of((2, padded, lanes)),
            shape_of((2, length, lanes)),
            shape_of((2, GROUP, length, (reach + 1) * LANES), f32),
            shape_of((2, GROUP, RIM + length, padded)),
            shape_of((2, length, lanes), f32),
            shape_of((half, lanes)),
            shape_of((half, lanes)),
            shape_of((8, width), f32),
            shape_of((1, lanes), f32),
        ],
        (
            at, mix, w_all, *token_parts, starts, table_high, table_low, spread_main, spread_rest,
        ),
        [
            pltpu.VMEM((2, length, lanes), bf16),
            pltpu.VMEM((2, length, lanes), f32),
            pltpu.VMEM((GROUP, RIM + length, padded), bf16),
            pltpu.VMEM((CQ, RIM + BLOCK, LANES), f32),
        ],
        flops=25 * 10**9,
        smem=2,
    )
    w_wide_other = swapped(w_wide, place.core_flip)
    grouped_near, *cot_parts[4:] = lax.optimization_barrier((grouped_near, *cot_parts[4:]))
    terms = chip_scatter(
        place,
        plane_terms(place, grouped_near, grouped_far, w_out_heads, w_out_other, False, "branch"),
    )
    flat = (count, width)
    middle, ffn_in = kernel_call(
        middle_kernel,
        "middle",
        [shape_of(flat, f32), shape_of(flat)],
        (*terms, own_tokens, gains),
        vmem=16,
    )

    ffn_parts = plane_gather(place, ffn_in)
    ffn_w, *ffn_parts[1:4] = lax.optimization_barrier((ffn_w, *ffn_parts[1:4]))
    w_gate_up, w_down_all = kernel_call(
        functools.partial(assemble_kernel, sub),
        "assemble_feed_forward",
        [shape_of((width, 2 * units)), shape_of((units, width))],
        (ffn_w,),
        vmem=24,
    )
    *ffn_parts[4:], w_gate_up, w_down_all = lax.optimization_barrier(
        (*ffn_parts[4:], w_gate_up, w_down_all)
    )
    gate_up_other = swapped(w_gate_up, place.core_flip)
    down_other = swapped(w_down_all, place.core_flip)
    hidden_near, hidden_far, grad_near, grad_far = kernel_call(
        hidden_kernel,
        "feed_forward",
        [
            shape_of((half, units)),
            shape_of((half, units)),
            shape_of((half, 2 * units)),
            shape_of((half, 2 * units)),
        ],
        (*ffn_parts, *cot_parts, w_gate_up, w_down_all),
        flops=10 * 10**9,
        vmem=26,
    )
    grad_got = swapped(grad_far, place.core_flip)
    grad_got, gate_up_other, hidden_near, hidden_far, grad_near, grad_far = (
        lax.optimization_barrier(
            (grad_got, gate_up_other, hidden_near, hidden_far, grad_near, grad_far)
        )
    )
    (ffn_g,) = kernel_call(
        functools.partial(hidden_grad_kernel, sub),
        "feed_forward_weights",
        [shape_of((depth, seq_count, 3, deep, sub))],
        (hidden_near, hidden_far, grad_near, grad_far, *ffn_parts, *cot_parts),
        [
            pltpu.VMEM((8 * count, width), bf16),
            pltpu.VMEM((8 * count, width), bf16),
            pltpu.SemaphoreType.DMA((16,)),
        ],
        hbm=16,
        flops=5 * 10**9,
        vmem=26,
    )
    ffn_g, grad_near = lax.optimization_barrier((ffn_g, grad_near))
    ffn_g = line_scatter(place, ffn_g)
    terms = plane_terms(
        place, grad_near, grad_far, w_gate_up, gate_up_other, True, "feed_forward_back",
        got=grad_got,
    )
    terms = chip_scatter(place, terms)
    grad_middle, grad_branch, gain_ffn_sum = kernel_call(
        middle_back_kernel,
        "middle_back",
        [shape_of(flat, f32), shape_of(flat), shape_of((8, width), f32)],
        (*terms, middle, own_cot, gains),
        vmem=16,
    )
    ffn_g = lax.all_to_all(ffn_g, "seq", 0, 0)

    branch_near = chip_gather(place, grad_branch)
    hidden_near, hidden_far = after(grad_branch, hidden_near, hidden_far)
    out_terms = plane_terms(
        place, hidden_near, hidden_far, w_down_all, down_other, False, "feed_forward_out"
    )
    held = lax.optimization_barrier((*branch_near, *out_terms))
    branch_near, out_terms = list(held[:4]), list(held[4:])
    branch_parts = core_gather(place, branch_near)
    out_terms = chip_scatter(place, out_terms)
    dqkv_near, dqkv_far, grad_taps, grad_mix, grad_gain_group = kernel_call(
        functools.partial(backward_kernel, blocks, reach),
        "attention_backward",
        [
            shape_of((half, 3 * lanes)),
            shape_of((half, 3 * lanes)),
            shape_of((GROUP, 16, CQ * LANES), f32),
            shape_of((GROUP * GROUP, 8, LANES), f32),
            shape_of((8, lanes), f32),
        ],
        (
            at, mix, *branch_parts, w_out_heads, gain_heads,
            attended, values, probs, starts, stops, table_high, high, keys, queries,
        ),
        [
            pltpu.VMEM((2, length, lanes), f32),
            pltpu.VMEM((2, length, 3 * lanes), bf16),
            pltpu.VMEM((GROUP, blocks, length + 8, LANES), f32),
            pltpu.VMEM((GROUP, 2 * LANES, CQ * LANES), f32),
            pltpu.VMEM((GROUP, padded, LANES), f32),
            pltpu.VMEM((length, lanes), f32),
        ],
        flops=30 * 10**9,
        smem=2,
        vmem=34,
        lazy=9,
    )
    dqkv_near, dqkv_far, *out_terms = lax.optimization_barrier(
        (dqkv_near, dqkv_far, *out_terms)
    )
    (table,) = kernel_call(
        functools.partial(weight_grads_kernel, slab),
        "attention_weights",
        [shape_of((depth, 8 * pack_rows + out_rows, LANES))],
        (
            dqkv_near, dqkv_far, *branch_parts,
            grouped_near, grouped_far, spread_main, spread_rest, normed,
        ),
        flops=5 * 10**9,
        vmem=36,
        lazy=5,
    )
    table, dqkv_near = lax.optimization_barrier((table, dqkv_near))
    table = line_scatter(place, table)
    *terms, gain_attn_sum = plane_terms(
        place, dqkv_near, dqkv_far, w_wide, w_wide_other, True, "project_back",
        tuple(token_parts[:4]),
    )
    (small,) = kernel_call(
        small_kernel,
        "small_sums",
        [shape_of((2 * (width // LANES) + 2 * HEADS, LANES), f32)],
        (at, gain_attn_sum, gain_ffn_sum, grad_taps, grad_mix, grad_gain_group),
        smem=1,
        vmem=16,
    )
    terms = chip_scatter(place, terms)
    for flip in (place.core_flip, 2, 4, place.y_flip, place.x_flip):
        small = small + swapped(small, flip)
    (grad_tokens,) = kernel_call(
        input_back_kernel,
        "input_back",
        [shape_of(flat)],
        (*terms, own_tokens, grad_middle, gains),
        vmem=16,
    )
    (output,) = kernel_call(
        output_kernel, "output", [shape_of(flat)], (*out_terms, middle), vmem=16
    )
    grad_w_gate, grad_w_up, grad_w_down = kernel_call(
        functools.partial(unpack_hidden_kernel, sub),
        "unpack_hidden",
        [
            shape_of((deep, seq_count * sub), f32),
            shape_of((deep, seq_count * sub), f32),
            shape_of((seq_count * sub, deep), f32),
        ],
        (ffn_g,),
        vmem=16,
    )
    output, grad_w_gate, grad_tokens, small, table = lax.optimization_barrier(
        (output, grad_w_gate, grad_tokens, small, table)
    )
    back = [(target, source) for source, target in out_pairs(place)]
    out_table = lax.ppermute(table[8 * pack_rows :], FLAT, back)
    table = plane_exchange(place, table[: 8 * pack_rows].reshape(8, pack_rows, LANES))
    grad_rows = kernel_call(
        functools.partial(unpack_kernel, slab),
        "unpack_projections",
        [shape_of((slab, width), f32)] * 4,
        (table, out_table),
        vmem=16,
    )
    small_flat = small.reshape(-1)
    row = (place.seq * place.wide_count + lax.axis_index("wide")) * slab
    tiles = width // LANES
    gain_grads = [lax.dynamic_slice_in_dim(small_flat, i * width + row, slab) for i in range(2)]
    head, side = row // HEAD_DIM, row % HEAD_DIM
    gain_grads.append(
        lax.dynamic_slice_in_dim(small_flat, (2 * tiles + head) * LANES + side, slab)
    )
    heads = small[2 * tiles + HEADS :]
    grad_conv = heads[:, : 16 * CQ].reshape(HEADS, CQ, 16)[:, :, :CK]
    grad_head_mix = heads[:, 16 * CQ : 16 * CQ + GROUP]
    return (
        output[None],
        grad_tokens[None],
        grad_rows[0],
        grad_rows[1],
        grad_rows[2],
        grad_rows[3],
        gain_grads[0],
        gain_grads[2],
        gain_grads[1],
        grad_conv,
        grad_head_mix,
        grad_w_gate,
        grad_w_up,
        grad_w_down,
    )


def solution(mesh):
    planes = mesh.shape["seq"] == 4 and mesh.shape["wide"] == 8
    return jax.shard_map(
        plane_shards if planes else shards,
        mesh=mesh,
        in_specs=(
            P("wide", "seq", None),
            P("wide", None),
            P(("seq", "wide"), None),
            P(("seq", "wide"), None),
            P(("seq", "wide"), None),
            P(("seq", "wide"), None),
            P(("seq", "wide")),
            P(("seq", "wide")),
            P(("seq", "wide")),
            P(),
            P(),
            P("seq", "wide"),
            P("seq", "wide"),
            P("wide", "seq"),
            P("wide", "seq", None),
        ),
        out_specs=(
            P("wide", "seq", None),
            P("wide", "seq", None),
            P(("seq", "wide"), None),
            P(("seq", "wide"), None),
            P(("seq", "wide"), None),
            P(("seq", "wide"), None),
            P(("seq", "wide")),
            P(("seq", "wide")),
            P(("seq", "wide")),
            P(),
            P(),
            P("seq", "wide"),
            P("seq", "wide"),
            P("wide", "seq"),
        ),
        check_vma=False,
    )
```
